512 devices in a mesh: depth: 4 (over x), row: 8 (over y, core), col: 16 (over z).
Axes of the slice: x: 4, y: 4, z: 16, core: 2. Of those that a mesh axis runs over, the one named last changes fastest.
Arguments:
- species: float32 [2, 64, 256, 2048], P(None, 'depth', 'row', 'col'), may hold values from -6 to 6
- diffusivity: float32 [64, 256, 2048], P('depth', 'row', 'col'), may hold values from 0.05 to 0.4
- reaction_rate: float32 [64, 256, 2048], P('depth', 'row', 'col'), may hold values from 0.2 to 2
- shear_rate: float32 [16], replicated, may hold values from -0.08 to 0.08
- colour_weight: float32 [16, 4, 2], replicated, may hold values from -4 to 4
- colour_bias: float32 [16, 4], replicated, may hold values from -1 to 1
- slab_order: int32 [16, 4], replicated, may hold values from 0 to 3, each once within a row
- lengths: int32 [16, 16, 256], P('depth', 'col', 'row'), may hold values from 1 to 128
- owners: int32 [16, 16, 256, 1], P('depth', 'col', 'row'), may hold values from 0 to 15; in each aligned block of 32 rows (0 to 31, 32 to 63, ..., all dimensions but the last counted through in order) at most 4 rows name the same one
- warp_matrix: bfloat16 [16, 128, 128], replicated, may hold values from -0.5 to 0.5
Outputs:
- species_out: float32 [2, 64, 256, 2048], P(None, 'depth', 'row', 'col')
- frame: float32 [16, 256, 4, 2048], P('depth', 'row', None, 'col')
The draws below stay inside these ranges and needn't reach their ends.
Inputs may be any that keep to these rules, and one draw needn't show every extreme that they name: `slab_order`: each row names each of the 4 slabs once. `owners`: for one view, the 32 scanlines of one device (aligned blocks of 32 along the third dimension) name any one owner at most 4 times.
All inputs are finite; a program needn't handle non-finite values.
Results may differ from the reference program's by a relative error of at most 0.001.
The reference program's roundings to bfloat16 on the way (of `picture` and `pieces`) count: a program that leaves them out, or rounds other values in their place, can miss the bound.
Values may be sent and summed in bfloat16 or wider, within the bound.
No kernel may reach another device: no remote copies, remote signals or barrier semaphores. Data moves between devices by JAX's collectives and lax.ppermute only.
A program may use at most 64 MiB of HBM per device.

```python
import math
import jax
import jax.numpy as jnp
import numpy as np
from jax import lax

CD = 16
CR = 32
CC = 128
VIEWS = 16
NDZ = 64
NR = 256
NC = 2048
NSLAB = 4
NTILE = 16
SH = 3
CAP = 4


def draw_lengths(key, part):
    values = jax.random.randint(key, (VIEWS, NTILE, NR), 1, CC + 1, dtype=jnp.int32)
    values = values.at[0, 0, 0].set(CC)
    return values.at[0, 0, 1].set(1)


def steps_of(own_key, extent, shards, least, top_value):
    gain, own = 1.0, jax.random.fold_in(own_key, 6)
    for axis_at, shards_of in shards:
        draws = jnp.exp(jax.random.uniform(jax.random.fold_in(own, axis_at), (shards_of,), jnp.float32, least / len(shards), top_value / len(shards)))
        gain = gain * jnp.repeat(draws, extent[axis_at] // shards_of).reshape([-1 if axis == axis_at else 1 for axis in range(len(extent))])
    return gain


def deal_out(rng, own, number, rows, count, top, bound, lean):
    sequence = jax.random.permutation(rng, count)
    heavy_load, usual = portions_of(count, rows * top, bound, lean, True), portions_of(count, rows * top, bound, lean, False)
    places = jnp.arange(count)

    def named(sizes, rotation):
        used = int((sizes > 0).sum())
        fixed = max(1, used // 4)
        passed = fixed + (places - fixed + rotation * (used - fixed)) % max(1, count - fixed)
        return jnp.zeros((count,), jnp.int32).at[sequence[jnp.where(places < fixed, places, passed)]].set(jnp.asarray(sizes, jnp.int32))

    sizes = jnp.where(number % 4 == 0, named(heavy_load, number // 4), named(usual, number - number // 4 - 1))
    mixed = jax.random.permutation(jax.random.fold_in(own, 3), count)
    source_of, taker = mixed[0:count // 2 * 2:2], mixed[1:count // 2 * 2:2]
    room = jnp.minimum(sizes[source_of] - 1, bound - sizes[taker]) // 2
    room = jnp.where((source_of == sequence[0]) | (taker == sequence[0]) | (sizes[taker] == 0), 0, jnp.maximum(room, 0))
    passed = jax.random.randint(jax.random.fold_in(own, 4), (count // 2,), 0, 1 << 20) % (room + 1)
    sizes = sizes.at[source_of].add(-passed).at[taker].add(passed)
    labels = jnp.searchsorted(jnp.cumsum(sizes), jnp.arange(rows * top), side="right").astype(jnp.int32)
    listing = labels.reshape(top, rows).T
    listing = listing[jax.random.permutation(jax.random.fold_in(own, 1), rows)]
    rotation = jax.random.randint(jax.random.fold_in(own, 2), (rows, 1), 0, top)
    return jnp.take_along_axis(listing, (jnp.arange(top)[None, :] + rotation) % top, axis=1)


def portions_of(number_of, total, bound, slope, full):
    weights = [(1 << 20) // math.isqrt(standing ** slope) + 1 for standing in range(1, number_of + 1)]
    largest = bound if full else min(bound, max(-(-total // number_of), total * weights[0] // sum(weights)))
    least = 1 if total - largest >= number_of - 1 else 0
    counts, rest = [largest] + [least] * (number_of - 1), total - largest - least * (number_of - 1)
    while rest > 0:
        candidates = [i for i in range(1, number_of) if counts[i] < largest] or [i for i in range(1, number_of) if counts[i] < bound]
        pool, left = sum([weights[i] for i in candidates]), rest
        for i in candidates:
            more = min(bound - counts[i], max(1, left * weights[i] // pool), rest)
            counts[i] = counts[i] + more
            rest = rest - more
    return np.array(counts)


def scatter_about(key, shape, scale, bound, shards=(), held_as=jnp.bfloat16):
    drawn = scale * jax.random.normal(key, shape, jnp.float32)
    if shards:
        drawn = drawn * steps_of(key, shape, shards, -0.22, 0.18)
    return jnp.clip(drawn, -bound, bound).astype(held_as)


def setup_inputs(seed: int = 0) -> dict:
    keys = jax.random.split(jax.random.key(seed), 11)
    species = scatter_about(keys[0], (2, NDZ, NR, NC), 1.0, 6.0, ((1, 4), (2, 8), (3, 16)), jnp.float32)
    diffusivity = jnp.clip(jnp.exp(math.log(0.4) - 2.0794415 * jax.random.uniform(keys[1], (NDZ, NR, NC), jnp.float32) ** steps_of(keys[1], (NDZ, NR, NC), ((0, 4), (1, 8), (2, 16)), -0.2, 0.2)), 0.05, 0.4)
    reaction_rate = jnp.clip(jnp.exp(math.log(2.0) - 2.3025851 * jax.random.uniform(keys[2], (NDZ, NR, NC), jnp.float32) ** steps_of(keys[2], (NDZ, NR, NC), ((0, 4), (1, 8), (2, 16)), -0.2, 0.2)), 0.2, 2.0)
    shear_rate = jnp.clip(jax.random.uniform(keys[3], (VIEWS,), jnp.float32, -0.08, 0.08), -0.08, 0.08)
    colour_weight = scatter_about(keys[4], (VIEWS, 4, 2), 1.0, 4.0, (), jnp.float32)
    colour_bias = jnp.clip(jax.random.uniform(keys[5], (VIEWS, 4), jnp.float32, -1.0, 1.0), -1.0, 1.0)
    slab_order = jax.vmap(lambda own: jax.random.permutation(own, NSLAB))(jax.random.split(keys[6], VIEWS)).reshape((VIEWS, NSLAB)).astype(jnp.int32)
    lengths = draw_lengths(jax.random.fold_in(keys[10], 71), 0)
    owners_keys = jax.random.split(jax.random.fold_in(keys[8], 1), VIEWS * NTILE * NR // CR)
    owners_turns = jax.random.permutation(jax.random.fold_in(keys[8], 3), VIEWS * NTILE * NR // CR)
    owners = jax.vmap(lambda own, number: deal_out(jax.random.fold_in(keys[8], 2), own, number, CR, NTILE, 1, CAP, 2))(owners_keys, owners_turns).reshape((VIEWS, NTILE, NR, 1))
    warp_matrix = scatter_about(keys[9], (VIEWS, CC, CC), CC ** -0.5, 0.5)
    return {"species": species, "diffusivity": diffusivity, "reaction_rate": reaction_rate, "shear_rate": shear_rate, "colour_weight": colour_weight, "colour_bias": colour_bias, "slab_order": slab_order, "lengths": lengths, "owners": owners, "warp_matrix": warp_matrix}


TIME_STEP = 0.1
RAY_STEP = 0.02
VEL_DEPTH = 0.3
VEL_ROW = 0.2
VEL_COL = 0.4


def tendency_of(padded, diffusivity, reaction_rate):
    centre = padded[:, 1:-1, 1:-1, 1:-1]
    below_depth = padded[:, :-2, 1:-1, 1:-1]
    above_depth = padded[:, 2:, 1:-1, 1:-1]
    below_row = padded[:, 1:-1, :-2, 1:-1]
    above_row = padded[:, 1:-1, 2:, 1:-1]
    below_col = padded[:, 1:-1, 1:-1, :-2]
    above_col = padded[:, 1:-1, 1:-1, 2:]
    laplace = below_depth + above_depth + below_row + above_row + below_col + above_col - 6.0 * centre
    advect = VEL_DEPTH * (centre - below_depth) + VEL_ROW * (centre - below_row) + VEL_COL * (centre - below_col)
    heat_part = centre[1]
    burned = reaction_rate * centre[0] * heat_part * heat_part / (1.0 + heat_part * heat_part)
    source = jnp.stack([-burned, burned])
    return diffusivity * laplace - advect + source


def pad_fields(fields):
    return jnp.pad(fields, ((0, 0), (1, 1), (1, 1), (1, 1)))


def advance(species, diffusivity, reaction_rate):
    first = species + TIME_STEP * tendency_of(pad_fields(species), diffusivity, reaction_rate)
    second = 0.75 * species + 0.25 * (first + TIME_STEP * tendency_of(pad_fields(first), diffusivity, reaction_rate))
    return species / 3.0 + (2.0 / 3.0) * (second + TIME_STEP * tendency_of(pad_fields(second), diffusivity, reaction_rate))


def transfer(samples, weight_one, bias_one):
    logits = weight_one[None, :, 0, None] * samples[0][:, None, :] + weight_one[None, :, 1, None] * samples[1][:, None, :] + bias_one[None, :, None]
    colours = jax.nn.sigmoid(logits[:, :3, :])
    fading = jnp.exp(-RAY_STEP * jax.nn.softplus(logits[:, 3, :]))
    return colours, fading


def render_view(padded, shear_one, weight_one, bias_one, order_row):
    def march(state_pair, depth_index):
        colour, through = state_pair
        offset = shear_one * (depth_index.astype(jnp.float32) + 0.5 - 0.5 * NDZ)
        floor_part = jnp.floor(offset)
        fraction = offset - floor_part
        start = floor_part.astype(jnp.int32) + SH
        depth_plane = lax.dynamic_index_in_dim(padded, depth_index, 1, keepdims=False)
        left_sample = lax.dynamic_slice_in_dim(depth_plane, start, NC, 2)
        right_sample = lax.dynamic_slice_in_dim(depth_plane, start + 1, NC, 2)
        samples = (1.0 - fraction) * left_sample + fraction * right_sample
        colours, fading = transfer(samples, weight_one, bias_one)
        colour = colour + (through * (1.0 - fading))[:, None, :] * colours
        return (colour, through * fading), None

    images = []
    for slab in range(NSLAB):
        start_state = (jnp.zeros((NR, 3, NC), jnp.float32), jnp.ones((NR, NC), jnp.float32))
        indices = jnp.arange(slab * CD, (slab + 1) * CD, dtype=jnp.int32)
        (colour, through), unused = lax.scan(march, start_state, indices)
        images.append(jnp.concatenate([colour, (1.0 - through)[:, None, :]], axis=1))
    stack = jnp.stack(images)
    result = stack[order_row[0]]
    for position in range(1, NSLAB):
        result = result + (1.0 - result[:, 3:4, :]) * stack[order_row[position]]
    return result.astype(jnp.bfloat16)


def reference(species, diffusivity, reaction_rate, shear_rate, colour_weight, colour_bias, slab_order, lengths, owners, warp_matrix):
    species_out = advance(species, diffusivity, reaction_rate)
    padded = jnp.pad(species_out, ((0, 0), (0, 0), (0, 0), (SH, SH)))

    def one_view(inputs):
        shear_one, weight_one, bias_one, order_row = inputs
        return render_view(padded, shear_one, weight_one, bias_one, order_row)

    picture = lax.map(one_view, (shear_rate, colour_weight, colour_bias, slab_order))
    tiles = picture.reshape(VIEWS, NR, 4, NTILE, CC)
    column = jnp.arange(CC, dtype=jnp.int32)
    keep = column[None, None, None, :] < jnp.transpose(lengths, (0, 2, 1))[:, :, :, None]
    pieces = jnp.where(keep[:, :, None, :, :], tiles, jnp.zeros((), jnp.bfloat16))
    warped = jnp.einsum('vyctx,vxz->vyctz', pieces.astype(jnp.float32), warp_matrix.astype(jnp.float32), precision=lax.Precision.HIGHEST)
    tile_ids = jnp.arange(NTILE, dtype=jnp.int32)
    chosen = (owners[:, :, :, 0][:, :, :, None] == tile_ids).astype(jnp.float32)
    frame = jnp.einsum('vtyo,vyctz->vycoz', chosen, warped, precision=lax.Precision.HIGHEST)
    return species_out, frame.reshape(VIEWS, NR, 4, NC)
```

```python
import functools

import jax
import jax.numpy as jnp
from jax import lax
from jax.experimental import pallas as pl
from jax.experimental.pallas import tpu as pltpu
from jax.sharding import PartitionSpec as P

TIME_STEP = 0.1
RAY_STEP = 0.02
VEL_DEPTH = 0.3
VEL_ROW = 0.2
VEL_COL = 0.4

HALO = 3
RIM = 3
EDGE = 8
PLANES = 24
ROWS = 40
SHIFTS = 2 * RIM + 1
CAPACITY = 4

F32 = jnp.float32
BF16 = jnp.bfloat16
VMEM_SPEC = pl.BlockSpec(memory_space=pltpu.VMEM)
SMEM_SPEC = pl.BlockSpec(memory_space=pltpu.SMEM)
NT = (((1,), (1,)), ((), ()))
TN = (((0,), (0,)), ((), ()))


def call(kernel, out_shape, in_specs, scratch=(), limit=24):
    return pl.pallas_call(
        kernel,
        out_shape=out_shape,
        in_specs=in_specs,
        out_specs=jax.tree.map(lambda unused: VMEM_SPEC, out_shape),
        scratch_shapes=list(scratch),
        compiler_params=pltpu.CompilerParams(vmem_limit_bytes=limit << 20),
    )


def shift_up(x, axis):
    n = lax.axis_size(axis)
    return lax.ppermute(x, axis, [(i, i + 1) for i in range(n - 1)])


def shift_down(x, axis):
    n = lax.axis_size(axis)
    return lax.ppermute(x, axis, [(i + 1, i) for i in range(n - 1)])


def pack_depth(species, diff, rate, low, high):
    for f in range(2):
        low[f] = species[f, :HALO].astype(BF16)
        high[f] = species[f, -HALO:].astype(BF16)
    for f, ref in ((2, diff), (3, rate)):
        low[f] = ref[:HALO].astype(BF16)
        high[f] = ref[-HALO:].astype(BF16)


def pack_rows(species, diff, rate, before, after, low, high, wide):
    n = 32
    for f in range(4):
        base = f * PLANES * n
        own = species.at[f] if f < 2 else (diff if f == 2 else rate)
        wide[pl.ds(base, HALO * n), :] = before[f].astype(F32).reshape(HALO * n, 128)
        wide[pl.ds(base + HALO * n, 16 * n), :] = own[...].reshape(16 * n, 128)
        wide[pl.ds(base + 19 * n, HALO * n), :] = after[f].astype(F32).reshape(HALO * n, 128)
        wide[pl.ds(base + 22 * n, 2 * n), :] = jnp.zeros((2 * n, 128), F32)
    for r in range(HALO):
        low[r] = wide[pl.ds(r, 4 * PLANES, stride=n), :].astype(BF16)
        high[r] = wide[pl.ds(n - HALO + r, 4 * PLANES, stride=n), :].astype(BF16)


def column_picker():
    j = lax.broadcasted_iota(jnp.int32, (2 * EDGE, 128), 0)
    lane = lax.broadcasted_iota(jnp.int32, (2 * EDGE, 128), 1)
    return (lane == jnp.where(j < EDGE, j, 128 - 2 * EDGE + j)).astype(BF16)


def pack_columns(species, diff, rate, before, after, above, below, low, high):
    pick = column_picker()
    at = 0

    def put(rows):
        nonlocal at
        edge = lax.dot_general(pick, rows, NT, preferred_element_type=F32).astype(BF16)
        count = rows.shape[0]
        low[:, at : at + count] = edge[:EDGE]
        high[:, at : at + count] = edge[EDGE:]
        at += count

    for f in range(2):
        put(species[f].astype(BF16).reshape(512, 128))
    put(diff[...].astype(BF16).reshape(512, 128))
    put(rate[...].astype(BF16).reshape(512, 128))
    put(before[...].reshape(384, 128))
    put(after[...].reshape(384, 128))
    put(above[...].reshape(288, 128))
    put(below[...].reshape(288, 128))


EDGE_LENGTH = 4 * 512 + 2 * 384 + 2 * 288


def stencil(
    place,
    species,
    diff,
    rate,
    before,
    after,
    above,
    below,
    left,
    right,
    out,
    shifted,
    main,
    rim,
    first_main,
    first_rim,
    second_main,
    second_rim,
):
    n = ROWS
    for f in range(4):
        own = species.at[f] if f < 2 else (diff if f == 2 else rate)
        main[f, HALO : HALO + 16, 0:32, :] = own[...]
        main[f, 0:HALO, 0:32, :] = before[f].astype(F32)
        main[f, HALO + 16 : 22, 0:32, :] = after[f].astype(F32)
        main[f, :, 32:40, :] = jnp.zeros((PLANES, 8, 128), F32)
        rim[f, :, 32:40, :] = jnp.zeros((PLANES, 8, 128), F32)
    j = lax.broadcasted_iota(jnp.int32, (EDGE, 128), 0)
    lane8 = lax.broadcasted_iota(jnp.int32, (EDGE, 128), 1)
    reach = HALO + RIM
    put_left = ((lane8 == 128 - EDGE + j) & (j >= EDGE - reach)).astype(BF16)
    put_right = ((lane8 == j) & (j < reach)).astype(BF16)

    def spread(at, count):
        return lax.dot_general(
            left[:, at : at + count], put_left, TN, preferred_element_type=F32
        ) + lax.dot_general(right[:, at : at + count], put_right, TN, preferred_element_type=F32)

    for f in range(4):
        rim[f, HALO : HALO + 16, 0:32, :] = spread(512 * f, 512).reshape(16, 32, 128)
    side = spread(2048, 384).reshape(4, HALO, 32, 128)
    for f in range(4):
        rim[f, 0:HALO, 0:32, :] = side[f]
    side = spread(2432, 384).reshape(4, HALO, 32, 128)
    for f in range(4):
        rim[f, HALO + 16 : 22, 0:32, :] = side[f]
    up = spread(2816, 288).reshape(HALO, 96, 128)
    down = spread(3104, 288).reshape(HALO, 96, 128)
    for r in range(HALO):
        for f in range(4):
            own = pl.ds(f * PLANES, PLANES)
            part = slice(f * PLANES, (f + 1) * PLANES)
            main[f, :, n - HALO + r, :] = above[r, part, :].astype(F32)
            main[f, :, 32 + r, :] = below[r, part, :].astype(F32)
            rim[f, :, n - HALO + r, :] = up[r, part, :]
            rim[f, :, 32 + r, :] = down[r, part, :]

    depth_at, row_at, col_at = place[0], place[1], place[2]
    depth_last, row_last, col_last = place[3], place[4], place[5]
    row = lax.broadcasted_iota(jnp.int32, (n, 128), 0)
    lane = lax.broadcasted_iota(jnp.int32, (n, 128), 1)
    rows_in = (
        (row < 32)
        | ((row < 32 + HALO) & (row_at < row_last))
        | ((row >= n - HALO) & (row_at > 0))
    )
    lanes_in = ((lane < reach) & (col_at < col_last)) | ((lane >= 128 - reach) & (col_at > 0))
    step_main = jnp.where(rows_in, TIME_STEP, 0.0).astype(F32)
    step_rim = jnp.where(rows_in & lanes_in, TIME_STEP, 0.0).astype(F32)
    first_lane = lane == 0
    last_lane = lane == 127

    def tendency(m, r, p):
        results = []
        for part in range(2):
            here, there = (m, r) if part == 0 else (r, m)
            coefs = main if part == 0 else rim
            diffusivity = coefs[2, p]
            reaction = coefs[3, p]
            fuel, heat = here[0, p], here[1, p]
            square = heat * heat
            burned = reaction * fuel * square / (1.0 + square)
            both = []
            for f in range(2):
                centre = fuel if f == 0 else heat
                other = there[f, p]
                below_depth = here[f, p - 1]
                above_depth = here[f, p + 1]
                below_row = pltpu.roll(centre, 1, 0)
                above_row = pltpu.roll(centre, n - 1, 0)
                below_col = jnp.where(
                    first_lane, pltpu.roll(other, 1, 1), pltpu.roll(centre, 1, 1)
                )
                above_col = jnp.where(
                    last_lane, pltpu.roll(other, 127, 1), pltpu.roll(centre, 127, 1)
                )
                laplace = (
                    below_depth
                    + above_depth
                    + below_row
                    + above_row
                    + below_col
                    + above_col
                    - 6.0 * centre
                )
                advect = (
                    VEL_DEPTH * (centre - below_depth)
                    + VEL_ROW * (centre - below_row)
                    + VEL_COL * (centre - below_col)
                )
                gain = -burned if f == 0 else burned
                both.append(diffusivity * laplace - advect + gain)
            results.append(both)
        return results

    def inside(p):
        ok = ((p >= HALO) | (depth_at > 0)) & ((p < HALO + 16) | (depth_at < depth_last))
        return jnp.where(ok, 1.0, 0.0).astype(F32)

    @pl.loop(1, 21)
    def _(p):
        slope = tendency(main, rim, p)
        scale = inside(p)
        for f in range(2):
            first_main[f, p] = main[f, p] + (step_main * scale) * slope[0][f]
            first_rim[f, p] = rim[f, p] + (step_rim * scale) * slope[1][f]

    @pl.loop(2, 20)
    def _(p):
        slope = tendency(first_main, first_rim, p)
        scale = inside(p)
        for f in range(2):
            second_main[f, p] = 0.75 * main[f, p] + 0.25 * (
                first_main[f, p] + (step_main * scale) * slope[0][f]
            )
            second_rim[f, p] = 0.75 * rim[f, p] + 0.25 * (
                first_rim[f, p] + (step_rim * scale) * slope[1][f]
            )

    lane32 = lax.broadcasted_iota(jnp.int32, (32, 128), 1)

    @pl.loop(3, 19)
    def _(p):
        slope = tendency(second_main, second_rim, p)
        k = p - HALO
        for f in range(2):
            new_main = (
                main[f, p] / 3.0 + (2.0 / 3.0) * (second_main[f, p] + step_main * slope[0][f])
            )[:32]
            new_rim = (
                rim[f, p] / 3.0 + (2.0 / 3.0) * (second_rim[f, p] + step_rim * slope[1][f])
            )[:32]
            out[f, k] = new_main
            for shift in range(-RIM, RIM + 1):
                if shift == 0:
                    shifted[RIM, f, k] = new_main
                    continue
                turn = -shift % 128
                outside = lane32 >= 128 - shift if shift > 0 else lane32 < -shift
                shifted[shift + RIM, f, k] = jnp.where(
                    outside, pltpu.roll(new_rim, turn, 1), pltpu.roll(new_main, turn, 1)
                )


def render(start_ref, fraction_ref, weights, view_first, shifted, image):
    count = image.shape[0]
    depth_cells = shifted.shape[2]
    first = view_first[0]

    @pl.loop(0, count)
    def _(j):
        v = first + j

        def march(k, state):
            c0, c1, c2, total, through = state
            i = start_ref[v, k]
            t = fraction_ref[v, k]
            s0 = (1.0 - t) * shifted[i, 0, k] + t * shifted[i + 1, 0, k]
            s1 = (1.0 - t) * shifted[i, 1, k] + t * shifted[i + 1, 1, k]
            logits = [
                weights[v, 3 * c] * s0 + weights[v, 3 * c + 1] * s1 + weights[v, 3 * c + 2]
                for c in range(4)
            ]
            dense = logits[3]
            total = total + (jnp.maximum(dense, 0.0) + jnp.log(1.0 + jnp.exp(-jnp.abs(dense))))
            after = jnp.exp(-RAY_STEP * total)
            part = through - after
            c0 = c0 + part * jnp.tanh(logits[0])
            c1 = c1 + part * jnp.tanh(logits[1])
            c2 = c2 + part * jnp.tanh(logits[2])
            return c0, c1, c2, total, after

        zero = jnp.zeros((32, 128), F32)
        c0, c1, c2, total, through = lax.fori_loop(
            0, depth_cells, march, (zero, zero, zero, zero, zero + 1.0), unroll=2
        )
        opacity = 1.0 - through
        image[j, 0] = 0.5 * (c0 + opacity)
        image[j, 1] = 0.5 * (c1 + opacity)
        image[j, 2] = 0.5 * (c2 + opacity)
        image[j, 3] = opacity


def composite(order, codes, lengths, slab0, slab1, slab2, slab3, outgoing, pieces):
    lane = lax.broadcasted_iota(jnp.int32, (32, 128), 1)
    slabs = (slab0, slab1, slab2, slab3)

    def fetch(which, v, c):
        value = slabs[3][v, c]
        for offset in (2, 1, 0):
            value = jnp.where(which == offset, slabs[offset][v, c], value)
        return value

    for v in range(4):
        keep = lane < lengths[32 * v : 32 * (v + 1), :]
        channels = [fetch(order[v, 0], v, c) for c in range(4)]
        for position in range(1, 4):
            clear = 1.0 - channels[3]
            channels = [channels[c] + clear * fetch(order[v, position], v, c) for c in range(4)]
        for c in range(4):
            pieces[32 * v : 32 * (v + 1), 128 * c : 128 * (c + 1)] = jnp.where(
                keep, channels[c], 0.0
            ).astype(BF16)
    row_id = lax.broadcasted_iota(jnp.int32, (128, 128), 0) + 1
    pieces[:, 512:640] = row_id.astype(F32).astype(BF16)
    slot = lax.broadcasted_iota(jnp.int32, (256, 128), 0)
    select = (slot == codes[...]).astype(F32).astype(BF16)
    outgoing[...] = jnp.dot(select, pieces[...], preferred_element_type=F32).astype(BF16)


def resample(incoming, warp, frame):
    names = incoming[:, 512:640].astype(F32)
    lane = lax.broadcasted_iota(jnp.int32, (256, 128), 1) + 1
    place = (names == lane.astype(F32)).astype(F32).astype(BF16)
    total = lax.dot_general(place, incoming[:, 0:512], TN, preferred_element_type=F32)
    for v in range(4):
        matrix = warp[v].astype(F32)
        for c in range(4):
            rows = total[32 * v : 32 * (v + 1), 128 * c : 128 * (c + 1)]
            frame[pl.ds(128 * v + c, 32, stride=4), :] = jnp.dot(
                rows, matrix, preferred_element_type=F32, precision=lax.Precision.HIGHEST
            )


def body(
    species,
    diffusivity,
    reaction_rate,
    shear_rate,
    colour_weight,
    colour_bias,
    slab_order,
    lengths,
    owners,
    warp_matrix,
):
    depth_at, row_at, col_at = (lax.axis_index(a) for a in ("depth", "row", "col"))
    depth_devices, row_devices, col_devices = (lax.axis_size(a) for a in ("depth", "row", "col"))
    depth_cells = species.shape[1]
    depth_total = depth_cells * depth_devices
    views = shear_rate.shape[0]
    view_count = views // depth_devices

    face = jax.ShapeDtypeStruct((4, HALO, 32, 128), BF16)
    low, high = call(pack_depth, (face, face), [VMEM_SPEC] * 3)(species, diffusivity, reaction_rate)
    before, after = shift_up(high, "depth"), shift_down(low, "depth")
    face = jax.ShapeDtypeStruct((HALO, 4 * PLANES, 128), BF16)
    low, high = call(
        pack_rows, (face, face), [VMEM_SPEC] * 5, [pltpu.VMEM((4 * PLANES * 32, 128), F32)]
    )(species, diffusivity, reaction_rate, before, after)
    above, below = shift_up(high, "row"), shift_down(low, "row")
    face = jax.ShapeDtypeStruct((EDGE, EDGE_LENGTH), BF16)
    low, high = call(pack_columns, (face, face), [VMEM_SPEC] * 7)(
        species, diffusivity, reaction_rate, before, after, above, below
    )
    left, right = shift_up(high, "col"), shift_down(low, "col")
    place = jnp.stack(
        [
            depth_at,
            row_at,
            col_at,
            jnp.int32(depth_devices - 1),
            jnp.int32(row_devices - 1),
            jnp.int32(col_devices - 1),
        ]
    ).astype(jnp.int32)
    wide = pltpu.VMEM((2, PLANES, ROWS, 128), F32)
    species_out, shifted = call(
        stencil,
        (
            jax.ShapeDtypeStruct(species.shape, F32),
            jax.ShapeDtypeStruct((SHIFTS,) + species.shape, F32),
        ),
        [SMEM_SPEC] + [VMEM_SPEC] * 9,
        [pltpu.VMEM((4, PLANES, ROWS, 128), F32)] * 2 + [wide] * 4,
        limit=40,
    )(
        place,
        species,
        diffusivity,
        reaction_rate,
        before,
        after,
        above,
        below,
        left,
        right,
    )

    depth_index = depth_at * depth_cells + jnp.arange(depth_cells, dtype=jnp.int32)
    offset = shear_rate[:, None] * (depth_index.astype(F32) + 0.5 - 0.5 * depth_total)[None, :]
    floor_part = jnp.floor(offset)
    fraction = offset - floor_part
    start = jnp.clip(floor_part.astype(jnp.int32) + RIM, 0, SHIFTS - 2)
    weights = jnp.concatenate([colour_weight, colour_bias[:, :, None]], axis=2)
    weights = (weights * jnp.array([0.5, 0.5, 0.5, 1.0], F32)[None, :, None]).reshape(views, 12)

    image = jax.ShapeDtypeStruct((view_count, 4, 32, 128), F32)
    render_call = call(render, image, [SMEM_SPEC] * 4 + [VMEM_SPEC])
    slabs = [None] * 4
    for away in (2, 1, 3, 0):
        group = (depth_at + away) % depth_devices
        drawn = render_call(
            start, fraction, weights, (group * view_count).reshape(1).astype(jnp.int32), shifted
        )
        if away:
            drawn = lax.ppermute(
                drawn, "depth", [(i, (i + away) % depth_devices) for i in range(depth_devices)]
            )
        slabs[away] = drawn
    own_order = lax.dynamic_slice_in_dim(slab_order, depth_at * view_count, view_count, 0)
    order = (depth_at - own_order) % depth_devices

    mine = owners[:, 0, :, 0]
    line = jnp.arange(mine.shape[1], dtype=jnp.int32)
    same = (mine[:, :, None] == mine[:, None, :]) & (line[None, :] < line[:, None])[None]
    rank = jnp.sum(same.astype(jnp.int32), axis=2)
    view = jnp.arange(view_count, dtype=jnp.int32)[:, None]
    codes = (mine * (view_count * CAPACITY) + view * CAPACITY + rank).reshape(1, -1)
    lengths_wide = jnp.broadcast_to(lengths[:, 0, :].reshape(-1, 1), (128, 128))

    slots = col_devices * view_count * CAPACITY
    outgoing = call(
        composite,
        jax.ShapeDtypeStruct((slots, 640), BF16),
        [SMEM_SPEC] + [VMEM_SPEC] * 6,
        [pltpu.VMEM((128, 640), BF16)],
    )(order, codes, lengths_wide, *slabs)
    incoming = lax.all_to_all(
        outgoing.reshape(col_devices, slots // col_devices, 640),
        "col",
        split_axis=0,
        concat_axis=0,
        tiled=True,
    ).reshape(slots, 640)
    warp_own = lax.dynamic_slice_in_dim(warp_matrix, depth_at * view_count, view_count, 0)
    frame = call(
        resample, jax.ShapeDtypeStruct((512, 128), F32), [VMEM_SPEC] * 2
    )(incoming, warp_own)
    return species_out, frame.reshape(view_count, 32, 4, 128)


def solution(mesh):
    in_specs = (
        P(None, "depth", "row", "col"),
        P("depth", "row", "col"),
        P("depth", "row", "col"),
        P(),
        P(),
        P(),
        P(),
        P("depth", "col", "row"),
        P("depth", "col", "row", None),
        P(),
    )
    out_specs = (P(None, "depth", "row", "col"), P("depth", "row", None, "col"))
    return jax.shard_map(body, mesh=mesh, in_specs=in_specs, out_specs=out_specs, check_vma=False)
```

```python
import functools

import jax
import jax.numpy as jnp
from jax import lax
from jax.experimental import pallas as pl
from jax.experimental.pallas import tpu as pltpu
from jax.sharding import PartitionSpec as P

TIME_STEP = 0.1
RAY_STEP = 0.02
LOG2E = 1.4426950408889634
VEL_DEPTH = 0.3
VEL_ROW = 0.2
VEL_COL = 0.4

HALO = 3
RIM = 3
EDGE = 8
PLANES = 24
ROWS = 40
SHIFTS = 2 * RIM + 1
CAPACITY = 4

F32 = jnp.float32
BF16 = jnp.bfloat16
VMEM_SPEC = pl.BlockSpec(memory_space=pltpu.VMEM)
SMEM_SPEC = pl.BlockSpec(memory_space=pltpu.SMEM)
HBM_SPEC = pl.BlockSpec(memory_space=pltpu.HBM)
NT = (((1,), (1,)), ((), ()))
TN = (((0,), (0,)), ((), ()))


def call(kernel, out_shape, in_specs, scratch=(), limit=8, aliases=None):
    return pl.pallas_call(
        kernel,
        out_shape=out_shape,
        in_specs=in_specs,
        out_specs=jax.tree.map(lambda unused: VMEM_SPEC, out_shape),
        scratch_shapes=list(scratch),
        input_output_aliases=aliases or {},
        compiler_params=pltpu.CompilerParams(vmem_limit_bytes=limit << 20),
    )


def in_hbm(x):
    return pltpu.with_memory_space_constraint(x, pltpu.HBM)


def shift_up(x, axis):
    n = lax.axis_size(axis)
    return lax.ppermute(x, axis, [(i, i + 1) for i in range(n - 1)])


def shift_down(x, axis):
    n = lax.axis_size(axis)
    return lax.ppermute(x, axis, [(i + 1, i) for i in range(n - 1)])


def pack_depth(species, diff, rate, low, high, held, sems):
    copies = []
    for side, first in ((0, 0), (1, 16 - HALO)):
        cut = pl.ds(first, HALO)
        for source, at in (
            (species.at[0, cut], 0),
            (species.at[1, cut], 1),
            (diff.at[cut], 2),
            (rate.at[cut], 3),
        ):
            copies.append(
                pltpu.make_async_copy(source, held.at[side, at], sems.at[4 * side + at])
            )
    for copy in copies:
        copy.start()
    for copy in copies:
        copy.wait()
    low[...] = held[0].astype(BF16)
    high[...] = held[1].astype(BF16)


def load_brick(species, diff, rate, brick, sems):
    copies = [
        pltpu.make_async_copy(
            source, brick.at[f, pl.ds(HALO, 16), pl.ds(0, 32), :], sems.at[f]
        )
        for f, source in enumerate((species.at[0], species.at[1], diff, rate))
    ]
    for copy in copies:
        copy.start()
    for f in range(4):
        brick[f, :, 32:ROWS, :] = jnp.zeros((PLANES, ROWS - 32, 128), F32)
        brick[f, HALO + 16 + HALO :, 0:32, :] = jnp.zeros((PLANES - 22, 32, 128), F32)
    for copy in copies:
        copy.wait()


def pack_rows(unused, before, after, brick, low, high):
    for f in range(4):
        brick[f, 0:HALO, 0:32, :] = before[f].astype(F32)
        brick[f, HALO + 16 : 22, 0:32, :] = after[f].astype(F32)
    lines = brick.reshape(4 * PLANES * ROWS, 128)
    for r in range(HALO):
        low[r] = lines[pl.ds(r, 4 * PLANES, stride=ROWS), :].astype(BF16)
        high[r] = lines[pl.ds(32 - HALO + r, 4 * PLANES, stride=ROWS), :].astype(BF16)


def column_picker():
    j = lax.broadcasted_iota(jnp.int32, (2 * EDGE, 128), 0)
    lane = lax.broadcasted_iota(jnp.int32, (2 * EDGE, 128), 1)
    return (lane == jnp.where(j < EDGE, j, 128 - 2 * EDGE + j)).astype(BF16)


def pack_columns(unused, above, below, brick, low, high):
    lines = brick.reshape(4 * PLANES * ROWS, 128)
    for r in range(HALO):
        lines[pl.ds(ROWS - HALO + r, 4 * PLANES, stride=ROWS), :] = above[r].astype(F32)
        lines[pl.ds(32 + r, 4 * PLANES, stride=ROWS), :] = below[r].astype(F32)
    pick = column_picker()
    count = PLANES * ROWS
    for f in range(4):
        rows = brick[f].reshape(count, 128).astype(BF16)
        edge = lax.dot_general(pick, rows, NT, preferred_element_type=F32).astype(BF16)
        low[:, f * count : (f + 1) * count] = edge[:EDGE]
        high[:, f * count : (f + 1) * count] = edge[EDGE:]


def stencil(
    place,
    main,
    left,
    right,
    out,
    shifted,
    rim,
    first_main,
    first_rim,
    second_main,
    second_rim,
):
    n = ROWS
    j = lax.broadcasted_iota(jnp.int32, (EDGE, 128), 0)
    lane8 = lax.broadcasted_iota(jnp.int32, (EDGE, 128), 1)
    reach = HALO + RIM
    put_left = ((lane8 == 128 - EDGE + j) & (j >= EDGE - reach)).astype(BF16)
    put_right = ((lane8 == j) & (j < reach)).astype(BF16)
    count = PLANES * ROWS
    for f in range(4):
        cut = slice(f * count, (f + 1) * count)
        spread = lax.dot_general(
            left[:, cut], put_left, TN, preferred_element_type=F32
        ) + lax.dot_general(right[:, cut], put_right, TN, preferred_element_type=F32)
        rim[f] = spread.reshape(PLANES, ROWS, 128)

    depth_at, row_at, col_at = place[0], place[1], place[2]
    depth_last, row_last, col_last = place[3], place[4], place[5]
    row = lax.broadcasted_iota(jnp.int32, (n, 128), 0)
    lane = lax.broadcasted_iota(jnp.int32, (n, 128), 1)
    rows_in = (
        (row < 32)
        | ((row < 32 + HALO) & (row_at < row_last))
        | ((row >= n - HALO) & (row_at > 0))
    )
    lanes_in = ((lane < reach) & (col_at < col_last)) | ((lane >= 128 - reach) & (col_at > 0))
    step_main = jnp.where(rows_in, TIME_STEP, 0.0).astype(F32)
    step_rim = jnp.where(rows_in & lanes_in, TIME_STEP, 0.0).astype(F32)
    first_lane = lane == 0
    last_lane = lane == 127

    def tendency(m, r, p):
        results = []
        for part in range(2):
            here, there = (m, r) if part == 0 else (r, m)
            coefs = main if part == 0 else rim
            diffusivity = coefs[2, p]
            reaction = coefs[3, p]
            fuel, heat = here[0, p], here[1, p]
            square = heat * heat
            burned = reaction * fuel * square / (1.0 + square)
            both = []
            for f in range(2):
                centre = fuel if f == 0 else heat
                other = there[f, p]
                below_depth = here[f, p - 1]
                above_depth = here[f, p + 1]
                below_row = pltpu.roll(centre, 1, 0)
                above_row = pltpu.roll(centre, n - 1, 0)
                below_col = jnp.where(
                    first_lane, pltpu.roll(other, 1, 1), pltpu.roll(centre, 1, 1)
                )
                above_col = jnp.where(
                    last_lane, pltpu.roll(other, 127, 1), pltpu.roll(centre, 127, 1)
                )
                laplace = (
                    below_depth
                    + above_depth
                    + below_row
                    + above_row
                    + below_col
                    + above_col
                    - 6.0 * centre
                )
                advect = (
                    VEL_DEPTH * (centre - below_depth)
                    + VEL_ROW * (centre - below_row)
                    + VEL_COL * (centre - below_col)
                )
                gain = -burned if f == 0 else burned
                both.append(diffusivity * laplace - advect + gain)
            results.append(both)
        return results

    def inside(p):
        ok = ((p >= HALO) | (depth_at > 0)) & ((p < HALO + 16) | (depth_at < depth_last))
        return jnp.where(ok, 1.0, 0.0).astype(F32)

    @pl.loop(1, 21)
    def _(p):
        slope = tendency(main, rim, p)
        scale = inside(p)
        for f in range(2):
            first_main[f, p] = main[f, p] + (step_main * scale) * slope[0][f]
            first_rim[f, p] = rim[f, p] + (step_rim * scale) * slope[1][f]

    @pl.loop(2, 20)
    def _(p):
        slope = tendency(first_main, first_rim, p)
        scale = inside(p)
        for f in range(2):
            second_main[f, p] = 0.75 * main[f, p] + 0.25 * (
                first_main[f, p] + (step_main * scale) * slope[0][f]
            )
            second_rim[f, p] = 0.75 * rim[f, p] + 0.25 * (
                first_rim[f, p] + (step_rim * scale) * slope[1][f]
            )

    lane32 = lax.broadcasted_iota(jnp.int32, (32, 128), 1)

    @pl.loop(3, 19)
    def _(p):
        slope = tendency(second_main, second_rim, p)
        k = p - HALO
        for f in range(2):
            new_main = (
                main[f, p] / 3.0 + (2.0 / 3.0) * (second_main[f, p] + step_main * slope[0][f])
            )[:32]
            new_rim = (
                rim[f, p] / 3.0 + (2.0 / 3.0) * (second_rim[f, p] + step_rim * slope[1][f])
            )[:32]
            out[f, k] = new_main
            for shift in range(-RIM, RIM + 1):
                if shift == 0:
                    shifted[RIM, f, k] = new_main
                    continue
                turn = -shift % 128
                outside = lane32 >= 128 - shift if shift > 0 else lane32 < -shift
                shifted[shift + RIM, f, k] = jnp.where(
                    outside, pltpu.roll(new_rim, turn, 1), pltpu.roll(new_main, turn, 1)
                )


def render(away, place, shear, weight, bias, shifted, image):
    count = image.shape[0]
    depth_cells = shifted.shape[2]
    depth_at, depth_last = place[0], place[3]
    first = lax.rem(depth_at + away, depth_last + 1) * count
    middle = 0.5 * depth_cells * (depth_last + 1).astype(F32)

    @pl.loop(0, count)
    def _(j):
        v = first + j
        table = [
            tuple(
                (0.5 if c < 3 else 1.0) * value
                for value in (weight[c, 0, v], weight[c, 1, v], bias[c, v])
            )
            for c in range(4)
        ]
        slope = shear[v]

        def march(k, state):
            c0, c1, c2, total, through = state
            place_in_depth = (depth_at * depth_cells + k).astype(F32) + 0.5
            offset = slope * (place_in_depth - middle)
            whole = offset.astype(jnp.int32)
            whole = jnp.where(whole.astype(F32) > offset, whole - 1, whole)
            t = offset - whole.astype(F32)
            i = jnp.clip(whole + RIM, 0, SHIFTS - 2)
            s0 = (1.0 - t) * shifted[i, 0, k] + t * shifted[i + 1, 0, k]
            s1 = (1.0 - t) * shifted[i, 1, k] + t * shifted[i + 1, 1, k]
            logits = [table[c][0] * s0 + table[c][1] * s1 + table[c][2] for c in range(4)]
            dense = logits[3]
            total = total + (jnp.maximum(dense, 0.0) + jnp.log(1.0 + jnp.exp(-jnp.abs(dense))))
            after = jnp.exp2((-RAY_STEP * LOG2E) * total)
            part = through - after
            c0 = c0 + part * jnp.tanh(logits[0])
            c1 = c1 + part * jnp.tanh(logits[1])
            c2 = c2 + part * jnp.tanh(logits[2])
            return c0, c1, c2, total, after

        zero = jnp.zeros((32, 128), F32)
        c0, c1, c2, total, through = lax.fori_loop(
            0, depth_cells, march, (zero, zero, zero, zero, zero + 1.0), unroll=4
        )
        opacity = 1.0 - through
        image[j, 0] = 0.5 * (c0 + opacity)
        image[j, 1] = 0.5 * (c1 + opacity)
        image[j, 2] = 0.5 * (c2 + opacity)
        image[j, 3] = opacity


def deal(place, owners, lengths, warp, select, lengths_wide, warp_own, sem):
    views = warp_own.shape[0]
    copy = pltpu.make_async_copy(warp.at[pl.ds(place[0] * views, views)], warp_own, sem.at[0])
    copy.start()
    row = lax.broadcasted_iota(jnp.int32, (128, 128), 0)
    lane = lax.broadcasted_iota(jnp.int32, (128, 128), 1)
    name = jnp.concatenate([owners[v : v + 1, :] for v in range(views)], axis=1)
    length = jnp.concatenate([lengths[v : v + 1, :] for v in range(views)], axis=1)
    along = jnp.broadcast_to(name, (128, 128))
    across = along.T
    earlier = (along == across) & (row < lane) & (row // 32 == lane // 32)
    rank = jnp.sum(earlier.astype(F32), axis=0, keepdims=True).astype(jnp.int32)
    view = lane[0:1] // 32
    codes = name * (views * CAPACITY) + view * CAPACITY + rank
    slot = lax.broadcasted_iota(jnp.int32, select.shape, 0)
    select[...] = (slot == codes).astype(F32).astype(BF16)
    lengths_wide[...] = jnp.broadcast_to(length, (128, 128)).T
    copy.wait()


def composite(place, order, select, lengths, slab0, slab1, slab2, slab3, outgoing, pieces):
    lane = lax.broadcasted_iota(jnp.int32, (32, 128), 1)
    slabs = (slab0, slab1, slab2, slab3)
    depth_at, devices = place[0], place[3] + 1

    def fetch(which, v, c):
        value = slabs[3][v, c]
        for offset in (2, 1, 0):
            value = jnp.where(which == offset, slabs[offset][v, c], value)
        return value

    for v in range(4):
        keep = lane < lengths[32 * v : 32 * (v + 1), :]
        turn = [
            lax.rem(depth_at - order[position, depth_at * 4 + v] + devices, devices)
            for position in range(4)
        ]
        channels = [fetch(turn[0], v, c) for c in range(4)]
        for position in range(1, 4):
            clear = 1.0 - channels[3]
            channels = [channels[c] + clear * fetch(turn[position], v, c) for c in range(4)]
        for c in range(4):
            pieces[32 * v : 32 * (v + 1), 128 * c : 128 * (c + 1)] = jnp.where(
                keep, channels[c], 0.0
            ).astype(BF16)
    row_id = lax.broadcasted_iota(jnp.int32, (128, 128), 0) + 1
    pieces[:, 512:640] = row_id.astype(F32).astype(BF16)
    outgoing[...] = jnp.dot(select[...], pieces[...], preferred_element_type=F32).astype(BF16)


def resample(incoming, warp, frame):
    names = incoming[:, 512:640].astype(F32)
    lane = lax.broadcasted_iota(jnp.int32, (256, 128), 1) + 1
    place = (names == lane.astype(F32)).astype(F32).astype(BF16)
    total = lax.dot_general(place, incoming[:, 0:512], TN, preferred_element_type=F32)
    for v in range(4):
        matrix = warp[v].astype(F32)
        for c in range(4):
            rows = total[32 * v : 32 * (v + 1), 128 * c : 128 * (c + 1)]
            frame[pl.ds(128 * v + c, 32, stride=4), :] = jnp.dot(
                rows, matrix, preferred_element_type=F32, precision=lax.Precision.HIGHEST
            )


def body(
    species,
    diffusivity,
    reaction_rate,
    shear_rate,
    colour_weight,
    colour_bias,
    slab_order,
    lengths,
    owners,
    warp_matrix,
):
    depth_at, row_at, col_at = (lax.axis_index(a) for a in ("depth", "row", "col"))
    depth_devices, row_devices, col_devices = (lax.axis_size(a) for a in ("depth", "row", "col"))
    view_count = shear_rate.shape[0] // depth_devices

    place = jnp.stack(
        [
            depth_at,
            row_at,
            col_at,
            jnp.int32(depth_devices - 1),
            jnp.int32(row_devices - 1),
            jnp.int32(col_devices - 1),
        ]
    ).astype(jnp.int32)
    fields = tuple(in_hbm(x) for x in (species, diffusivity, reaction_rate))

    face = jax.ShapeDtypeStruct((4, HALO, 32, 128), BF16)
    low, high = call(
        pack_depth,
        (face, face),
        [HBM_SPEC] * 3,
        [pltpu.VMEM((2, 4, HALO, 32, 128), F32), pltpu.SemaphoreType.DMA((8,))],
    )(*fields)
    before, after = shift_up(high, "depth"), shift_down(low, "depth")
    brick_type = jax.ShapeDtypeStruct((4, PLANES, ROWS, 128), F32)
    brick = call(load_brick, brick_type, [HBM_SPEC] * 3, [pltpu.SemaphoreType.DMA((4,))])(*fields)
    face = jax.ShapeDtypeStruct((HALO, 4 * PLANES, 128), BF16)
    brick, low, high = call(
        pack_rows, (brick_type, face, face), [VMEM_SPEC] * 3, aliases={0: 0}
    )(brick, before, after)
    above, below = shift_up(high, "row"), shift_down(low, "row")
    slots = col_devices * view_count * CAPACITY
    lines = view_count * 32
    select, lengths_wide, warp_own = call(
        deal,
        (
            jax.ShapeDtypeStruct((slots, lines), BF16),
            jax.ShapeDtypeStruct((lines, 128), jnp.int32),
            jax.ShapeDtypeStruct((view_count, 128, 128), BF16),
        ),
        [SMEM_SPEC, VMEM_SPEC, VMEM_SPEC, HBM_SPEC],
        [pltpu.SemaphoreType.DMA((1,))],
    )(place, owners.reshape(view_count, 32), lengths.reshape(view_count, 32), in_hbm(warp_matrix))

    brick, select, lengths_wide, warp_own = lax.optimization_barrier(
        (brick, select, lengths_wide, warp_own)
    )
    face = jax.ShapeDtypeStruct((EDGE, 4 * PLANES * ROWS), BF16)
    brick, low, high = call(
        pack_columns, (brick_type, face, face), [VMEM_SPEC] * 3, aliases={0: 0}
    )(brick, above, below)
    left, right = shift_up(high, "col"), shift_down(low, "col")
    wide = pltpu.VMEM((2, PLANES, ROWS, 128), F32)
    species_out, shifted = call(
        stencil,
        (
            jax.ShapeDtypeStruct(species.shape, F32),
            jax.ShapeDtypeStruct((SHIFTS,) + species.shape, F32),
        ),
        [SMEM_SPEC] + [VMEM_SPEC] * 3,
        [pltpu.VMEM((4, PLANES, ROWS, 128), F32)] + [wide] * 4,
        limit=16,
    )(place, brick, left, right)

    image = jax.ShapeDtypeStruct((view_count, 4, 32, 128), F32)
    weight, bias = jnp.transpose(colour_weight, (1, 2, 0)), colour_bias.T
    slabs = [None] * 4
    for away in (2, 1, 3, 0):
        drawn = call(
            functools.partial(render, away), image, [SMEM_SPEC] * 4 + [VMEM_SPEC]
        )(place, shear_rate, weight, bias, shifted)
        if away:
            drawn = lax.ppermute(
                drawn, "depth", [(i, (i + away) % depth_devices) for i in range(depth_devices)]
            )
        slabs[away] = drawn
    outgoing = call(
        composite,
        jax.ShapeDtypeStruct((slots, 640), BF16),
        [SMEM_SPEC] * 2 + [VMEM_SPEC] * 6,
        [pltpu.VMEM((lines, 640), BF16)],
    )(place, slab_order.T, select, lengths_wide, *slabs)
    incoming = lax.all_to_all(
        outgoing.reshape(col_devices, slots // col_devices, 640),
        "col",
        split_axis=0,
        concat_axis=0,
        tiled=True,
    ).reshape(slots, 640)
    frame = call(resample, jax.ShapeDtypeStruct((4 * lines, 128), F32), [VMEM_SPEC] * 2)(
        incoming, warp_own
    )
    return species_out, frame.reshape(view_count, 32, 4, 128)


def solution(mesh):
    in_specs = (
        P(None, "depth", "row", "col"),
        P("depth", "row", "col"),
        P("depth", "row", "col"),
        P(),
        P(),
        P(),
        P(),
        P("depth", "col", "row"),
        P("depth", "col", "row", None),
        P(),
    )
    out_specs = (P(None, "depth", "row", "col"), P("depth", "row", None, "col"))
    return jax.shard_map(body, mesh=mesh, in_specs=in_specs, out_specs=out_specs, check_vma=False)
```

```python
import functools

import jax
import jax.numpy as jnp
from jax import lax
from jax.experimental import pallas as pl
from jax.experimental.pallas import tpu as pltpu
from jax.sharding import PartitionSpec as P

TIME_STEP = 0.1
RAY_STEP = 0.02
LOG2E = 1.4426950408889634
VEL_DEPTH = 0.3
VEL_ROW = 0.2
VEL_COL = 0.4

HALO = 3
RIM = 3
EDGE = 8
PLANES = 24
ROWS = 40
SHIFTS = 2 * RIM + 1
CAPACITY = 4

F32 = jnp.float32
BF16 = jnp.bfloat16
VMEM_SPEC = pl.BlockSpec(memory_space=pltpu.VMEM)
SMEM_SPEC = pl.BlockSpec(memory_space=pltpu.SMEM)
HBM_SPEC = pl.BlockSpec(memory_space=pltpu.HBM)
NT = (((1,), (1,)), ((), ()))
TN = (((0,), (0,)), ((), ()))


def call(kernel, out_shape, in_specs, scratch=(), limit=8, aliases=None):
    return pl.pallas_call(
        kernel,
        out_shape=out_shape,
        in_specs=in_specs,
        out_specs=jax.tree.map(lambda unused: VMEM_SPEC, out_shape),
        scratch_shapes=list(scratch),
        input_output_aliases=aliases or {},
        compiler_params=pltpu.CompilerParams(vmem_limit_bytes=limit << 20),
    )


def in_hbm(x):
    return pltpu.with_memory_space_constraint(x, pltpu.HBM)


def turn_by(x, axis, steps):
    n = lax.axis_size(axis)
    return lax.ppermute(x, axis, [(i, (i + steps) % n) for i in range(n)])


def shift_up(x, axis):
    n = lax.axis_size(axis)
    return lax.ppermute(x, axis, [(i, i + 1) for i in range(n - 1)])


def shift_down(x, axis):
    n = lax.axis_size(axis)
    return lax.ppermute(x, axis, [(i + 1, i) for i in range(n - 1)])


def pack_depth(species, diff, rate, low, high, held, sems):
    copies = []
    for side, first in ((0, 0), (1, 16 - HALO)):
        cut = pl.ds(first, HALO)
        for source, at in (
            (species.at[0, cut], 0),
            (species.at[1, cut], 1),
            (diff.at[cut], 2),
            (rate.at[cut], 3),
        ):
            copies.append(
                pltpu.make_async_copy(source, held.at[side, at], sems.at[4 * side + at])
            )
    for copy in copies:
        copy.start()
    for copy in copies:
        copy.wait()
    low[...] = held[0].astype(BF16)
    high[...] = held[1].astype(BF16)


def load_brick(species, diff, rate, brick, sems):
    copies = [
        pltpu.make_async_copy(
            source, brick.at[f, pl.ds(HALO, 16), pl.ds(0, 32), :], sems.at[f]
        )
        for f, source in enumerate((species.at[0], species.at[1], diff, rate))
    ]
    for copy in copies:
        copy.start()
    for f in range(4):
        brick[f, :, 32:ROWS, :] = jnp.zeros((PLANES, ROWS - 32, 128), F32)
        brick[f, HALO + 16 + HALO :, 0:32, :] = jnp.zeros((PLANES - 22, 32, 128), F32)
    for copy in copies:
        copy.wait()


def pack_rows(unused, before, after, brick, low, high):
    for f in range(4):
        brick[f, 0:HALO, 0:32, :] = before[f].astype(F32)
        brick[f, HALO + 16 : 22, 0:32, :] = after[f].astype(F32)
    lines = brick.reshape(4 * PLANES * ROWS, 128)
    for r in range(HALO):
        low[r] = lines[pl.ds(r, 4 * PLANES, stride=ROWS), :].astype(BF16)
        high[r] = lines[pl.ds(32 - HALO + r, 4 * PLANES, stride=ROWS), :].astype(BF16)


def column_picker():
    j = lax.broadcasted_iota(jnp.int32, (2 * EDGE, 128), 0)
    lane = lax.broadcasted_iota(jnp.int32, (2 * EDGE, 128), 1)
    return (lane == jnp.where(j < EDGE, j, 128 - 2 * EDGE + j)).astype(BF16)


def pack_columns(place, unused, above, below, brick, low, high):
    has_above = jnp.where(place[1] > 0, 1.0, 0.0).astype(F32)
    has_below = jnp.where(place[1] < place[4], 1.0, 0.0).astype(F32)
    lines = brick.reshape(4 * PLANES * ROWS, 128)
    for r in range(HALO):
        lines[pl.ds(ROWS - HALO + r, 4 * PLANES, stride=ROWS), :] = has_above * above[r].astype(F32)
        lines[pl.ds(32 + r, 4 * PLANES, stride=ROWS), :] = has_below * below[r].astype(F32)
    pick = column_picker()
    count = PLANES * ROWS
    for f in range(4):
        rows = brick[f].reshape(count, 128).astype(BF16)
        edge = lax.dot_general(pick, rows, NT, preferred_element_type=F32).astype(BF16)
        low[:, f * count : (f + 1) * count] = edge[:EDGE]
        high[:, f * count : (f + 1) * count] = edge[EDGE:]


def stencil(
    place,
    main,
    left,
    right,
    out,
    shifted,
    rim,
    first_main,
    first_rim,
    second_main,
    second_rim,
):
    n = ROWS
    j = lax.broadcasted_iota(jnp.int32, (EDGE, 128), 0)
    lane8 = lax.broadcasted_iota(jnp.int32, (EDGE, 128), 1)
    reach = HALO + RIM
    put_left = ((lane8 == 128 - EDGE + j) & (j >= EDGE - reach)).astype(BF16)
    put_right = ((lane8 == j) & (j < reach)).astype(BF16)
    count = PLANES * ROWS
    for f in range(4):
        cut = slice(f * count, (f + 1) * count)
        spread = lax.dot_general(
            left[:, cut], put_left, TN, preferred_element_type=F32
        ) + lax.dot_general(right[:, cut], put_right, TN, preferred_element_type=F32)
        rim[f] = spread.reshape(PLANES, ROWS, 128)

    depth_at, row_at, col_at = place[0], place[1], place[2]
    depth_last, row_last, col_last = place[3], place[4], place[5]
    row = lax.broadcasted_iota(jnp.int32, (n, 128), 0)
    lane = lax.broadcasted_iota(jnp.int32, (n, 128), 1)
    rows_in = (
        (row < 32)
        | ((row < 32 + HALO) & (row_at < row_last))
        | ((row >= n - HALO) & (row_at > 0))
    )
    lanes_in = ((lane < reach) & (col_at < col_last)) | ((lane >= 128 - reach) & (col_at > 0))
    step_main = jnp.where(rows_in, TIME_STEP, 0.0).astype(F32)
    step_rim = jnp.where(rows_in & lanes_in, TIME_STEP, 0.0).astype(F32)
    first_lane = lane == 0
    last_lane = lane == 127

    def tendency(m, r, p):
        results = []
        for part in range(2):
            here, there = (m, r) if part == 0 else (r, m)
            coefs = main if part == 0 else rim
            diffusivity = coefs[2, p]
            reaction = coefs[3, p]
            fuel, heat = here[0, p], here[1, p]
            square = heat * heat
            burned = reaction * fuel * square / (1.0 + square)
            both = []
            for f in range(2):
                centre = fuel if f == 0 else heat
                other = there[f, p]
                below_depth = here[f, p - 1]
                above_depth = here[f, p + 1]
                below_row = pltpu.roll(centre, 1, 0)
                above_row = pltpu.roll(centre, n - 1, 0)
                below_col = jnp.where(
                    first_lane, pltpu.roll(other, 1, 1), pltpu.roll(centre, 1, 1)
                )
                above_col = jnp.where(
                    last_lane, pltpu.roll(other, 127, 1), pltpu.roll(centre, 127, 1)
                )
                laplace = (
                    below_depth
                    + above_depth
                    + below_row
                    + above_row
                    + below_col
                    + above_col
                    - 6.0 * centre
                )
                advect = (
                    VEL_DEPTH * (centre - below_depth)
                    + VEL_ROW * (centre - below_row)
                    + VEL_COL * (centre - below_col)
                )
                gain = -burned if f == 0 else burned
                both.append(diffusivity * laplace - advect + gain)
            results.append(both)
        return results

    def inside(p):
        ok = ((p >= HALO) | (depth_at > 0)) & ((p < HALO + 16) | (depth_at < depth_last))
        return jnp.where(ok, 1.0, 0.0).astype(F32)

    @pl.loop(1, 21)
    def _(p):
        slope = tendency(main, rim, p)
        scale = inside(p)
        for f in range(2):
            first_main[f, p] = main[f, p] + (step_main * scale) * slope[0][f]
            first_rim[f, p] = rim[f, p] + (step_rim * scale) * slope[1][f]

    @pl.loop(2, 20)
    def _(p):
        slope = tendency(first_main, first_rim, p)
        scale = inside(p)
        for f in range(2):
            second_main[f, p] = 0.75 * main[f, p] + 0.25 * (
                first_main[f, p] + (step_main * scale) * slope[0][f]
            )
            second_rim[f, p] = 0.75 * rim[f, p] + 0.25 * (
                first_rim[f, p] + (step_rim * scale) * slope[1][f]
            )

    lane32 = lax.broadcasted_iota(jnp.int32, (32, 128), 1)

    @pl.loop(3, 19)
    def _(p):
        slope = tendency(second_main, second_rim, p)
        k = p - HALO
        for f in range(2):
            new_main = (
                main[f, p] / 3.0 + (2.0 / 3.0) * (second_main[f, p] + step_main * slope[0][f])
            )[:32]
            new_rim = (
                rim[f, p] / 3.0 + (2.0 / 3.0) * (second_rim[f, p] + step_rim * slope[1][f])
            )[:32]
            out[f, k] = new_main
            for shift in range(-RIM, RIM + 1):
                if shift == 0:
                    shifted[RIM, f, k] = new_main
                    continue
                turn = -shift % 128
                outside = lane32 >= 128 - shift if shift > 0 else lane32 < -shift
                shifted[shift + RIM, f, k] = jnp.where(
                    outside, pltpu.roll(new_rim, turn, 1), pltpu.roll(new_main, turn, 1)
                )


def render(away, place, shear, weight, bias, shifted, image):
    count = image.shape[0]
    depth_cells = shifted.shape[2]
    depth_at, depth_last = place[0], place[3]
    first = lax.rem(depth_at + away, depth_last + 1) * count
    middle = 0.5 * depth_cells * (depth_last + 1).astype(F32)

    @pl.loop(0, count)
    def _(j):
        v = first + j
        table = [
            tuple(
                (0.5 if c < 3 else 1.0) * value
                for value in (weight[c, 0, v], weight[c, 1, v], bias[c, v])
            )
            for c in range(4)
        ]
        slope = shear[v]

        for part in range(4):
            strip = slice(part * 8, (part + 1) * 8)

            def march(k, state):
                c0, c1, c2, total, through = state
                place_in_depth = (depth_at * depth_cells + k).astype(F32) + 0.5
                offset = slope * (place_in_depth - middle)
                whole = offset.astype(jnp.int32)
                whole = jnp.where(whole.astype(F32) > offset, whole - 1, whole)
                t = offset - whole.astype(F32)
                i = jnp.clip(whole + RIM, 0, SHIFTS - 2)
                s0 = (1.0 - t) * shifted[i, 0, k, strip] + t * shifted[i + 1, 0, k, strip]
                s1 = (1.0 - t) * shifted[i, 1, k, strip] + t * shifted[i + 1, 1, k, strip]
                logits = [table[c][0] * s0 + table[c][1] * s1 + table[c][2] for c in range(4)]
                dense = logits[3]
                total = total + (jnp.maximum(dense, 0.0) + jnp.log(1.0 + jnp.exp(-jnp.abs(dense))))
                after = jnp.exp2((-RAY_STEP * LOG2E) * total)
                part = through - after
                c0 = c0 + part * jnp.tanh(logits[0])
                c1 = c1 + part * jnp.tanh(logits[1])
                c2 = c2 + part * jnp.tanh(logits[2])
                return c0, c1, c2, total, after

            zero = jnp.zeros((8, 128), F32)
            c0, c1, c2, _, through = lax.fori_loop(
                0, depth_cells, march, (zero, zero, zero, zero, zero + 1.0), unroll=16
            )
            opacity = 1.0 - through
            image[j, 0, strip] = 0.5 * (c0 + opacity)
            image[j, 1, strip] = 0.5 * (c1 + opacity)
            image[j, 2, strip] = 0.5 * (c2 + opacity)
            image[j, 3, strip] = opacity


def deal(place, owners, lengths, warp, select, lengths_wide, warp_own, sem):
    views = warp_own.shape[0]
    copy = pltpu.make_async_copy(warp.at[pl.ds(place[0] * views, views)], warp_own, sem.at[0])
    copy.start()
    row = lax.broadcasted_iota(jnp.int32, (128, 128), 0)
    lane = lax.broadcasted_iota(jnp.int32, (128, 128), 1)
    name = jnp.concatenate([owners[v : v + 1, :] for v in range(views)], axis=1)
    length = jnp.concatenate([lengths[v : v + 1, :] for v in range(views)], axis=1)
    along = jnp.broadcast_to(name, (128, 128))
    across = along.T
    earlier = (along == across) & (row < lane) & (row // 32 == lane // 32)
    rank = jnp.sum(earlier.astype(F32), axis=0, keepdims=True).astype(jnp.int32)
    view = lane[0:1] // 32
    half = select.shape[0] // 2
    codes = name * (views * CAPACITY // 2) + view * (CAPACITY // 2) + rank // 2
    codes = codes + (rank % 2) * half
    slot = lax.broadcasted_iota(jnp.int32, select.shape, 0)
    select[...] = (slot == codes).astype(F32).astype(BF16)
    lengths_wide[...] = jnp.broadcast_to(length, (128, 128)).T
    copy.wait()


def composite(place, order, select, lengths, slab0, slab1, slab2, slab3, outgoing, pieces):
    lane = lax.broadcasted_iota(jnp.int32, (32, 128), 1)
    slabs = (slab0, slab1, slab2, slab3)
    depth_at, devices = place[0], place[3] + 1

    def fetch(which, v, c):
        value = slabs[3][v, c]
        for offset in (2, 1, 0):
            value = jnp.where(which == offset, slabs[offset][v, c], value)
        return value

    for v in range(4):
        keep = lane < lengths[32 * v : 32 * (v + 1), :]
        turn = [
            lax.rem(depth_at - order[position, depth_at * 4 + v] + devices, devices)
            for position in range(4)
        ]
        channels = [fetch(turn[0], v, c) for c in range(4)]
        for position in range(1, 4):
            clear = 1.0 - channels[3]
            channels = [channels[c] + clear * fetch(turn[position], v, c) for c in range(4)]
        for c in range(4):
            pieces[32 * v : 32 * (v + 1), 128 * c : 128 * (c + 1)] = jnp.where(
                keep, channels[c], 0.0
            ).astype(BF16)
    row_id = lax.broadcasted_iota(jnp.int32, (128, 128), 0) + 1
    pieces[:, 512:640] = row_id.astype(F32).astype(BF16)
    dealt = jnp.dot(select[...], pieces[...], preferred_element_type=F32).astype(BF16)
    half = outgoing.shape[0]
    outgoing[:, 0:512] = dealt[:half, 0:512]
    outgoing[:, 512:1024] = dealt[half:, 0:512]
    outgoing[:, 1024:1088] = dealt[:half, 512:576]
    outgoing[:, 1088:1152] = dealt[half:, 576:640]


def resample(incoming, warp, frame):
    rows = incoming.shape[0]
    ids = incoming[:, 1024:1152].astype(F32)
    lane = lax.broadcasted_iota(jnp.int32, (rows, 128), 1)
    swapped = pltpu.roll(ids, 64, 1)
    line = (lane + 1).astype(F32)
    total = jnp.zeros((128, 512), F32)
    for odd in range(2):
        names = jnp.where((lane < 64) == (odd == 0), ids, swapped)
        place = (names == line).astype(F32).astype(BF16)
        part = incoming[:, 512 * odd : 512 * (odd + 1)]
        total = total + lax.dot_general(place, part, TN, preferred_element_type=F32)
    for v in range(4):
        matrix = warp[v].astype(F32)
        for c in range(4):
            rows = total[32 * v : 32 * (v + 1), 128 * c : 128 * (c + 1)]
            frame[pl.ds(128 * v + c, 32, stride=4), :] = jnp.dot(
                rows, matrix, preferred_element_type=F32, precision=lax.Precision.HIGHEST
            )


def body(
    species,
    diffusivity,
    reaction_rate,
    shear_rate,
    colour_weight,
    colour_bias,
    slab_order,
    lengths,
    owners,
    warp_matrix,
):
    depth_at, row_at, col_at = (lax.axis_index(a) for a in ("depth", "row", "col"))
    depth_devices, row_devices, col_devices = (lax.axis_size(a) for a in ("depth", "row", "col"))
    view_count = shear_rate.shape[0] // depth_devices

    place = jnp.stack(
        [
            depth_at,
            row_at,
            col_at,
            jnp.int32(depth_devices - 1),
            jnp.int32(row_devices - 1),
            jnp.int32(col_devices - 1),
        ]
    ).astype(jnp.int32)
    fields = tuple(in_hbm(x) for x in (species, diffusivity, reaction_rate))

    face = jax.ShapeDtypeStruct((4, HALO, 32, 128), BF16)
    low, high = call(
        pack_depth,
        (face, face),
        [HBM_SPEC] * 3,
        [pltpu.VMEM((2, 4, HALO, 32, 128), F32), pltpu.SemaphoreType.DMA((8,))],
    )(*fields)
    before, after = shift_up(high, "depth"), shift_down(low, "depth")
    brick_type = jax.ShapeDtypeStruct((4, PLANES, ROWS, 128), F32)
    brick = call(load_brick, brick_type, [HBM_SPEC] * 3, [pltpu.SemaphoreType.DMA((4,))])(*fields)
    face = jax.ShapeDtypeStruct((HALO, 4 * PLANES, 128), BF16)
    brick, low, high = call(
        pack_rows, (brick_type, face, face), [VMEM_SPEC] * 3, aliases={0: 0}
    )(brick, before, after)
    above, below = turn_by(high, "row", 1), turn_by(low, "row", -1)
    slots = col_devices * view_count * CAPACITY
    lines = view_count * 32
    select, lengths_wide, warp_own = call(
        deal,
        (
            jax.ShapeDtypeStruct((slots, lines), BF16),
            jax.ShapeDtypeStruct((lines, 128), jnp.int32),
            jax.ShapeDtypeStruct((view_count, 128, 128), BF16),
        ),
        [SMEM_SPEC, VMEM_SPEC, VMEM_SPEC, HBM_SPEC],
        [pltpu.SemaphoreType.DMA((1,))],
    )(place, owners.reshape(view_count, 32), lengths.reshape(view_count, 32), in_hbm(warp_matrix))

    brick, select, lengths_wide, warp_own = lax.optimization_barrier(
        (brick, select, lengths_wide, warp_own)
    )
    face = jax.ShapeDtypeStruct((EDGE, 4 * PLANES * ROWS), BF16)
    brick, low, high = call(
        pack_columns, (brick_type, face, face), [SMEM_SPEC] + [VMEM_SPEC] * 3, aliases={1: 0}
    )(place, brick, above, below)
    left, right = shift_up(high, "col"), shift_down(low, "col")
    wide = pltpu.VMEM((2, PLANES, ROWS, 128), F32)
    species_out, shifted = call(
        stencil,
        (
            jax.ShapeDtypeStruct(species.shape, F32),
            jax.ShapeDtypeStruct((SHIFTS,) + species.shape, F32),
        ),
        [SMEM_SPEC] + [VMEM_SPEC] * 3,
        [pltpu.VMEM((4, PLANES, ROWS, 128), F32)] + [wide] * 4,
        limit=16,
    )(place, brick, left, right)

    image = jax.ShapeDtypeStruct((view_count, 4, 32, 128), F32)
    weight, bias = jnp.transpose(colour_weight, (1, 2, 0)), colour_bias.T
    slabs = [None] * 4
    for away in (2, 1, 3, 0):
        drawn = call(
            functools.partial(render, away), image, [SMEM_SPEC] * 4 + [VMEM_SPEC]
        )(place, shear_rate, weight, bias, shifted)
        if away:
            drawn = turn_by(drawn, "depth", away)
        slabs[away] = drawn
    outgoing = call(
        composite,
        jax.ShapeDtypeStruct((slots // 2, 1152), BF16),
        [SMEM_SPEC] * 2 + [VMEM_SPEC] * 6,
        [pltpu.VMEM((lines, 640), BF16)],
    )(place, slab_order.T, select, lengths_wide, *slabs)
    incoming = lax.all_to_all(
        outgoing.reshape(col_devices, -1, 1152),
        "col",
        split_axis=0,
        concat_axis=0,
        tiled=True,
    ).reshape(slots // 2, 1152)
    frame = call(resample, jax.ShapeDtypeStruct((4 * lines, 128), F32), [VMEM_SPEC] * 2)(
        incoming, warp_own
    )
    return species_out, frame.reshape(view_count, 32, 4, 128)


def solution(mesh):
    in_specs = (
        P(None, "depth", "row", "col"),
        P("depth", "row", "col"),
        P("depth", "row", "col"),
        P(),
        P(),
        P(),
        P(),
        P("depth", "col", "row"),
        P("depth", "col", "row", None),
        P(),
    )
    out_specs = (P(None, "depth", "row", "col"), P("depth", "row", None, "col"))
    return jax.shard_map(body, mesh=mesh, in_specs=in_specs, out_specs=out_specs, check_vma=False)
```

```python
import functools

import jax
import jax.numpy as jnp
from jax import lax
from jax.experimental import pallas as pl
from jax.experimental.pallas import tpu as pltpu
from jax.sharding import PartitionSpec as P

TIME_STEP = 0.1
RAY_STEP = 0.02
LOG2E = 1.4426950408889634
VEL_DEPTH = 0.3
VEL_ROW = 0.2
VEL_COL = 0.4

HALO = 3
RIM = 3
EDGE = 8
PLANES = 24
ROWS = 40
LINES = 1024
SHIFTS = 2 * RIM + 1
CAPACITY = 4

F32 = jnp.float32
BF16 = jnp.bfloat16
VMEM_SPEC = pl.BlockSpec(memory_space=pltpu.VMEM)
SMEM_SPEC = pl.BlockSpec(memory_space=pltpu.SMEM)
HBM_SPEC = pl.BlockSpec(memory_space=pltpu.HBM)
NT = (((1,), (1,)), ((), ()))
TN = (((0,), (0,)), ((), ()))


def call(kernel, out_shape, in_specs, scratch=(), limit=8, aliases=None):
    return pl.pallas_call(
        kernel,
        out_shape=out_shape,
        in_specs=in_specs,
        out_specs=jax.tree.map(lambda unused: VMEM_SPEC, out_shape),
        scratch_shapes=list(scratch),
        input_output_aliases=aliases or {},
        compiler_params=pltpu.CompilerParams(vmem_limit_bytes=limit << 20),
    )


def in_hbm(x):
    return pltpu.with_memory_space_constraint(x, pltpu.HBM)


def turn_by(x, axis, steps):
    n = lax.axis_size(axis)
    return lax.ppermute(x, axis, [(i, (i + steps) % n) for i in range(n)])


def shift_up(x, axis):
    n = lax.axis_size(axis)
    return lax.ppermute(x, axis, [(i, i + 1) for i in range(n - 1)])


def shift_down(x, axis):
    n = lax.axis_size(axis)
    return lax.ppermute(x, axis, [(i + 1, i) for i in range(n - 1)])


def pack_depth(species, diff, rate, low, high, held, sems):
    copies = []
    for side, first in ((0, 0), (1, 16 - HALO)):
        cut = pl.ds(first, HALO)
        for source, at in (
            (species.at[0, cut], 0),
            (species.at[1, cut], 1),
            (diff.at[cut], 2),
            (rate.at[cut], 3),
        ):
            copies.append(
                pltpu.make_async_copy(source, held.at[side, at], sems.at[4 * side + at])
            )
    for copy in copies:
        copy.start()
    for copy in copies:
        copy.wait()
    low[...] = held[0].astype(BF16)
    high[...] = held[1].astype(BF16)


def load_brick(species, diff, rate, brick, sems):
    copies = [
        pltpu.make_async_copy(
            source, brick.at[f, pl.ds(HALO, 16), pl.ds(0, 32), :], sems.at[f]
        )
        for f, source in enumerate((species.at[0], species.at[1], diff, rate))
    ]
    for copy in copies:
        copy.start()
    for f in range(4):
        brick[f, :, 32:ROWS, :] = jnp.zeros((PLANES, ROWS - 32, 128), F32)
        brick[f, HALO + 16 + HALO :, 0:32, :] = jnp.zeros((PLANES - 22, 32, 128), F32)
    for copy in copies:
        copy.wait()


def pack_rows(unused, before, after, brick, low, high):
    for f in range(4):
        brick[f, 0:HALO, 0:32, :] = before[f].astype(F32)
        brick[f, HALO + 16 : 22, 0:32, :] = after[f].astype(F32)
    lines = brick.reshape(4 * PLANES * ROWS, 128)
    for r in range(HALO):
        low[r] = lines[pl.ds(r, 4 * PLANES, stride=ROWS), :].astype(BF16)
        high[r] = lines[pl.ds(32 - HALO + r, 4 * PLANES, stride=ROWS), :].astype(BF16)


def column_picker():
    j = lax.broadcasted_iota(jnp.int32, (2 * EDGE, 128), 0)
    lane = lax.broadcasted_iota(jnp.int32, (2 * EDGE, 128), 1)
    return (lane == jnp.where(j < EDGE, j, 128 - 2 * EDGE + j)).astype(F32)


def pack_columns(place, unused, above, below, brick, low, high):
    has_above = jnp.where(place[1] > 0, 1.0, 0.0).astype(F32)
    has_below = jnp.where(place[1] < place[4], 1.0, 0.0).astype(F32)
    lines = brick.reshape(4 * PLANES * ROWS, 128)
    for r in range(HALO):
        lines[pl.ds(ROWS - HALO + r, 4 * PLANES, stride=ROWS), :] = has_above * above[r].astype(F32)
        lines[pl.ds(32 + r, 4 * PLANES, stride=ROWS), :] = has_below * below[r].astype(F32)
    pick = column_picker().astype(BF16)
    count = PLANES * ROWS
    for f in range(4):
        rows = brick[f].reshape(count, 128).astype(BF16)
        edge = lax.dot_general(pick, rows, NT, preferred_element_type=F32).astype(BF16)
        at = f * LINES
        low[:, at : at + count] = edge[:EDGE]
        high[:, at : at + count] = edge[EDGE:]
        low[:, at + count : at + LINES] = jnp.zeros((EDGE, LINES - count), BF16)
        high[:, at + count : at + LINES] = jnp.zeros((EDGE, LINES - count), BF16)


def slope_of(fields, diffusivity, reaction, neighbours):
    fuel, heat = fields
    square = heat * heat
    burned = reaction * fuel * square / (1.0 + square)
    slopes = []
    for f in range(2):
        centre = fields[f]
        below_depth, above_depth, below_row, above_row, below_col, above_col = neighbours(f)
        laplace = (
            below_depth + above_depth + below_row + above_row + below_col + above_col - 6.0 * centre
        )
        advect = (
            VEL_DEPTH * (centre - below_depth)
            + VEL_ROW * (centre - below_row)
            + VEL_COL * (centre - below_col)
        )
        gain = -burned if f == 0 else burned
        slopes.append(diffusivity * laplace - advect + gain)
    return slopes


def advance_own(place, brick, shifted, edges, first, second):
    n = ROWS
    depth_at, row_at = place[0], place[1]
    depth_last, row_last = place[3], place[4]
    row = lax.broadcasted_iota(jnp.int32, (n, 128), 0)
    rows_in = (
        (row < 32)
        | ((row < 32 + HALO) & (row_at < row_last))
        | ((row >= n - HALO) & (row_at > 0))
    )
    step = jnp.where(rows_in, TIME_STEP, 0.0).astype(F32)

    def tendency(source, p):
        def neighbours(f):
            centre = source[f, p]
            return (
                source[f, p - 1],
                source[f, p + 1],
                pltpu.roll(centre, 1, 0),
                pltpu.roll(centre, n - 1, 0),
                pltpu.roll(centre, 1, 1),
                pltpu.roll(centre, 127, 1),
            )

        return slope_of((source[0, p], source[1, p]), brick[2, p], brick[3, p], neighbours)

    def inside(p):
        ok = ((p >= HALO) | (depth_at > 0)) & ((p < HALO + 16) | (depth_at < depth_last))
        return jnp.where(ok, 1.0, 0.0).astype(F32)

    @pl.loop(1, 21)
    def _(p):
        slope = tendency(brick, p)
        scale = inside(p)
        for f in range(2):
            first[f, p] = brick[f, p] + (step * scale) * slope[f]

    @pl.loop(2, 20)
    def _(p):
        slope = tendency(first, p)
        scale = inside(p)
        for f in range(2):
            second[f, p] = 0.75 * brick[f, p] + 0.25 * (first[f, p] + (step * scale) * slope[f])

    @pl.loop(3, 19)
    def _(p):
        slope = tendency(second, p)
        k = p - HALO
        for f in range(2):
            new = (brick[f, p] / 3.0 + (2.0 / 3.0) * (second[f, p] + step * slope[f]))[:32]
            for shift in range(-RIM, RIM + 1):
                shifted[shift + RIM, f, k] = pltpu.roll(new, -shift % 128, 1) if shift else new

    pick = column_picker()
    count = PLANES * ROWS
    for f in range(2):
        edges[:, f * LINES : f * LINES + count] = lax.dot_general(
            pick,
            brick[f].reshape(count, 128),
            NT,
            preferred_element_type=F32,
            precision=lax.Precision.HIGHEST,
        )
        edges[:, f * LINES + count : (f + 1) * LINES] = jnp.zeros((2 * EDGE, LINES - count), F32)


def advance_edges(place, unused, edges, low, high, left, right, shifted, out, turned):
    row_at, col_at, depth_at = place[1], place[2], place[0]
    depth_last, row_last, col_last = place[3], place[4], place[5]
    shape = (4 * EDGE, LINES)
    col = lax.broadcasted_iota(jnp.int32, shape, 0)
    lane = lax.broadcasted_iota(jnp.int32, shape, 1)
    plane = jnp.floor((lane.astype(F32) + 0.5) * (1.0 / ROWS)).astype(jnp.int32)
    row = lane - plane * ROWS
    rows_in = (
        (row < 32)
        | ((row < 32 + HALO) & (row_at < row_last))
        | ((row >= ROWS - HALO) & (row_at > 0))
    )
    cols_in = ((col >= EDGE) | (col_at > 0)) & ((col < 3 * EDGE) | (col_at < col_last))
    planes_in = ((plane >= HALO) | (depth_at > 0)) & (
        (plane < HALO + 16) | ((plane < 22) & (depth_at < depth_last))
    )
    step = jnp.where(rows_in & cols_in & planes_in, TIME_STEP, 0.0).astype(F32)
    first_row, last_row = row == 0, row == ROWS - 1

    def gather(f):
        cut = slice(f * LINES, (f + 1) * LINES)
        if f < 2:
            own = (edges[0:EDGE, cut], edges[EDGE : 2 * EDGE, cut])
        else:
            own = (low[:, cut].astype(F32), high[:, cut].astype(F32))
        return jnp.concatenate(
            [left[:, cut].astype(F32), own[0], own[1], right[:, cut].astype(F32)], axis=0
        )

    start = (gather(0), gather(1))
    diffusivity, reaction = gather(2), gather(3)

    def tendency(fields):
        def neighbours(f):
            x = fields[f]
            return (
                pltpu.roll(x, ROWS, 1),
                pltpu.roll(x, LINES - ROWS, 1),
                jnp.where(first_row, pltpu.roll(x, LINES - ROWS + 1, 1), pltpu.roll(x, 1, 1)),
                jnp.where(last_row, pltpu.roll(x, ROWS - 1, 1), pltpu.roll(x, LINES - 1, 1)),
                pltpu.roll(x, 1, 0),
                pltpu.roll(x, 4 * EDGE - 1, 0),
            )

        return slope_of(fields, diffusivity, reaction, neighbours)

    slope = tendency(start)
    first = tuple(start[f] + step * slope[f] for f in range(2))
    slope = tendency(first)
    second = tuple(0.75 * start[f] + 0.25 * (first[f] + step * slope[f]) for f in range(2))
    slope = tendency(second)
    blank = jnp.zeros((128 - 4 * EDGE, 128), F32)
    for f in range(2):
        new = start[f] / 3.0 + (2.0 / 3.0) * (second[f] + step * slope[f])
        for block in range(LINES // 128):
            cut = slice(128 * block, 128 * (block + 1))
            turned[f, cut, :] = jnp.concatenate([new[:, cut], blank], axis=0).T

    lane = lax.broadcasted_iota(jnp.int32, (32, 128), 1)

    @pl.loop(0, 16)
    def _(k):
        for f in range(2):
            lines = turned[f, pl.ds(pl.multiple_of((k + HALO) * ROWS, 8), 32), :]
            near = pltpu.roll(lines, 128 - EDGE, 1)
            far = pltpu.roll(lines, 128 - 3 * EDGE, 1)
            for shift in range(-RIM, RIM + 1):
                from_far = (lane >= 64) & (lane < 128 + min(shift, 0)) | (lane < shift)
                patch = jnp.where(from_far, far, near)
                patch = pltpu.roll(patch, -shift % 128, 1) if shift else patch
                wrong = (lane <= RIM - 1 - shift) | (lane >= 128 - RIM - shift)
                value = jnp.where(wrong, patch, shifted[shift + RIM, f, k])
                shifted[shift + RIM, f, k] = value
                if shift == 0:
                    out[f, k] = value


def render(away, place, shear, weight, bias, shifted, image):
    count = image.shape[0]
    depth_cells = shifted.shape[2]
    depth_at, depth_last = place[0], place[3]
    first = lax.rem(depth_at + away, depth_last + 1) * count
    middle = 0.5 * depth_cells * (depth_last + 1).astype(F32)

    @pl.loop(0, count)
    def _(j):
        v = first + j
        table = [
            tuple(
                (0.5 if c < 3 else 1.0) * value
                for value in (weight[c, 0, v], weight[c, 1, v], bias[c, v])
            )
            for c in range(4)
        ]
        slope = shear[v]

        for part in range(4):
            strip = slice(part * 8, (part + 1) * 8)

            def march(k, state):
                c0, c1, c2, total, through = state
                place_in_depth = (depth_at * depth_cells + k).astype(F32) + 0.5
                offset = slope * (place_in_depth - middle)
                whole = offset.astype(jnp.int32)
                whole = jnp.where(whole.astype(F32) > offset, whole - 1, whole)
                t = offset - whole.astype(F32)
                i = jnp.clip(whole + RIM, 0, SHIFTS - 2)
                s0 = (1.0 - t) * shifted[i, 0, k, strip] + t * shifted[i + 1, 0, k, strip]
                s1 = (1.0 - t) * shifted[i, 1, k, strip] + t * shifted[i + 1, 1, k, strip]
                logits = [table[c][0] * s0 + table[c][1] * s1 + table[c][2] for c in range(4)]
                dense = logits[3]
                total = total + (jnp.maximum(dense, 0.0) + jnp.log(1.0 + jnp.exp(-jnp.abs(dense))))
                after = jnp.exp2((-RAY_STEP * LOG2E) * total)
                part = through - after
                c0 = c0 + part * jnp.tanh(logits[0])
                c1 = c1 + part * jnp.tanh(logits[1])
                c2 = c2 + part * jnp.tanh(logits[2])
                return c0, c1, c2, total, after

            zero = jnp.zeros((8, 128), F32)
            c0, c1, c2, _, through = lax.fori_loop(
                0, depth_cells, march, (zero, zero, zero, zero, zero + 1.0), unroll=16
            )
            opacity = 1.0 - through
            image[j, 0, strip] = 0.5 * (c0 + opacity)
            image[j, 1, strip] = 0.5 * (c1 + opacity)
            image[j, 2, strip] = 0.5 * (c2 + opacity)
            image[j, 3, strip] = opacity


def deal(place, owners, lengths, warp, select, lengths_wide, warp_own, sem):
    views = warp_own.shape[0]
    copy = pltpu.make_async_copy(warp.at[pl.ds(place[0] * views, views)], warp_own, sem.at[0])
    copy.start()
    row = lax.broadcasted_iota(jnp.int32, (128, 128), 0)
    lane = lax.broadcasted_iota(jnp.int32, (128, 128), 1)
    name = jnp.concatenate([owners[v : v + 1, :] for v in range(views)], axis=1)
    length = jnp.concatenate([lengths[v : v + 1, :] for v in range(views)], axis=1)
    along = jnp.broadcast_to(name, (128, 128))
    across = along.T
    earlier = (along == across) & (row < lane) & (row // 32 == lane // 32)
    rank = jnp.sum(earlier.astype(F32), axis=0, keepdims=True).astype(jnp.int32)
    view = lane[0:1] // 32
    half = select.shape[0] // 2
    codes = name * (views * CAPACITY // 2) + view * (CAPACITY // 2) + rank // 2
    codes = codes + (rank % 2) * half
    slot = lax.broadcasted_iota(jnp.int32, select.shape, 0)
    select[...] = (slot == codes).astype(F32).astype(BF16)
    lengths_wide[...] = jnp.broadcast_to(length, (128, 128)).T
    copy.wait()


def composite(place, order, select, lengths, slab0, slab1, slab2, slab3, outgoing, pieces):
    lane = lax.broadcasted_iota(jnp.int32, (32, 128), 1)
    slabs = (slab0, slab1, slab2, slab3)
    depth_at, devices = place[0], place[3] + 1

    def fetch(which, v, c):
        value = slabs[3][v, c]
        for offset in (2, 1, 0):
            value = jnp.where(which == offset, slabs[offset][v, c], value)
        return value

    for v in range(4):
        keep = lane < lengths[32 * v : 32 * (v + 1), :]
        turn = [
            lax.rem(depth_at - order[position, depth_at * 4 + v] + devices, devices)
            for position in range(4)
        ]
        channels = [fetch(turn[0], v, c) for c in range(4)]
        for position in range(1, 4):
            clear = 1.0 - channels[3]
            channels = [channels[c] + clear * fetch(turn[position], v, c) for c in range(4)]
        for c in range(4):
            pieces[32 * v : 32 * (v + 1), 128 * c : 128 * (c + 1)] = jnp.where(
                keep, channels[c], 0.0
            ).astype(BF16)
    row_id = lax.broadcasted_iota(jnp.int32, (128, 128), 0) + 1
    pieces[:, 512:640] = row_id.astype(F32).astype(BF16)
    dealt = jnp.dot(select[...], pieces[...], preferred_element_type=F32).astype(BF16)
    half = outgoing.shape[0]
    outgoing[:, 0:512] = dealt[:half, 0:512]
    outgoing[:, 512:1024] = dealt[half:, 0:512]
    outgoing[:, 1024:1088] = dealt[:half, 512:576]
    outgoing[:, 1088:1152] = dealt[half:, 576:640]


def resample(incoming, warp, frame):
    rows = incoming.shape[0]
    ids = incoming[:, 1024:1152].astype(F32)
    lane = lax.broadcasted_iota(jnp.int32, (rows, 128), 1)
    swapped = pltpu.roll(ids, 64, 1)
    line = (lane + 1).astype(F32)
    total = jnp.zeros((128, 512), F32)
    for odd in range(2):
        names = jnp.where((lane < 64) == (odd == 0), ids, swapped)
        place = (names == line).astype(F32).astype(BF16)
        part = incoming[:, 512 * odd : 512 * (odd + 1)]
        total = total + lax.dot_general(place, part, TN, preferred_element_type=F32)
    for v in range(4):
        matrix = warp[v].astype(F32)
        for c in range(4):
            rows = total[32 * v : 32 * (v + 1), 128 * c : 128 * (c + 1)]
            frame[pl.ds(128 * v + c, 32, stride=4), :] = jnp.dot(
                rows, matrix, preferred_element_type=F32, precision=lax.Precision.HIGHEST
            )


def body(
    species,
    diffusivity,
    reaction_rate,
    shear_rate,
    colour_weight,
    colour_bias,
    slab_order,
    lengths,
    owners,
    warp_matrix,
):
    depth_at, row_at, col_at = (lax.axis_index(a) for a in ("depth", "row", "col"))
    depth_devices, row_devices, col_devices = (lax.axis_size(a) for a in ("depth", "row", "col"))
    view_count = shear_rate.shape[0] // depth_devices

    place = jnp.stack(
        [
            depth_at,
            row_at,
            col_at,
            jnp.int32(depth_devices - 1),
            jnp.int32(row_devices - 1),
            jnp.int32(col_devices - 1),
        ]
    ).astype(jnp.int32)
    fields = tuple(in_hbm(x) for x in (species, diffusivity, reaction_rate))

    face = jax.ShapeDtypeStruct((4, HALO, 32, 128), BF16)
    low, high = call(
        pack_depth,
        (face, face),
        [HBM_SPEC] * 3,
        [pltpu.VMEM((2, 4, HALO, 32, 128), F32), pltpu.SemaphoreType.DMA((8,))],
    )(*fields)
    before, after = shift_up(high, "depth"), shift_down(low, "depth")
    brick_type = jax.ShapeDtypeStruct((4, PLANES, ROWS, 128), F32)
    brick = call(load_brick, brick_type, [HBM_SPEC] * 3, [pltpu.SemaphoreType.DMA((4,))])(*fields)
    face = jax.ShapeDtypeStruct((HALO, 4 * PLANES, 128), BF16)
    brick, low, high = call(
        pack_rows, (brick_type, face, face), [VMEM_SPEC] * 3, aliases={0: 0}
    )(brick, before, after)
    above, below = turn_by(high, "row", 1), turn_by(low, "row", -1)
    slots = col_devices * view_count * CAPACITY
    lines = view_count * 32
    select, lengths_wide, warp_own = call(
        deal,
        (
            jax.ShapeDtypeStruct((slots, lines), BF16),
            jax.ShapeDtypeStruct((lines, 128), jnp.int32),
            jax.ShapeDtypeStruct((view_count, 128, 128), BF16),
        ),
        [SMEM_SPEC, VMEM_SPEC, VMEM_SPEC, HBM_SPEC],
        [pltpu.SemaphoreType.DMA((1,))],
    )(place, owners.reshape(view_count, 32), lengths.reshape(view_count, 32), in_hbm(warp_matrix))

    brick, select, lengths_wide, warp_own = lax.optimization_barrier(
        (brick, select, lengths_wide, warp_own)
    )
    face = jax.ShapeDtypeStruct((EDGE, 4 * LINES), BF16)
    brick, low, high = call(
        pack_columns, (brick_type, face, face), [SMEM_SPEC] + [VMEM_SPEC] * 3, aliases={1: 0}
    )(place, brick, above, below)
    left = shift_up(high, "col")
    right = shift_down(low, "col")
    wide = pltpu.VMEM((2, PLANES, ROWS, 128), F32)
    shifted_type = jax.ShapeDtypeStruct((SHIFTS,) + species.shape, F32)
    shifted, edges = call(
        advance_own,
        (shifted_type, jax.ShapeDtypeStruct((2 * EDGE, 2 * LINES), F32)),
        [SMEM_SPEC, VMEM_SPEC],
        [wide, wide],
    )(place, brick)
    shifted, species_out = call(
        advance_edges,
        (shifted_type, jax.ShapeDtypeStruct(species.shape, F32)),
        [SMEM_SPEC] + [VMEM_SPEC] * 6,
        [pltpu.VMEM((2, LINES, 128), F32)],
        aliases={1: 0},
    )(place, shifted, edges, low, high, left, right)

    image = jax.ShapeDtypeStruct((view_count, 4, 32, 128), F32)
    weight, bias = jnp.transpose(colour_weight, (1, 2, 0)), colour_bias.T
    slabs = [None] * 4
    for away in (2, 1, 3, 0):
        drawn = call(
            functools.partial(render, away), image, [SMEM_SPEC] * 4 + [VMEM_SPEC]
        )(place, shear_rate, weight, bias, shifted)
        if away:
            drawn = turn_by(drawn, "depth", away)
        slabs[away] = drawn
    outgoing = call(
        composite,
        jax.ShapeDtypeStruct((slots // 2, 1152), BF16),
        [SMEM_SPEC] * 2 + [VMEM_SPEC] * 6,
        [pltpu.VMEM((lines, 640), BF16)],
    )(place, slab_order.T, select, lengths_wide, *slabs)
    incoming = lax.all_to_all(
        outgoing.reshape(col_devices, -1, 1152),
        "col",
        split_axis=0,
        concat_axis=0,
        tiled=True,
    ).reshape(slots // 2, 1152)
    frame = call(resample, jax.ShapeDtypeStruct((4 * lines, 128), F32), [VMEM_SPEC] * 2)(
        incoming, warp_own
    )
    return species_out, frame.reshape(view_count, 32, 4, 128)


def solution(mesh):
    in_specs = (
        P(None, "depth", "row", "col"),
        P("depth", "row", "col"),
        P("depth", "row", "col"),
        P(),
        P(),
        P(),
        P(),
        P("depth", "col", "row"),
        P("depth", "col", "row", None),
        P(),
    )
    out_specs = (P(None, "depth", "row", "col"), P("depth", "row", None, "col"))
    return jax.shard_map(body, mesh=mesh, in_specs=in_specs, out_specs=out_specs, check_vma=False)
```

```python
import functools

import jax
import jax.numpy as jnp
from jax import lax
from jax.experimental import pallas as pl
from jax.experimental.pallas import tpu as pltpu
from jax.sharding import PartitionSpec as P

TIME_STEP = 0.1
RAY_STEP = 0.02
LOG2E = 1.4426950408889634
VEL_DEPTH = 0.3
VEL_ROW = 0.2
VEL_COL = 0.4

HALO = 3
RIM = 3
EDGE = 6
PLANES = 22
ROWS = 40
LINES = 896
BLOCKS = LINES // 128
SHIFTS = 2 * RIM + 1
CAPACITY = 4

F32 = jnp.float32
BF16 = jnp.bfloat16
VMEM_SPEC = pl.BlockSpec(memory_space=pltpu.VMEM)
SMEM_SPEC = pl.BlockSpec(memory_space=pltpu.SMEM)
HBM_SPEC = pl.BlockSpec(memory_space=pltpu.HBM)
NT = (((1,), (1,)), ((), ()))
TN = (((0,), (0,)), ((), ()))


def call(kernel, out_shape, in_specs, scratch=(), limit=8, aliases=None):
    return pl.pallas_call(
        kernel,
        out_shape=out_shape,
        in_specs=in_specs,
        out_specs=jax.tree.map(lambda unused: VMEM_SPEC, out_shape),
        scratch_shapes=list(scratch),
        input_output_aliases=aliases or {},
        compiler_params=pltpu.CompilerParams(vmem_limit_bytes=limit << 20),
    )


def in_hbm(x):
    return pltpu.with_memory_space_constraint(x, pltpu.HBM)


def turn_by(x, axis, steps):
    n = lax.axis_size(axis)
    return lax.ppermute(x, axis, [(i, (i + steps) % n) for i in range(n)])


def shift_up(x, axis):
    n = lax.axis_size(axis)
    return lax.ppermute(x, axis, [(i, i + 1) for i in range(n - 1)])


def shift_down(x, axis):
    n = lax.axis_size(axis)
    return lax.ppermute(x, axis, [(i + 1, i) for i in range(n - 1)])


def pack_depth(species, diff, rate, low, high, held, sems):
    copies = []
    for side, first in ((0, 0), (1, 16 - HALO)):
        cut = pl.ds(first, HALO)
        for source, at in (
            (species.at[0, cut], 0),
            (species.at[1, cut], 1),
            (diff.at[cut], 2),
            (rate.at[cut], 3),
        ):
            copies.append(
                pltpu.make_async_copy(source, held.at[side, at], sems.at[4 * side + at])
            )
    for copy in copies:
        copy.start()
    for copy in copies:
        copy.wait()
    low[...] = held[0].astype(BF16)
    high[...] = held[1].astype(BF16)


def load_brick(species, diff, rate, brick, sems):
    copies = [
        pltpu.make_async_copy(
            source, brick.at[f, pl.ds(HALO, 16), pl.ds(0, 32), :], sems.at[f]
        )
        for f, source in enumerate((species.at[0], species.at[1], diff, rate))
    ]
    for copy in copies:
        copy.start()
    for f in range(4):
        brick[f, :, 32:ROWS, :] = jnp.zeros((PLANES, ROWS - 32, 128), F32)
    for copy in copies:
        copy.wait()


def pack_rows(unused, before, after, brick, low, high):
    for f in range(4):
        brick[f, 0:HALO, 0:32, :] = before[f].astype(F32)
        brick[f, HALO + 16 : 22, 0:32, :] = after[f].astype(F32)
    lines = brick.reshape(4 * PLANES * ROWS, 128)
    for r in range(HALO):
        low[r] = lines[pl.ds(r, 4 * PLANES, stride=ROWS), :].astype(BF16)
        high[r] = lines[pl.ds(32 - HALO + r, 4 * PLANES, stride=ROWS), :].astype(BF16)


def column_picker(first_low, first_high):
    j = lax.broadcasted_iota(jnp.int32, (16, 128), 0)
    lane = lax.broadcasted_iota(jnp.int32, (16, 128), 1)
    at = jnp.where(j < 8, first_low + j, first_high + j - 8)
    return ((lane == at) & (j % 8 < EDGE)).astype(F32).astype(BF16)


def pack_columns(place, unused, above, below, brick, low, high):
    has_above = jnp.where(place[1] > 0, 1.0, 0.0).astype(F32)
    has_below = jnp.where(place[1] < place[4], 1.0, 0.0).astype(F32)
    lines = brick.reshape(4 * PLANES * ROWS, 128)
    for r in range(HALO):
        lines[pl.ds(ROWS - HALO + r, 4 * PLANES, stride=ROWS), :] = has_above * above[r].astype(F32)
        lines[pl.ds(32 + r, 4 * PLANES, stride=ROWS), :] = has_below * below[r].astype(F32)
    pick = column_picker(0, 128 - EDGE)
    count = PLANES * ROWS
    blank = jnp.zeros((8, LINES - count), BF16)
    for f in range(4):
        rows = brick[f].reshape(count, 128).astype(BF16)
        edge = lax.dot_general(pick, rows, NT, preferred_element_type=F32).astype(BF16)
        at = f * LINES
        for side, part in ((low, edge[:8]), (high, edge[8:])):
            side[:, at : at + count] = part
            side[:, at + count : at + LINES] = blank


def slope_of(fields, diffusivity, reaction, neighbours):
    fuel, heat = fields
    square = heat * heat
    burned = reaction * fuel * square / (1.0 + square)
    slopes = []
    for f in range(2):
        centre = fields[f]
        below_depth, above_depth, below_row, above_row, below_col, above_col = neighbours(f)
        laplace = (
            below_depth + above_depth + below_row + above_row + below_col + above_col - 6.0 * centre
        )
        advect = (
            VEL_DEPTH * (centre - below_depth)
            + VEL_ROW * (centre - below_row)
            + VEL_COL * (centre - below_col)
        )
        gain = -burned if f == 0 else burned
        slopes.append(diffusivity * laplace - advect + gain)
    return slopes


def advance_own(place, brick, shifted, edges, first, second):
    n = ROWS
    depth_at, row_at = place[0], place[1]
    depth_last, row_last = place[3], place[4]
    row = lax.broadcasted_iota(jnp.int32, (n, 128), 0)
    rows_in = (
        (row < 32)
        | ((row < 32 + HALO) & (row_at < row_last))
        | ((row >= n - HALO) & (row_at > 0))
    )
    step = jnp.where(rows_in, TIME_STEP, 0.0).astype(F32)

    def tendency(source, p):
        def neighbours(f):
            centre = source[f, p]
            return (
                source[f, p - 1],
                source[f, p + 1],
                pltpu.roll(centre, 1, 0),
                pltpu.roll(centre, n - 1, 0),
                pltpu.roll(centre, 1, 1),
                pltpu.roll(centre, 127, 1),
            )

        return slope_of((source[0, p], source[1, p]), brick[2, p], brick[3, p], neighbours)

    def inside(p):
        ok = ((p >= HALO) | (depth_at > 0)) & ((p < HALO + 16) | (depth_at < depth_last))
        return jnp.where(ok, 1.0, 0.0).astype(F32)

    @pl.loop(1, 21, unroll=2)
    def _(p):
        slope = tendency(brick, p)
        scale = inside(p)
        for f in range(2):
            first[f, p] = brick[f, p] + (step * scale) * slope[f]

    @pl.loop(2, 20, unroll=2)
    def _(p):
        slope = tendency(first, p)
        scale = inside(p)
        for f in range(2):
            second[f, p] = 0.75 * brick[f, p] + 0.25 * (first[f, p] + (step * scale) * slope[f])

    @pl.loop(3, 19, unroll=2)
    def _(p):
        slope = tendency(second, p)
        k = p - HALO
        for f in range(2):
            new = (brick[f, p] / 3.0 + (2.0 / 3.0) * (second[f, p] + step * slope[f]))[:32]
            for shift in range(-RIM, RIM + 1):
                shifted[shift + RIM, f, k] = pltpu.roll(new, -shift % 128, 1) if shift else new

    pick = column_picker(0, 128 - EDGE)
    count = PLANES * ROWS
    for f in range(2):
        rows = brick[f].reshape(count, 128)
        rest = (rows - rows.astype(BF16).astype(F32)).astype(BF16)
        edges[:, f * LINES : f * LINES + count] = lax.dot_general(
            pick, rest, NT, preferred_element_type=F32
        )
        edges[:, f * LINES + count : (f + 1) * LINES] = jnp.zeros((16, LINES - count), F32)


def advance_edges(
    place, unused, edges, low, high, left, right, shifted, out, start, coefs, first, second, turned
):
    row_at, col_at, depth_at = place[1], place[2], place[0]
    depth_last, row_last, col_last = place[3], place[4], place[5]
    shape = (4 * EDGE, 128)
    col = lax.broadcasted_iota(jnp.int32, shape, 0)
    lane = lax.broadcasted_iota(jnp.int32, shape, 1)
    cols_in = ((col >= EDGE) | (col_at > 0)) & ((col < 3 * EDGE) | (col_at < col_last))

    def table(b):
        line = lane + 128 * b
        plane = jnp.floor((line.astype(F32) + 0.5) * (1.0 / ROWS)).astype(jnp.int32)
        row = line - plane * ROWS
        rows_in = (
            (row < 32)
            | ((row < 32 + HALO) & (row_at < row_last))
            | ((row >= ROWS - HALO) & (row_at > 0))
        )
        planes_in = ((plane >= HALO) | (depth_at > 0)) & (
            (plane < HALO + 16) | ((plane < PLANES) & (depth_at < depth_last))
        )
        step = jnp.where(rows_in & cols_in & planes_in, TIME_STEP, 0.0).astype(F32)
        return step, row == 0, row == ROWS - 1

    for f in range(4):
        for b in range(BLOCKS):
            cut = slice(f * LINES + 128 * b, f * LINES + 128 * (b + 1))
            own_low, own_high = low[:, cut].astype(F32), high[:, cut].astype(F32)
            if f < 2:
                own_low = own_low + edges[0:8, cut]
                own_high = own_high + edges[8:16, cut]
            gathered = jnp.concatenate(
                [
                    left[:, cut].astype(F32)[:EDGE],
                    own_low[:EDGE],
                    own_high[:EDGE],
                    right[:, cut].astype(F32)[:EDGE],
                ],
                axis=0,
            )
            if f < 2:
                start[f, b] = gathered
            else:
                coefs[f - 2, b] = gathered

    def stage(source, finish):
        held = {}

        def turn(f, b, by):
            b = b % BLOCKS
            if (f, b, by) not in held:
                held[f, b, by] = pltpu.roll(source[f, b], by, 1)
            return held[f, b, by]

        def from_before(f, b, by):
            return jnp.where(lane < by, turn(f, b - 1, by), turn(f, b, by))

        def from_after(f, b, by):
            return jnp.where(lane >= 128 - by, turn(f, b + 1, 128 - by), turn(f, b, 128 - by))

        for b in range(BLOCKS):
            step, first_row, last_row = table(b)

            def neighbours(f):
                x = source[f, b]
                return (
                    from_before(f, b, ROWS),
                    from_after(f, b, ROWS),
                    jnp.where(first_row, from_after(f, b, ROWS - 1), from_before(f, b, 1)),
                    jnp.where(last_row, from_before(f, b, ROWS - 1), from_after(f, b, 1)),
                    pltpu.roll(x, 1, 0),
                    pltpu.roll(x, 4 * EDGE - 1, 0),
                )

            slope = slope_of((source[0, b], source[1, b]), coefs[0, b], coefs[1, b], neighbours)
            for f in range(2):
                finish(f, b, step * slope[f])

    def finish_first(f, b, change):
        first[f, b] = start[f, b] + change

    def finish_second(f, b, change):
        second[f, b] = 0.75 * start[f, b] + 0.25 * (first[f, b] + change)

    blank = jnp.zeros((128 - 4 * EDGE, 128), F32)

    def finish_third(f, b, change):
        new = start[f, b] / 3.0 + (2.0 / 3.0) * (second[f, b] + change)
        turned[f, 128 * b : 128 * (b + 1), :] = jnp.concatenate([new, blank], axis=0).T

    stage(start, finish_first)
    stage(first, finish_second)
    stage(second, finish_third)
    lane32 = lax.broadcasted_iota(jnp.int32, (32, 128), 1)

    @pl.loop(0, 16, unroll=2)
    def _(k):
        for f in range(2):
            lines = turned[f, pl.ds(pl.multiple_of((k + HALO) * ROWS, 8), 32), :]
            near = pltpu.roll(lines, 128 - EDGE, 1)
            far = pltpu.roll(lines, 128 - 3 * EDGE, 1)
            for shift in range(-RIM, RIM + 1):
                from_far = (lane32 >= 64) & (lane32 < 128 + min(shift, 0)) | (lane32 < shift)
                patch = jnp.where(from_far, far, near)
                patch = pltpu.roll(patch, -shift % 128, 1) if shift else patch
                wrong = (lane32 <= RIM - 1 - shift) | (lane32 >= 128 - RIM - shift)
                if shift == 0:
                    patch = jnp.where(wrong, patch, shifted[RIM, f, k])
                    shifted[RIM, f, k] = patch
                    out[f, k] = patch
                else:
                    pltpu.store(shifted.at[shift + RIM, f, k], patch, mask=wrong)


def render(away, place, shear, weight, bias, shifted, image):
    count = image.shape[0]
    depth_cells = shifted.shape[2]
    depth_at, depth_last = place[0], place[3]
    first = lax.rem(depth_at + away, depth_last + 1) * count
    middle = 0.5 * depth_cells * (depth_last + 1).astype(F32)

    @pl.loop(0, count)
    def _(j):
        v = first + j
        table = [
            tuple(
                (0.5 if c < 3 else 1.0) * value
                for value in (weight[c, 0, v], weight[c, 1, v], bias[c, v])
            )
            for c in range(4)
        ]
        slope = shear[v]

        for part in range(4):
            strip = slice(part * 8, (part + 1) * 8)

            def march(k, state):
                c0, c1, c2, total, through = state
                place_in_depth = (depth_at * depth_cells + k).astype(F32) + 0.5
                offset = slope * (place_in_depth - middle)
                whole = offset.astype(jnp.int32)
                whole = jnp.where(whole.astype(F32) > offset, whole - 1, whole)
                t = offset - whole.astype(F32)
                i = jnp.clip(whole + RIM, 0, SHIFTS - 2)
                s0 = (1.0 - t) * shifted[i, 0, k, strip] + t * shifted[i + 1, 0, k, strip]
                s1 = (1.0 - t) * shifted[i, 1, k, strip] + t * shifted[i + 1, 1, k, strip]
                logits = [table[c][0] * s0 + table[c][1] * s1 + table[c][2] for c in range(4)]
                dense = logits[3]
                total = total + (jnp.maximum(dense, 0.0) + jnp.log(1.0 + jnp.exp(-jnp.abs(dense))))
                after = jnp.exp2((-RAY_STEP * LOG2E) * total)
                part = through - after
                c0 = c0 + part * jnp.tanh(logits[0])
                c1 = c1 + part * jnp.tanh(logits[1])
                c2 = c2 + part * jnp.tanh(logits[2])
                return c0, c1, c2, total, after

            zero = jnp.zeros((8, 128), F32)
            c0, c1, c2, _, through = lax.fori_loop(
                0, depth_cells, march, (zero, zero, zero, zero, zero + 1.0), unroll=16
            )
            opacity = 1.0 - through
            image[j, 0, strip] = 0.5 * (c0 + opacity)
            image[j, 1, strip] = 0.5 * (c1 + opacity)
            image[j, 2, strip] = 0.5 * (c2 + opacity)
            image[j, 3, strip] = opacity


def deal(place, owners, lengths, warp, select, lengths_wide, warp_own, sem):
    views = warp_own.shape[0]
    copy = pltpu.make_async_copy(warp.at[pl.ds(place[0] * views, views)], warp_own, sem.at[0])
    copy.start()
    row = lax.broadcasted_iota(jnp.int32, (128, 128), 0)
    lane = lax.broadcasted_iota(jnp.int32, (128, 128), 1)
    name = jnp.concatenate([owners[v : v + 1, :] for v in range(views)], axis=1)
    length = jnp.concatenate([lengths[v : v + 1, :] for v in range(views)], axis=1)
    along = jnp.broadcast_to(name, (128, 128))
    across = along.T
    earlier = (along == across) & (row < lane) & (row // 32 == lane // 32)
    rank = jnp.sum(earlier.astype(F32), axis=0, keepdims=True).astype(jnp.int32)
    view = lane[0:1] // 32
    half = select.shape[0] // 2
    codes = name * (views * CAPACITY // 2) + view * (CAPACITY // 2) + rank // 2
    codes = codes + (rank % 2) * half
    slot = lax.broadcasted_iota(jnp.int32, select.shape, 0)
    select[...] = (slot == codes).astype(F32).astype(BF16)
    lengths_wide[...] = jnp.broadcast_to(length, (128, 128)).T
    copy.wait()


def composite(place, order, select, lengths, slab0, slab1, slab2, slab3, outgoing, pieces):
    lane = lax.broadcasted_iota(jnp.int32, (32, 128), 1)
    slabs = (slab0, slab1, slab2, slab3)
    depth_at, devices = place[0], place[3] + 1

    def fetch(which, v, c):
        value = slabs[3][v, c]
        for offset in (2, 1, 0):
            value = jnp.where(which == offset, slabs[offset][v, c], value)
        return value

    for v in range(4):
        keep = lane < lengths[32 * v : 32 * (v + 1), :]
        turn = [
            lax.rem(depth_at - order[position, depth_at * 4 + v] + devices, devices)
            for position in range(4)
        ]
        channels = [fetch(turn[0], v, c) for c in range(4)]
        for position in range(1, 4):
            clear = 1.0 - channels[3]
            channels = [channels[c] + clear * fetch(turn[position], v, c) for c in range(4)]
        for c in range(4):
            pieces[32 * v : 32 * (v + 1), 128 * c : 128 * (c + 1)] = jnp.where(
                keep, channels[c], 0.0
            ).astype(BF16)
    row_id = lax.broadcasted_iota(jnp.int32, (128, 128), 0) + 1
    pieces[:, 512:640] = row_id.astype(F32).astype(BF16)
    dealt = jnp.dot(select[...], pieces[...], preferred_element_type=F32).astype(BF16)
    half = outgoing.shape[0]
    outgoing[:, 0:512] = dealt[:half, 0:512]
    outgoing[:, 512:1024] = dealt[half:, 0:512]
    outgoing[:, 1024:1088] = dealt[:half, 512:576]
    outgoing[:, 1088:1152] = dealt[half:, 576:640]


def resample(incoming, warp, frame):
    rows = incoming.shape[0]
    ids = incoming[:, 1024:1152].astype(F32)
    lane = lax.broadcasted_iota(jnp.int32, (rows, 128), 1)
    swapped = pltpu.roll(ids, 64, 1)
    line = (lane + 1).astype(F32)
    total = jnp.zeros((128, 512), F32)
    for odd in range(2):
        names = jnp.where((lane < 64) == (odd == 0), ids, swapped)
        place = (names == line).astype(F32).astype(BF16)
        part = incoming[:, 512 * odd : 512 * (odd + 1)]
        total = total + lax.dot_general(place, part, TN, preferred_element_type=F32)
    for v in range(4):
        matrix = warp[v].astype(F32)
        for c in range(4):
            rows = total[32 * v : 32 * (v + 1), 128 * c : 128 * (c + 1)]
            frame[pl.ds(128 * v + c, 32, stride=4), :] = jnp.dot(
                rows, matrix, preferred_element_type=F32, precision=lax.Precision.HIGHEST
            )


def body(
    species,
    diffusivity,
    reaction_rate,
    shear_rate,
    colour_weight,
    colour_bias,
    slab_order,
    lengths,
    owners,
    warp_matrix,
):
    depth_at, row_at, col_at = (lax.axis_index(a) for a in ("depth", "row", "col"))
    depth_devices, row_devices, col_devices = (lax.axis_size(a) for a in ("depth", "row", "col"))
    view_count = shear_rate.shape[0] // depth_devices

    place = jnp.stack(
        [
            depth_at,
            row_at,
            col_at,
            jnp.int32(depth_devices - 1),
            jnp.int32(row_devices - 1),
            jnp.int32(col_devices - 1),
        ]
    ).astype(jnp.int32)
    fields = tuple(in_hbm(x) for x in (species, diffusivity, reaction_rate))

    face = jax.ShapeDtypeStruct((4, HALO, 32, 128), BF16)
    low, high = call(
        pack_depth,
        (face, face),
        [HBM_SPEC] * 3,
        [pltpu.VMEM((2, 4, HALO, 32, 128), F32), pltpu.SemaphoreType.DMA((8,))],
    )(*fields)
    before, after = shift_up(high, "depth"), shift_down(low, "depth")
    brick_type = jax.ShapeDtypeStruct((4, PLANES, ROWS, 128), F32)
    brick = call(load_brick, brick_type, [HBM_SPEC] * 3, [pltpu.SemaphoreType.DMA((4,))])(*fields)
    face = jax.ShapeDtypeStruct((HALO, 4 * PLANES, 128), BF16)
    brick, low, high = call(
        pack_rows, (brick_type, face, face), [VMEM_SPEC] * 3, aliases={0: 0}
    )(brick, before, after)
    above, below = turn_by(high, "row", 1), turn_by(low, "row", -1)
    slots = col_devices * view_count * CAPACITY
    lines = view_count * 32
    select, lengths_wide, warp_own = call(
        deal,
        (
            jax.ShapeDtypeStruct((slots, lines), BF16),
            jax.ShapeDtypeStruct((lines, 128), jnp.int32),
            jax.ShapeDtypeStruct((view_count, 128, 128), BF16),
        ),
        [SMEM_SPEC, VMEM_SPEC, VMEM_SPEC, HBM_SPEC],
        [pltpu.SemaphoreType.DMA((1,))],
    )(place, owners.reshape(view_count, 32), lengths.reshape(view_count, 32), in_hbm(warp_matrix))

    brick, select, lengths_wide, warp_own = lax.optimization_barrier(
        (brick, select, lengths_wide, warp_own)
    )
    face = jax.ShapeDtypeStruct((8, 4 * LINES), BF16)
    brick, low, high = call(
        pack_columns, (brick_type, face, face), [SMEM_SPEC] + [VMEM_SPEC] * 3, aliases={1: 0}
    )(place, brick, above, below)
    left = shift_up(high, "col")
    right = shift_down(low, "col")
    wide = pltpu.VMEM((2, PLANES, ROWS, 128), F32)
    shifted_type = jax.ShapeDtypeStruct((SHIFTS,) + species.shape, F32)
    shifted, edges = call(
        advance_own,
        (shifted_type, jax.ShapeDtypeStruct((16, 2 * LINES), F32)),
        [SMEM_SPEC, VMEM_SPEC],
        [wide, wide],
    )(place, brick)
    shifted, species_out = call(
        advance_edges,
        (shifted_type, jax.ShapeDtypeStruct(species.shape, F32)),
        [SMEM_SPEC] + [VMEM_SPEC] * 6,
        [pltpu.VMEM((2, BLOCKS, 4 * EDGE, 128), F32)] * 4 + [pltpu.VMEM((2, LINES, 128), F32)],
        aliases={1: 0},
    )(place, shifted, edges, low, high, left, right)

    image = jax.ShapeDtypeStruct((view_count, 4, 32, 128), F32)
    weight, bias = jnp.transpose(colour_weight, (1, 2, 0)), colour_bias.T
    slabs = [None] * 4
    for away in (2, 1, 3, 0):
        drawn = call(
            functools.partial(render, away), image, [SMEM_SPEC] * 4 + [VMEM_SPEC]
        )(place, shear_rate, weight, bias, shifted)
        if away:
            drawn = turn_by(drawn, "depth", away)
        slabs[away] = drawn
    outgoing = call(
        composite,
        jax.ShapeDtypeStruct((slots // 2, 1152), BF16),
        [SMEM_SPEC] * 2 + [VMEM_SPEC] * 6,
        [pltpu.VMEM((lines, 640), BF16)],
    )(place, slab_order.T, select, lengths_wide, *slabs)
    incoming = lax.all_to_all(
        outgoing.reshape(col_devices, -1, 1152),
        "col",
        split_axis=0,
        concat_axis=0,
        tiled=True,
    ).reshape(slots // 2, 1152)
    frame = call(resample, jax.ShapeDtypeStruct((4 * lines, 128), F32), [VMEM_SPEC] * 2)(
        incoming, warp_own
    )
    return species_out, frame.reshape(view_count, 32, 4, 128)


def solution(mesh):
    in_specs = (
        P(None, "depth", "row", "col"),
        P("depth", "row", "col"),
        P("depth", "row", "col"),
        P(),
        P(),
        P(),
        P(),
        P("depth", "col", "row"),
        P("depth", "col", "row", None),
        P(),
    )
    out_specs = (P(None, "depth", "row", "col"), P("depth", "row", None, "col"))
    return jax.shard_map(body, mesh=mesh, in_specs=in_specs, out_specs=out_specs, check_vma=False)
```

```python
import functools

import jax
import jax.numpy as jnp
from jax import lax
from jax.experimental import pallas as pl
from jax.experimental.pallas import tpu as pltpu
from jax.sharding import PartitionSpec as P

TIME_STEP = 0.1
RAY_STEP = 0.02
LOG2E = 1.4426950408889634
VEL_DEPTH = 0.3
VEL_ROW = 0.2
VEL_COL = 0.4

HALO = 3
RIM = 3
EDGE = 6
PLANES = 22
ROWS = 40
LINES = 896
BLOCKS = LINES // 128
SHIFTS = 2 * RIM + 1
CAPACITY = 4
SAVER = 1

F32 = jnp.float32
BF16 = jnp.bfloat16
VMEM_SPEC = pl.BlockSpec(memory_space=pltpu.VMEM)
SMEM_SPEC = pl.BlockSpec(memory_space=pltpu.SMEM)
HBM_SPEC = pl.BlockSpec(memory_space=pltpu.HBM)
NT = (((1,), (1,)), ((), ()))
TN = (((0,), (0,)), ((), ()))


def call(kernel, out_shape, in_specs, scratch=(), limit=8, aliases=None, out_specs=None):
    return pl.pallas_call(
        kernel,
        out_shape=out_shape,
        in_specs=in_specs,
        out_specs=out_specs or jax.tree.map(lambda unused: VMEM_SPEC, out_shape),
        scratch_shapes=list(scratch),
        input_output_aliases=aliases or {},
        compiler_params=pltpu.CompilerParams(vmem_limit_bytes=limit << 20),
    )


def in_hbm(x):
    return pltpu.with_memory_space_constraint(x, pltpu.HBM)


def turn_by(x, axis, steps):
    n = lax.axis_size(axis)
    return lax.ppermute(x, axis, [(i, (i + steps) % n) for i in range(n)])


def shift_up(x, axis):
    n = lax.axis_size(axis)
    return lax.ppermute(x, axis, [(i, i + 1) for i in range(n - 1)])


def shift_down(x, axis):
    n = lax.axis_size(axis)
    return lax.ppermute(x, axis, [(i + 1, i) for i in range(n - 1)])


def pack_depth(species, diff, rate, low, high, held, sems):
    copies = []
    for side, first in ((0, 0), (1, 16 - HALO)):
        cut = pl.ds(first, HALO)
        for source, at in (
            (species.at[0, cut], 0),
            (species.at[1, cut], 1),
            (diff.at[cut], 2),
            (rate.at[cut], 3),
        ):
            copies.append(
                pltpu.make_async_copy(source, held.at[side, at], sems.at[4 * side + at])
            )
    for copy in copies:
        copy.start()
    for copy in copies:
        copy.wait()
    low[...] = held[0].astype(BF16)
    high[...] = held[1].astype(BF16)


def load_brick(species, diff, rate, brick, sems):
    copies = [
        pltpu.make_async_copy(
            source, brick.at[f, pl.ds(HALO, 16), pl.ds(0, 32), :], sems.at[f]
        )
        for f, source in enumerate((species.at[0], species.at[1], diff, rate))
    ]
    for copy in copies:
        copy.start()
    for f in range(4):
        brick[f, :, 32:ROWS, :] = jnp.zeros((PLANES, ROWS - 32, 128), F32)
    for copy in copies:
        copy.wait()


def pack_rows(unused, before, after, brick, low, high):
    for f in range(4):
        brick[f, 0:HALO, 0:32, :] = before[f].astype(F32)
        brick[f, HALO + 16 : 22, 0:32, :] = after[f].astype(F32)
    lines = brick.reshape(4 * PLANES * ROWS, 128)
    for r in range(HALO):
        low[r] = lines[pl.ds(r, 4 * PLANES, stride=ROWS), :].astype(BF16)
        high[r] = lines[pl.ds(32 - HALO + r, 4 * PLANES, stride=ROWS), :].astype(BF16)


def column_picker(first_low, first_high):
    j = lax.broadcasted_iota(jnp.int32, (16, 128), 0)
    lane = lax.broadcasted_iota(jnp.int32, (16, 128), 1)
    at = jnp.where(j < 8, first_low + j, first_high + j - 8)
    return ((lane == at) & (j % 8 < EDGE)).astype(F32).astype(BF16)


def pack_columns(place, unused, above, below, brick, low, high):
    has_above = jnp.where(place[1] > 0, 1.0, 0.0).astype(F32)
    has_below = jnp.where(place[1] < place[4], 1.0, 0.0).astype(F32)
    lines = brick.reshape(4 * PLANES * ROWS, 128)
    for r in range(HALO):
        lines[pl.ds(ROWS - HALO + r, 4 * PLANES, stride=ROWS), :] = has_above * above[r].astype(F32)
        lines[pl.ds(32 + r, 4 * PLANES, stride=ROWS), :] = has_below * below[r].astype(F32)
    pick = column_picker(0, 128 - EDGE)
    count = PLANES * ROWS
    blank = jnp.zeros((8, LINES - count), BF16)
    for f in range(4):
        rows = brick[f].reshape(count, 128).astype(BF16)
        edge = lax.dot_general(pick, rows, NT, preferred_element_type=F32).astype(BF16)
        at = f * LINES
        for side, part in ((low, edge[:8]), (high, edge[8:])):
            side[:, at : at + count] = part
            side[:, at + count : at + LINES] = blank


def slope_of(fields, diffusivity, reaction, neighbours):
    fuel, heat = fields
    square = heat * heat
    burned = reaction * fuel * square / (1.0 + square)
    slopes = []
    for f in range(2):
        centre = fields[f]
        below_depth, above_depth, below_row, above_row, below_col, above_col = neighbours(f)
        laplace = (
            below_depth + above_depth + below_row + above_row + below_col + above_col - 6.0 * centre
        )
        advect = (
            VEL_DEPTH * (centre - below_depth)
            + VEL_ROW * (centre - below_row)
            + VEL_COL * (centre - below_col)
        )
        gain = -burned if f == 0 else burned
        slopes.append(diffusivity * laplace - advect + gain)
    return slopes


def advance_own(place, brick, shifted, edges, first, second):
    n = ROWS
    depth_at, row_at = place[0], place[1]
    depth_last, row_last = place[3], place[4]
    row = lax.broadcasted_iota(jnp.int32, (n, 128), 0)
    rows_in = (
        (row < 32)
        | ((row < 32 + HALO) & (row_at < row_last))
        | ((row >= n - HALO) & (row_at > 0))
    )
    step = jnp.where(rows_in, TIME_STEP, 0.0).astype(F32)

    def tendency(source, p):
        def neighbours(f):
            centre = source[f, p]
            return (
                source[f, p - 1],
                source[f, p + 1],
                pltpu.roll(centre, 1, 0),
                pltpu.roll(centre, n - 1, 0),
                pltpu.roll(centre, 1, 1),
                pltpu.roll(centre, 127, 1),
            )

        return slope_of((source[0, p], source[1, p]), brick[2, p], brick[3, p], neighbours)

    def inside(p):
        ok = ((p >= HALO) | (depth_at > 0)) & ((p < HALO + 16) | (depth_at < depth_last))
        return jnp.where(ok, 1.0, 0.0).astype(F32)

    @pl.loop(1, 21, unroll=2)
    def _(p):
        slope = tendency(brick, p)
        scale = inside(p)
        for f in range(2):
            first[f, p] = brick[f, p] + (step * scale) * slope[f]

    @pl.loop(2, 20, unroll=2)
    def _(p):
        slope = tendency(first, p)
        scale = inside(p)
        for f in range(2):
            second[f, p] = 0.75 * brick[f, p] + 0.25 * (first[f, p] + (step * scale) * slope[f])

    @pl.loop(3, 19, unroll=2)
    def _(p):
        slope = tendency(second, p)
        k = p - HALO
        for f in range(2):
            new = (brick[f, p] / 3.0 + (2.0 / 3.0) * (second[f, p] + step * slope[f]))[:32]
            for shift in range(-RIM, RIM + 1):
                shifted[shift + RIM, f, k] = pltpu.roll(new, -shift % 128, 1) if shift else new

    pick = column_picker(0, 128 - EDGE)
    count = PLANES * ROWS
    for f in range(2):
        rows = brick[f].reshape(count, 128)
        rest = (rows - rows.astype(BF16).astype(F32)).astype(BF16)
        edges[:, f * LINES : f * LINES + count] = lax.dot_general(
            pick, rest, NT, preferred_element_type=F32
        )
        edges[:, f * LINES + count : (f + 1) * LINES] = jnp.zeros((16, LINES - count), F32)


def advance_edges(
    place, unused, edges, low, high, left, right, shifted, start, coefs, first, second, turned
):
    row_at, col_at, depth_at = place[1], place[2], place[0]
    depth_last, row_last, col_last = place[3], place[4], place[5]
    shape = (4 * EDGE, 128)
    col = lax.broadcasted_iota(jnp.int32, shape, 0)
    lane = lax.broadcasted_iota(jnp.int32, shape, 1)
    cols_in = ((col >= EDGE) | (col_at > 0)) & ((col < 3 * EDGE) | (col_at < col_last))

    def table(b):
        line = lane + 128 * b
        plane = jnp.floor((line.astype(F32) + 0.5) * (1.0 / ROWS)).astype(jnp.int32)
        row = line - plane * ROWS
        rows_in = (
            (row < 32)
            | ((row < 32 + HALO) & (row_at < row_last))
            | ((row >= ROWS - HALO) & (row_at > 0))
        )
        planes_in = ((plane >= HALO) | (depth_at > 0)) & (
            (plane < HALO + 16) | ((plane < PLANES) & (depth_at < depth_last))
        )
        step = jnp.where(rows_in & cols_in & planes_in, TIME_STEP, 0.0).astype(F32)
        return step, row == 0, row == ROWS - 1

    for f in range(4):
        for b in range(BLOCKS):
            cut = slice(f * LINES + 128 * b, f * LINES + 128 * (b + 1))
            own_low, own_high = low[:, cut].astype(F32), high[:, cut].astype(F32)
            if f < 2:
                own_low = own_low + edges[0:8, cut]
                own_high = own_high + edges[8:16, cut]
            gathered = jnp.concatenate(
                [
                    left[:, cut].astype(F32)[:EDGE],
                    own_low[:EDGE],
                    own_high[:EDGE],
                    right[:, cut].astype(F32)[:EDGE],
                ],
                axis=0,
            )
            if f < 2:
                start[f, b] = gathered
            else:
                coefs[f - 2, b] = gathered

    def stage(source, finish):
        held = {}

        def turn(f, b, by):
            b = b % BLOCKS
            if (f, b, by) not in held:
                held[f, b, by] = pltpu.roll(source[f, b], by, 1)
            return held[f, b, by]

        def from_before(f, b, by):
            return jnp.where(lane < by, turn(f, b - 1, by), turn(f, b, by))

        def from_after(f, b, by):
            return jnp.where(lane >= 128 - by, turn(f, b + 1, 128 - by), turn(f, b, 128 - by))

        for b in range(BLOCKS):
            step, first_row, last_row = table(b)

            def neighbours(f):
                x = source[f, b]
                return (
                    from_before(f, b, ROWS),
                    from_after(f, b, ROWS),
                    jnp.where(first_row, from_after(f, b, ROWS - 1), from_before(f, b, 1)),
                    jnp.where(last_row, from_before(f, b, ROWS - 1), from_after(f, b, 1)),
                    pltpu.roll(x, 1, 0),
                    pltpu.roll(x, 4 * EDGE - 1, 0),
                )

            slope = slope_of((source[0, b], source[1, b]), coefs[0, b], coefs[1, b], neighbours)
            for f in range(2):
                finish(f, b, step * slope[f])

    def finish_first(f, b, change):
        first[f, b] = start[f, b] + change

    def finish_second(f, b, change):
        second[f, b] = 0.75 * start[f, b] + 0.25 * (first[f, b] + change)

    blank = jnp.zeros((128 - 4 * EDGE, 128), F32)

    def finish_third(f, b, change):
        new = start[f, b] / 3.0 + (2.0 / 3.0) * (second[f, b] + change)
        turned[f, 128 * b : 128 * (b + 1), :] = jnp.concatenate([new, blank], axis=0).T

    stage(start, finish_first)
    stage(first, finish_second)
    stage(second, finish_third)
    lane32 = lax.broadcasted_iota(jnp.int32, (32, 128), 1)

    @pl.loop(0, 16, unroll=2)
    def _(k):
        for f in range(2):
            lines = turned[f, pl.ds(pl.multiple_of((k + HALO) * ROWS, 8), 32), :]
            near = pltpu.roll(lines, 128 - EDGE, 1)
            far = pltpu.roll(lines, 128 - 3 * EDGE, 1)
            for shift in range(-RIM, RIM + 1):
                from_far = (lane32 >= 64) & (lane32 < 128 + min(shift, 0)) | (lane32 < shift)
                patch = jnp.where(from_far, far, near)
                patch = pltpu.roll(patch, -shift % 128, 1) if shift else patch
                wrong = (lane32 <= RIM - 1 - shift) | (lane32 >= 128 - RIM - shift)
                pltpu.store(shifted.at[shift + RIM, f, k], patch, mask=wrong)


def render_and_save(away, place, shear, weight, bias, shifted, image, out, sem):
    copy = pltpu.make_async_copy(shifted.at[RIM], out, sem.at[0])
    copy.start()
    render(away, place, shear, weight, bias, shifted, image)
    copy.wait()


def render(away, place, shear, weight, bias, shifted, image):
    count = image.shape[0]
    depth_cells = shifted.shape[2]
    depth_at, depth_last = place[0], place[3]
    first = lax.rem(depth_at + away, depth_last + 1) * count
    middle = 0.5 * depth_cells * (depth_last + 1).astype(F32)

    @pl.loop(0, count)
    def _(j):
        v = first + j
        table = [
            tuple(
                (0.5 if c < 3 else 1.0) * value
                for value in (weight[c, 0, v], weight[c, 1, v], bias[c, v])
            )
            for c in range(4)
        ]
        slope = shear[v]

        for part in range(4):
            strip = slice(part * 8, (part + 1) * 8)

            def march(k, state):
                c0, c1, c2, total, through = state
                place_in_depth = (depth_at * depth_cells + k).astype(F32) + 0.5
                offset = slope * (place_in_depth - middle)
                whole = offset.astype(jnp.int32)
                whole = jnp.where(whole.astype(F32) > offset, whole - 1, whole)
                t = offset - whole.astype(F32)
                i = jnp.clip(whole + RIM, 0, SHIFTS - 2)
                s0 = (1.0 - t) * shifted[i, 0, k, strip] + t * shifted[i + 1, 0, k, strip]
                s1 = (1.0 - t) * shifted[i, 1, k, strip] + t * shifted[i + 1, 1, k, strip]
                logits = [table[c][0] * s0 + table[c][1] * s1 + table[c][2] for c in range(4)]
                dense = logits[3]
                total = total + (jnp.maximum(dense, 0.0) + jnp.log(1.0 + jnp.exp(-jnp.abs(dense))))
                after = jnp.exp2((-RAY_STEP * LOG2E) * total)
                part = through - after
                c0 = c0 + part * jnp.tanh(logits[0])
                c1 = c1 + part * jnp.tanh(logits[1])
                c2 = c2 + part * jnp.tanh(logits[2])
                return c0, c1, c2, total, after

            zero = jnp.zeros((8, 128), F32)
            c0, c1, c2, _, through = lax.fori_loop(
                0, depth_cells, march, (zero, zero, zero, zero, zero + 1.0), unroll=16
            )
            opacity = 1.0 - through
            image[j, 0, strip] = 0.5 * (c0 + opacity)
            image[j, 1, strip] = 0.5 * (c1 + opacity)
            image[j, 2, strip] = 0.5 * (c2 + opacity)
            image[j, 3, strip] = opacity


def deal(place, owners, lengths, warp, select, lengths_wide, warp_own, sem):
    views = warp_own.shape[0]
    copy = pltpu.make_async_copy(warp.at[pl.ds(place[0] * views, views)], warp_own, sem.at[0])
    copy.start()
    row = lax.broadcasted_iota(jnp.int32, (128, 128), 0)
    lane = lax.broadcasted_iota(jnp.int32, (128, 128), 1)
    name = jnp.concatenate([owners[v : v + 1, :] for v in range(views)], axis=1)
    length = jnp.concatenate([lengths[v : v + 1, :] for v in range(views)], axis=1)
    along = jnp.broadcast_to(name, (128, 128))
    across = along.T
    earlier = (along == across) & (row < lane) & (row // 32 == lane // 32)
    rank = jnp.sum(earlier.astype(F32), axis=0, keepdims=True).astype(jnp.int32)
    view = lane[0:1] // 32
    half = select.shape[0] // 2
    codes = name * (views * CAPACITY // 2) + view * (CAPACITY // 2) + rank // 2
    codes = codes + (rank % 2) * half
    slot = lax.broadcasted_iota(jnp.int32, select.shape, 0)
    select[...] = (slot == codes).astype(F32).astype(BF16)
    lengths_wide[...] = jnp.broadcast_to(length, (128, 128)).T
    copy.wait()


def composite(place, order, select, lengths, slab0, slab1, slab2, slab3, outgoing, pieces):
    lane = lax.broadcasted_iota(jnp.int32, (32, 128), 1)
    slabs = (slab0, slab1, slab2, slab3)
    depth_at, devices = place[0], place[3] + 1

    def fetch(which, v, c):
        value = slabs[3][v, c]
        for offset in (2, 1, 0):
            value = jnp.where(which == offset, slabs[offset][v, c], value)
        return value

    for v in range(4):
        keep = lane < lengths[32 * v : 32 * (v + 1), :]
        turn = [
            lax.rem(depth_at - order[position, depth_at * 4 + v] + devices, devices)
            for position in range(4)
        ]
        channels = [fetch(turn[0], v, c) for c in range(4)]
        for position in range(1, 4):
            clear = 1.0 - channels[3]
            channels = [channels[c] + clear * fetch(turn[position], v, c) for c in range(4)]
        for c in range(4):
            pieces[32 * v : 32 * (v + 1), 128 * c : 128 * (c + 1)] = jnp.where(
                keep, channels[c], 0.0
            ).astype(BF16)
    row_id = lax.broadcasted_iota(jnp.int32, (128, 128), 0) + 1
    pieces[:, 512:640] = row_id.astype(F32).astype(BF16)
    dealt = jnp.dot(select[...], pieces[...], preferred_element_type=F32).astype(BF16)
    half = outgoing.shape[0]
    outgoing[:, 0:512] = dealt[:half, 0:512]
    outgoing[:, 512:1024] = dealt[half:, 0:512]
    outgoing[:, 1024:1088] = dealt[:half, 512:576]
    outgoing[:, 1088:1152] = dealt[half:, 576:640]


def resample(incoming, warp, frame):
    rows = incoming.shape[0]
    ids = incoming[:, 1024:1152].astype(F32)
    lane = lax.broadcasted_iota(jnp.int32, (rows, 128), 1)
    swapped = pltpu.roll(ids, 64, 1)
    line = (lane + 1).astype(F32)
    total = jnp.zeros((128, 512), F32)
    for odd in range(2):
        names = jnp.where((lane < 64) == (odd == 0), ids, swapped)
        place = (names == line).astype(F32).astype(BF16)
        part = incoming[:, 512 * odd : 512 * (odd + 1)]
        total = total + lax.dot_general(place, part, TN, preferred_element_type=F32)
    for v in range(4):
        rows = jnp.concatenate(
            [total[32 * v : 32 * (v + 1), 128 * c : 128 * (c + 1)] for c in range(4)], axis=0
        )
        warped = jnp.zeros((128, 128), F32)
        for _ in range(3):
            part = rows.astype(BF16)
            warped = warped + jnp.dot(part, warp[v], preferred_element_type=F32)
            rows = rows - part.astype(F32)
        for c in range(4):
            frame[pl.ds(128 * v + c, 32, stride=4), :] = warped[32 * c : 32 * (c + 1)]


def body(
    species,
    diffusivity,
    reaction_rate,
    shear_rate,
    colour_weight,
    colour_bias,
    slab_order,
    lengths,
    owners,
    warp_matrix,
):
    depth_at, row_at, col_at = (lax.axis_index(a) for a in ("depth", "row", "col"))
    depth_devices, row_devices, col_devices = (lax.axis_size(a) for a in ("depth", "row", "col"))
    view_count = shear_rate.shape[0] // depth_devices

    place = jnp.stack(
        [
            depth_at,
            row_at,
            col_at,
            jnp.int32(depth_devices - 1),
            jnp.int32(row_devices - 1),
            jnp.int32(col_devices - 1),
        ]
    ).astype(jnp.int32)
    fields = tuple(in_hbm(x) for x in (species, diffusivity, reaction_rate))

    face = jax.ShapeDtypeStruct((4, HALO, 32, 128), BF16)
    low, high = call(
        pack_depth,
        (face, face),
        [HBM_SPEC] * 3,
        [pltpu.VMEM((2, 4, HALO, 32, 128), F32), pltpu.SemaphoreType.DMA((8,))],
    )(*fields)
    before, after = shift_up(high, "depth"), shift_down(low, "depth")
    brick_type = jax.ShapeDtypeStruct((4, PLANES, ROWS, 128), F32)
    brick = call(load_brick, brick_type, [HBM_SPEC] * 3, [pltpu.SemaphoreType.DMA((4,))])(*fields)
    face = jax.ShapeDtypeStruct((HALO, 4 * PLANES, 128), BF16)
    brick, low, high = call(
        pack_rows, (brick_type, face, face), [VMEM_SPEC] * 3, aliases={0: 0}
    )(brick, before, after)
    above, below = turn_by(high, "row", 1), turn_by(low, "row", -1)
    slots = col_devices * view_count * CAPACITY
    lines = view_count * 32
    select, lengths_wide, warp_own = call(
        deal,
        (
            jax.ShapeDtypeStruct((slots, lines), BF16),
            jax.ShapeDtypeStruct((lines, 128), jnp.int32),
            jax.ShapeDtypeStruct((view_count, 128, 128), BF16),
        ),
        [SMEM_SPEC, VMEM_SPEC, VMEM_SPEC, HBM_SPEC],
        [pltpu.SemaphoreType.DMA((1,))],
    )(place, owners.reshape(view_count, 32), lengths.reshape(view_count, 32), in_hbm(warp_matrix))

    brick, select, lengths_wide, warp_own = lax.optimization_barrier(
        (brick, select, lengths_wide, warp_own)
    )
    face = jax.ShapeDtypeStruct((8, 4 * LINES), BF16)
    brick, low, high = call(
        pack_columns, (brick_type, face, face), [SMEM_SPEC] + [VMEM_SPEC] * 3, aliases={1: 0}
    )(place, brick, above, below)
    left = shift_up(high, "col")
    right = shift_down(low, "col")
    wide = pltpu.VMEM((2, PLANES, ROWS, 128), F32)
    shifted_type = jax.ShapeDtypeStruct((SHIFTS,) + species.shape, F32)
    shifted, edges = call(
        advance_own,
        (shifted_type, jax.ShapeDtypeStruct((16, 2 * LINES), F32)),
        [SMEM_SPEC, VMEM_SPEC],
        [wide, wide],
    )(place, brick)
    shifted = call(
        advance_edges,
        shifted_type,
        [SMEM_SPEC] + [VMEM_SPEC] * 6,
        [pltpu.VMEM((2, BLOCKS, 4 * EDGE, 128), F32)] * 4 + [pltpu.VMEM((2, LINES, 128), F32)],
        aliases={1: 0},
    )(place, shifted, edges, low, high, left, right)

    image = jax.ShapeDtypeStruct((view_count, 4, 32, 128), F32)
    weight, bias = jnp.transpose(colour_weight, (1, 2, 0)), colour_bias.T
    slabs = [None] * 4
    for away in (2, 1, 3, 0):
        if away == SAVER:
            drawn, species_out = call(
                functools.partial(render_and_save, away),
                (image, jax.ShapeDtypeStruct(species.shape, F32)),
                [SMEM_SPEC] * 4 + [VMEM_SPEC],
                [pltpu.SemaphoreType.DMA((1,))],
                out_specs=(VMEM_SPEC, HBM_SPEC),
            )(place, shear_rate, weight, bias, shifted)
        else:
            drawn = call(
                functools.partial(render, away), image, [SMEM_SPEC] * 4 + [VMEM_SPEC]
            )(place, shear_rate, weight, bias, shifted)
        if away:
            drawn = turn_by(drawn, "depth", away)
        slabs[away] = drawn
    outgoing = call(
        composite,
        jax.ShapeDtypeStruct((slots // 2, 1152), BF16),
        [SMEM_SPEC] * 2 + [VMEM_SPEC] * 6,
        [pltpu.VMEM((lines, 640), BF16)],
    )(place, slab_order.T, select, lengths_wide, *slabs)
    incoming = lax.all_to_all(
        outgoing.reshape(col_devices, -1, 1152),
        "col",
        split_axis=0,
        concat_axis=0,
        tiled=True,
    ).reshape(slots // 2, 1152)
    frame = call(resample, jax.ShapeDtypeStruct((4 * lines, 128), F32), [VMEM_SPEC] * 2)(
        incoming, warp_own
    )
    return species_out, frame.reshape(view_count, 32, 4, 128)


def solution(mesh):
    in_specs = (
        P(None, "depth", "row", "col"),
        P("depth", "row", "col"),
        P("depth", "row", "col"),
        P(),
        P(),
        P(),
        P(),
        P("depth", "col", "row"),
        P("depth", "col", "row", None),
        P(),
    )
    out_specs = (P(None, "depth", "row", "col"), P("depth", "row", None, "col"))
    return jax.shard_map(body, mesh=mesh, in_specs=in_specs, out_specs=out_specs, check_vma=False)
```

```python
import functools

import jax
import jax.numpy as jnp
from jax import lax
from jax.experimental import pallas as pl
from jax.experimental.pallas import tpu as pltpu
from jax.sharding import PartitionSpec as P

TIME_STEP = 0.1
RAY_STEP = 0.02
LOG2E = 1.4426950408889634
VEL_DEPTH = 0.3
VEL_ROW = 0.2
VEL_COL = 0.4

HALO = 3
RIM = 3
EDGE = 6
PLANES = 22
ROWS = 40
LINES = 896
BLOCKS = LINES // 128
SHIFTS = 2 * RIM + 1
CAPACITY = 4
SAVER = 1

F32 = jnp.float32
BF16 = jnp.bfloat16
VMEM_SPEC = pl.BlockSpec(memory_space=pltpu.VMEM)
SMEM_SPEC = pl.BlockSpec(memory_space=pltpu.SMEM)
HBM_SPEC = pl.BlockSpec(memory_space=pltpu.HBM)
NT = (((1,), (1,)), ((), ()))
TN = (((0,), (0,)), ((), ()))


def call(kernel, out_shape, in_specs, scratch=(), limit=8, aliases=None, out_specs=None):
    return pl.pallas_call(
        kernel,
        out_shape=out_shape,
        in_specs=in_specs,
        out_specs=out_specs or jax.tree.map(lambda unused: VMEM_SPEC, out_shape),
        scratch_shapes=list(scratch),
        input_output_aliases=aliases or {},
        compiler_params=pltpu.CompilerParams(vmem_limit_bytes=limit << 20),
    )


def in_hbm(x):
    return pltpu.with_memory_space_constraint(x, pltpu.HBM)


def turn_by(x, axis, steps):
    n = lax.axis_size(axis)
    return lax.ppermute(x, axis, [(i, (i + steps) % n) for i in range(n)])


def shift_up(x, axis):
    n = lax.axis_size(axis)
    return lax.ppermute(x, axis, [(i, i + 1) for i in range(n - 1)])


def shift_down(x, axis):
    n = lax.axis_size(axis)
    return lax.ppermute(x, axis, [(i + 1, i) for i in range(n - 1)])


def pack_depth(species, diff, rate, low, high, held, sems):
    copies = []
    for side, first in ((0, 0), (1, 16 - HALO)):
        cut = pl.ds(first, HALO)
        for source, at in (
            (species.at[0, cut], 0),
            (species.at[1, cut], 1),
            (diff.at[cut], 2),
            (rate.at[cut], 3),
        ):
            copies.append(
                pltpu.make_async_copy(source, held.at[side, at], sems.at[4 * side + at])
            )
    for copy in copies:
        copy.start()
    for copy in copies:
        copy.wait()
    low[...] = held[0].astype(BF16)
    high[...] = held[1].astype(BF16)


def load_brick(species, diff, rate, brick, sems):
    copies = [
        pltpu.make_async_copy(
            source, brick.at[f, pl.ds(HALO, 16), pl.ds(0, 32), :], sems.at[f]
        )
        for f, source in enumerate((species.at[0], species.at[1], diff, rate))
    ]
    for copy in copies:
        copy.start()
    for f in range(4):
        brick[f, :, 32:ROWS, :] = jnp.zeros((PLANES, ROWS - 32, 128), F32)
    for copy in copies:
        copy.wait()


def pack_rows(unused, before, after, brick, low, high):
    for f in range(4):
        brick[f, 0:HALO, 0:32, :] = before[f].astype(F32)
        brick[f, HALO + 16 : 22, 0:32, :] = after[f].astype(F32)
    lines = brick.reshape(4 * PLANES * ROWS, 128)
    for r in range(HALO):
        low[r] = lines[pl.ds(r, 4 * PLANES, stride=ROWS), :].astype(BF16)
        high[r] = lines[pl.ds(32 - HALO + r, 4 * PLANES, stride=ROWS), :].astype(BF16)


def column_picker(first_low, first_high):
    j = lax.broadcasted_iota(jnp.int32, (16, 128), 0)
    lane = lax.broadcasted_iota(jnp.int32, (16, 128), 1)
    at = jnp.where(j < 8, first_low + j, first_high + j - 8)
    return ((lane == at) & (j % 8 < EDGE)).astype(F32).astype(BF16)


def pack_columns(place, unused, above, below, brick, low, high):
    has_above = jnp.where(place[1] > 0, 1.0, 0.0).astype(F32)
    has_below = jnp.where(place[1] < place[4], 1.0, 0.0).astype(F32)
    lines = brick.reshape(4 * PLANES * ROWS, 128)
    for r in range(HALO):
        lines[pl.ds(ROWS - HALO + r, 4 * PLANES, stride=ROWS), :] = has_above * above[r].astype(F32)
        lines[pl.ds(32 + r, 4 * PLANES, stride=ROWS), :] = has_below * below[r].astype(F32)
    pick = column_picker(0, 128 - EDGE)
    count = PLANES * ROWS
    blank = jnp.zeros((8, LINES - count), BF16)
    for f in range(4):
        rows = brick[f].reshape(count, 128).astype(BF16)
        edge = lax.dot_general(pick, rows, NT, preferred_element_type=F32).astype(BF16)
        at = f * LINES
        for side, part in ((low, edge[:8]), (high, edge[8:])):
            side[:, at : at + count] = part
            side[:, at + count : at + LINES] = blank


def coefficients(step, diffusivity, reaction):
    spread = step * diffusivity
    return (
        1.0 - (6.0 * spread + (VEL_DEPTH + VEL_ROW + VEL_COL) * step),
        spread + VEL_DEPTH * step,
        spread + VEL_ROW * step,
        spread + VEL_COL * step,
        spread,
        step * reaction,
    )


def stepped(fields, coefs, neighbours):
    fuel, heat = fields
    cell, from_depth, from_row, from_col, from_above, reaction = coefs
    square = heat * heat
    burned = reaction * (fuel * (square / (1.0 + square)))
    results = []
    for f in range(2):
        below_depth, above_depth, below_row, above_row, below_col, above_col = neighbours(f)
        total = (
            (cell * fields[f] + from_depth * below_depth)
            + (from_row * below_row + from_col * below_col)
            + from_above * (above_depth + above_row + above_col)
        )
        results.append(total - burned if f == 0 else total + burned)
    return results


def advance_own(place, brick, shifted, edges, first, second, coefs):
    n = ROWS
    depth_at, row_at = place[0], place[1]
    depth_last, row_last = place[3], place[4]
    row = lax.broadcasted_iota(jnp.int32, (n, 128), 0)
    rows_in = (
        (row < 32)
        | ((row < 32 + HALO) & (row_at < row_last))
        | ((row >= n - HALO) & (row_at > 0))
    )
    step = jnp.where(rows_in, TIME_STEP, 0.0).astype(F32)

    def advanced(source, table, p):
        def neighbours(f):
            centre = source[f, p]
            return (
                source[f, p - 1],
                source[f, p + 1],
                pltpu.roll(centre, 1, 0),
                pltpu.roll(centre, n - 1, 0),
                pltpu.roll(centre, 1, 1),
                pltpu.roll(centre, 127, 1),
            )

        return stepped((source[0, p], source[1, p]), table, neighbours)

    def table_at(p):
        return tuple(coefs[i, p] for i in range(6))

    @pl.loop(1, 21, unroll=4)
    def _(p):
        ok = ((p >= HALO) | (depth_at > 0)) & ((p < HALO + 16) | (depth_at < depth_last))
        scale = jnp.where(ok, 1.0, 0.0).astype(F32)
        table = coefficients(step * scale, brick[2, p], brick[3, p])
        for i in range(6):
            coefs[i, p] = table[i]
        moved = advanced(brick, table, p)
        for f in range(2):
            first[f, p] = moved[f]

    @pl.loop(2, 20, unroll=3)
    def _(p):
        moved = advanced(first, table_at(p), p)
        for f in range(2):
            second[f, p] = 0.75 * brick[f, p] + 0.25 * moved[f]

    def shift_plane(k):
        for f in range(2):
            new = shifted[RIM, f, k]
            for shift in range(-RIM, RIM + 1):
                if shift:
                    shifted[shift + RIM, f, k] = pltpu.roll(new, -shift % 128, 1)

    @pl.loop(0, 16, unroll=2)
    def _(k):
        p = k + HALO
        shift_plane(jnp.maximum(k - 1, 0))
        moved = advanced(second, table_at(p), p)
        for f in range(2):
            shifted[RIM, f, k] = (brick[f, p] * (1.0 / 3.0) + (2.0 / 3.0) * moved[f])[:32]

    shift_plane(15)

    pick = column_picker(0, 128 - EDGE)
    count = PLANES * ROWS
    for f in range(2):
        rows = brick[f].reshape(count, 128)
        rest = (rows - rows.astype(BF16).astype(F32)).astype(BF16)
        edges[:, f * LINES : f * LINES + count] = lax.dot_general(
            pick, rest, NT, preferred_element_type=F32
        )
        edges[:, f * LINES + count : (f + 1) * LINES] = jnp.zeros((16, LINES - count), F32)


def advance_edges(
    place, unused, edges, low, high, left, right, shifted, start, coefs, first, second, turned
):
    row_at, col_at, depth_at = place[1], place[2], place[0]
    depth_last, row_last, col_last = place[3], place[4], place[5]
    shape = (4 * EDGE, 128)
    col = lax.broadcasted_iota(jnp.int32, shape, 0)
    lane = lax.broadcasted_iota(jnp.int32, shape, 1)
    cols_in = ((col >= EDGE) | (col_at > 0)) & ((col < 3 * EDGE) | (col_at < col_last))

    def table(b):
        line = lane + 128 * b
        plane = jnp.floor((line.astype(F32) + 0.5) * (1.0 / ROWS)).astype(jnp.int32)
        row = line - plane * ROWS
        rows_in = (
            (row < 32)
            | ((row < 32 + HALO) & (row_at < row_last))
            | ((row >= ROWS - HALO) & (row_at > 0))
        )
        planes_in = ((plane >= HALO) | (depth_at > 0)) & (
            (plane < HALO + 16) | ((plane < PLANES) & (depth_at < depth_last))
        )
        step = jnp.where(rows_in & cols_in & planes_in, TIME_STEP, 0.0).astype(F32)
        return step, row == 0, row == ROWS - 1

    for f in range(4):
        for b in range(BLOCKS):
            cut = slice(f * LINES + 128 * b, f * LINES + 128 * (b + 1))
            own_low, own_high = low[:, cut].astype(F32), high[:, cut].astype(F32)
            if f < 2:
                own_low = own_low + edges[0:8, cut]
                own_high = own_high + edges[8:16, cut]
            gathered = jnp.concatenate(
                [
                    left[:, cut].astype(F32)[:EDGE],
                    own_low[:EDGE],
                    own_high[:EDGE],
                    right[:, cut].astype(F32)[:EDGE],
                ],
                axis=0,
            )
            if f < 2:
                start[f, b] = gathered
            else:
                first[f - 2, b] = gathered
    masks = []
    for b in range(BLOCKS):
        step, first_row, last_row = table(b)
        masks.append((first_row, last_row))
        made = coefficients(step, first[0, b], first[1, b])
        for i in range(6):
            coefs[i, b] = made[i]

    def stage(source, finish):
        held = {}

        def turn(f, b, by):
            b = b % BLOCKS
            if (f, b, by) not in held:
                held[f, b, by] = pltpu.roll(source[f, b], by, 1)
            return held[f, b, by]

        def from_before(f, b, by):
            return jnp.where(lane < by, turn(f, b - 1, by), turn(f, b, by))

        def from_after(f, b, by):
            return jnp.where(lane >= 128 - by, turn(f, b + 1, 128 - by), turn(f, b, 128 - by))

        for b in range(BLOCKS):
            first_row, last_row = masks[b]

            def neighbours(f):
                x = source[f, b]
                return (
                    from_before(f, b, ROWS),
                    from_after(f, b, ROWS),
                    jnp.where(first_row, from_after(f, b, ROWS - 1), from_before(f, b, 1)),
                    jnp.where(last_row, from_before(f, b, ROWS - 1), from_after(f, b, 1)),
                    pltpu.roll(x, 1, 0),
                    pltpu.roll(x, 4 * EDGE - 1, 0),
                )

            moved = stepped(
                (source[0, b], source[1, b]), tuple(coefs[i, b] for i in range(6)), neighbours
            )
            for f in range(2):
                finish(f, b, moved[f])

    def finish_first(f, b, moved):
        first[f, b] = moved

    def finish_second(f, b, moved):
        second[f, b] = 0.75 * start[f, b] + 0.25 * moved

    blank = jnp.zeros((128 - 4 * EDGE, 128), F32)

    def finish_third(f, b, moved):
        new = start[f, b] * (1.0 / 3.0) + (2.0 / 3.0) * moved
        turned[f, 128 * b : 128 * (b + 1), :] = jnp.concatenate([new, blank], axis=0).T

    stage(start, finish_first)
    stage(first, finish_second)
    stage(second, finish_third)
    lane32 = lax.broadcasted_iota(jnp.int32, (32, 128), 1)

    @pl.loop(0, 16, unroll=4)
    def _(k):
        for f in range(2):
            lines = turned[f, pl.ds(pl.multiple_of((k + HALO) * ROWS, 8), 32), :]
            near = pltpu.roll(lines, 128 - EDGE, 1)
            far = pltpu.roll(lines, 128 - 3 * EDGE, 1)
            for shift in range(-RIM, RIM + 1):
                from_far = (lane32 >= 64) & (lane32 < 128 + min(shift, 0)) | (lane32 < shift)
                patch = jnp.where(from_far, far, near)
                patch = pltpu.roll(patch, -shift % 128, 1) if shift else patch
                wrong = (lane32 <= RIM - 1 - shift) | (lane32 >= 128 - RIM - shift)
                pltpu.store(shifted.at[shift + RIM, f, k], patch, mask=wrong)


def render_and_save(away, place, shear, weight, bias, shifted, image, out, sem):
    copy = pltpu.make_async_copy(shifted.at[RIM], out, sem.at[0])
    copy.start()
    render(away, place, shear, weight, bias, shifted, image)
    copy.wait()


def render(away, place, shear, weight, bias, shifted, image):
    count = image.shape[0]
    depth_cells = shifted.shape[2]
    depth_at, depth_last = place[0], place[3]
    first = lax.rem(depth_at + away, depth_last + 1) * count
    middle = 0.5 * depth_cells * (depth_last + 1).astype(F32)

    @pl.loop(0, count)
    def _(j):
        v = first + j
        table = [
            tuple(
                (0.5 if c < 3 else 1.0) * value
                for value in (weight[c, 0, v], weight[c, 1, v], bias[c, v])
            )
            for c in range(4)
        ]
        slope = shear[v]

        for part in range(4):
            strip = slice(part * 8, (part + 1) * 8)

            def march(k, state):
                c0, c1, c2, total, through = state
                place_in_depth = (depth_at * depth_cells + k).astype(F32) + 0.5
                offset = slope * (place_in_depth - middle)
                whole = offset.astype(jnp.int32)
                whole = jnp.where(whole.astype(F32) > offset, whole - 1, whole)
                t = offset - whole.astype(F32)
                i = jnp.clip(whole + RIM, 0, SHIFTS - 2)
                s0 = (1.0 - t) * shifted[i, 0, k, strip] + t * shifted[i + 1, 0, k, strip]
                s1 = (1.0 - t) * shifted[i, 1, k, strip] + t * shifted[i + 1, 1, k, strip]
                logits = [table[c][0] * s0 + table[c][1] * s1 + table[c][2] for c in range(4)]
                dense = logits[3]
                total = total + (jnp.maximum(dense, 0.0) + jnp.log(1.0 + jnp.exp(-jnp.abs(dense))))
                after = jnp.exp2((-RAY_STEP * LOG2E) * total)
                part = through - after
                c0 = c0 + part * jnp.tanh(logits[0])
                c1 = c1 + part * jnp.tanh(logits[1])
                c2 = c2 + part * jnp.tanh(logits[2])
                return c0, c1, c2, total, after

            zero = jnp.zeros((8, 128), F32)
            c0, c1, c2, _, through = lax.fori_loop(
                0, depth_cells, march, (zero, zero, zero, zero, zero + 1.0), unroll=16
            )
            opacity = 1.0 - through
            image[j, 0, strip] = 0.5 * (c0 + opacity)
            image[j, 1, strip] = 0.5 * (c1 + opacity)
            image[j, 2, strip] = 0.5 * (c2 + opacity)
            image[j, 3, strip] = opacity


def deal(place, owners, lengths, warp, select, lengths_wide, warp_own, sem):
    views = warp_own.shape[0]
    copy = pltpu.make_async_copy(warp.at[pl.ds(place[0] * views, views)], warp_own, sem.at[0])
    copy.start()
    row = lax.broadcasted_iota(jnp.int32, (128, 128), 0)
    lane = lax.broadcasted_iota(jnp.int32, (128, 128), 1)
    name = jnp.concatenate([owners[v : v + 1, :] for v in range(views)], axis=1)
    length = jnp.concatenate([lengths[v : v + 1, :] for v in range(views)], axis=1)
    along = jnp.broadcast_to(name, (128, 128))
    across = along.T
    earlier = (along == across) & (row < lane) & (row // 32 == lane // 32)
    rank = jnp.sum(earlier.astype(F32), axis=0, keepdims=True).astype(jnp.int32)
    view = lane[0:1] // 32
    half = select.shape[0] // 2
    codes = name * (views * CAPACITY // 2) + view * (CAPACITY // 2) + rank // 2
    codes = codes + (rank % 2) * half
    slot = lax.broadcasted_iota(jnp.int32, select.shape, 0)
    select[...] = (slot == codes).astype(F32).astype(BF16)
    lengths_wide[...] = jnp.broadcast_to(length, (128, 128)).T
    copy.wait()


def composite(place, order, select, lengths, slab0, slab1, slab2, slab3, outgoing, pieces):
    lane = lax.broadcasted_iota(jnp.int32, (32, 128), 1)
    slabs = (slab0, slab1, slab2, slab3)
    depth_at, devices = place[0], place[3] + 1

    def fetch(which, v, c):
        value = slabs[3][v, c]
        for offset in (2, 1, 0):
            value = jnp.where(which == offset, slabs[offset][v, c], value)
        return value

    for v in range(4):
        keep = lane < lengths[32 * v : 32 * (v + 1), :]
        turn = [
            lax.rem(depth_at - order[position, depth_at * 4 + v] + devices, devices)
            for position in range(4)
        ]
        channels = [fetch(turn[0], v, c) for c in range(4)]
        for position in range(1, 4):
            clear = 1.0 - channels[3]
            channels = [channels[c] + clear * fetch(turn[position], v, c) for c in range(4)]
        for c in range(4):
            pieces[32 * v : 32 * (v + 1), 128 * c : 128 * (c + 1)] = jnp.where(
                keep, channels[c], 0.0
            ).astype(BF16)
    row_id = lax.broadcasted_iota(jnp.int32, (128, 128), 0) + 1
    pieces[:, 512:640] = row_id.astype(F32).astype(BF16)
    dealt = jnp.dot(select[...], pieces[...], preferred_element_type=F32).astype(BF16)
    half = outgoing.shape[0]
    outgoing[:, 0:512] = dealt[:half, 0:512]
    outgoing[:, 512:1024] = dealt[half:, 0:512]
    outgoing[:, 1024:1088] = dealt[:half, 512:576]
    outgoing[:, 1088:1152] = dealt[half:, 576:640]


def resample(incoming, warp, frame):
    rows = incoming.shape[0]
    ids = incoming[:, 1024:1152].astype(F32)
    lane = lax.broadcasted_iota(jnp.int32, (rows, 128), 1)
    swapped = pltpu.roll(ids, 64, 1)
    line = (lane + 1).astype(F32)
    total = jnp.zeros((128, 512), F32)
    for odd in range(2):
        names = jnp.where((lane < 64) == (odd == 0), ids, swapped)
        place = (names == line).astype(F32).astype(BF16)
        part = incoming[:, 512 * odd : 512 * (odd + 1)]
        total = total + lax.dot_general(place, part, TN, preferred_element_type=F32)
    for v in range(4):
        rows = jnp.concatenate(
            [total[32 * v : 32 * (v + 1), 128 * c : 128 * (c + 1)] for c in range(4)], axis=0
        )
        warped = jnp.zeros((128, 128), F32)
        for _ in range(3):
            part = rows.astype(BF16)
            warped = warped + jnp.dot(part, warp[v], preferred_element_type=F32)
            rows = rows - part.astype(F32)
        for c in range(4):
            frame[pl.ds(128 * v + c, 32, stride=4), :] = warped[32 * c : 32 * (c + 1)]


def body(
    species,
    diffusivity,
    reaction_rate,
    shear_rate,
    colour_weight,
    colour_bias,
    slab_order,
    lengths,
    owners,
    warp_matrix,
):
    depth_at, row_at, col_at = (lax.axis_index(a) for a in ("depth", "row", "col"))
    depth_devices, row_devices, col_devices = (lax.axis_size(a) for a in ("depth", "row", "col"))
    view_count = shear_rate.shape[0] // depth_devices

    place = jnp.stack(
        [
            depth_at,
            row_at,
            col_at,
            jnp.int32(depth_devices - 1),
            jnp.int32(row_devices - 1),
            jnp.int32(col_devices - 1),
        ]
    ).astype(jnp.int32)
    fields = tuple(in_hbm(x) for x in (species, diffusivity, reaction_rate))

    face = jax.ShapeDtypeStruct((4, HALO, 32, 128), BF16)
    low, high = call(
        pack_depth,
        (face, face),
        [HBM_SPEC] * 3,
        [pltpu.VMEM((2, 4, HALO, 32, 128), F32), pltpu.SemaphoreType.DMA((8,))],
    )(*fields)
    before, after = shift_up(high, "depth"), shift_down(low, "depth")
    brick_type = jax.ShapeDtypeStruct((4, PLANES, ROWS, 128), F32)
    brick = call(load_brick, brick_type, [HBM_SPEC] * 3, [pltpu.SemaphoreType.DMA((4,))])(*fields)
    face = jax.ShapeDtypeStruct((HALO, 4 * PLANES, 128), BF16)
    brick, low, high = call(
        pack_rows, (brick_type, face, face), [VMEM_SPEC] * 3, aliases={0: 0}
    )(brick, before, after)
    above, below = turn_by(high, "row", 1), turn_by(low, "row", -1)
    slots = col_devices * view_count * CAPACITY
    lines = view_count * 32
    select, lengths_wide, warp_own = call(
        deal,
        (
            jax.ShapeDtypeStruct((slots, lines), BF16),
            jax.ShapeDtypeStruct((lines, 128), jnp.int32),
            jax.ShapeDtypeStruct((view_count, 128, 128), BF16),
        ),
        [SMEM_SPEC, VMEM_SPEC, VMEM_SPEC, HBM_SPEC],
        [pltpu.SemaphoreType.DMA((1,))],
    )(place, owners.reshape(view_count, 32), lengths.reshape(view_count, 32), in_hbm(warp_matrix))

    brick, select, lengths_wide, warp_own = lax.optimization_barrier(
        (brick, select, lengths_wide, warp_own)
    )
    face = jax.ShapeDtypeStruct((8, 4 * LINES), BF16)
    brick, low, high = call(
        pack_columns, (brick_type, face, face), [SMEM_SPEC] + [VMEM_SPEC] * 3, aliases={1: 0}
    )(place, brick, above, below)
    left = shift_up(high, "col")
    right = shift_down(low, "col")
    wide = pltpu.VMEM((2, PLANES, ROWS, 128), F32)
    shifted_type = jax.ShapeDtypeStruct((SHIFTS,) + species.shape, F32)
    shifted, edges = call(
        advance_own,
        (shifted_type, jax.ShapeDtypeStruct((16, 2 * LINES), F32)),
        [SMEM_SPEC, VMEM_SPEC],
        [wide, wide, pltpu.VMEM((6, PLANES, ROWS, 128), F32)],
        limit=12,
    )(place, brick)
    shifted = call(
        advance_edges,
        shifted_type,
        [SMEM_SPEC] + [VMEM_SPEC] * 6,
        [pltpu.VMEM((n, BLOCKS, 4 * EDGE, 128), F32) for n in (2, 6, 2, 2)]
        + [pltpu.VMEM((2, LINES, 128), F32)],
        aliases={1: 0},
    )(place, shifted, edges, low, high, left, right)

    image = jax.ShapeDtypeStruct((view_count, 4, 32, 128), F32)
    weight, bias = jnp.transpose(colour_weight, (1, 2, 0)), colour_bias.T
    slabs = [None] * 4
    for away in (2, 1, 3, 0):
        if away == SAVER:
            drawn, species_out = call(
                functools.partial(render_and_save, away),
                (image, jax.ShapeDtypeStruct(species.shape, F32)),
                [SMEM_SPEC] * 4 + [VMEM_SPEC],
                [pltpu.SemaphoreType.DMA((1,))],
                out_specs=(VMEM_SPEC, HBM_SPEC),
            )(place, shear_rate, weight, bias, shifted)
        else:
            drawn = call(
                functools.partial(render, away), image, [SMEM_SPEC] * 4 + [VMEM_SPEC]
            )(place, shear_rate, weight, bias, shifted)
        if away:
            drawn = turn_by(drawn, "depth", away)
        slabs[away] = drawn
    outgoing = call(
        composite,
        jax.ShapeDtypeStruct((slots // 2, 1152), BF16),
        [SMEM_SPEC] * 2 + [VMEM_SPEC] * 6,
        [pltpu.VMEM((lines, 640), BF16)],
    )(place, slab_order.T, select, lengths_wide, *slabs)
    incoming = lax.all_to_all(
        outgoing.reshape(col_devices, -1, 1152),
        "col",
        split_axis=0,
        concat_axis=0,
        tiled=True,
    ).reshape(slots // 2, 1152)
    frame = call(resample, jax.ShapeDtypeStruct((4 * lines, 128), F32), [VMEM_SPEC] * 2)(
        incoming, warp_own
    )
    return species_out, frame.reshape(view_count, 32, 4, 128)


def solution(mesh):
    in_specs = (
        P(None, "depth", "row", "col"),
        P("depth", "row", "col"),
        P("depth", "row", "col"),
        P(),
        P(),
        P(),
        P(),
        P("depth", "col", "row"),
        P("depth", "col", "row", None),
        P(),
    )
    out_specs = (P(None, "depth", "row", "col"), P("depth", "row", None, "col"))
    return jax.shard_map(body, mesh=mesh, in_specs=in_specs, out_specs=out_specs, check_vma=False)
```

```python
import functools

import jax
import jax.numpy as jnp
from jax import lax
from jax.experimental import pallas as pl
from jax.experimental.pallas import tpu as pltpu
from jax.sharding import PartitionSpec as P

TIME_STEP = 0.1
RAY_STEP = 0.02
LOG2E = 1.4426950408889634
VEL_DEPTH = 0.3
VEL_ROW = 0.2
VEL_COL = 0.4

HALO = 3
RIM = 3
EDGE = 6
PLANES = 22
ROWS = 40
LINES = 896
BLOCKS = LINES // 128
SHIFTS = 2 * RIM + 1
CAPACITY = 4
SAVER = 1

F32 = jnp.float32
BF16 = jnp.bfloat16
VMEM_SPEC = pl.BlockSpec(memory_space=pltpu.VMEM)
SMEM_SPEC = pl.BlockSpec(memory_space=pltpu.SMEM)
HBM_SPEC = pl.BlockSpec(memory_space=pltpu.HBM)
NT = (((1,), (1,)), ((), ()))
TN = (((0,), (0,)), ((), ()))


def call(kernel, out_shape, in_specs, scratch=(), limit=8, aliases=None, out_specs=None):
    return pl.pallas_call(
        kernel,
        out_shape=out_shape,
        in_specs=in_specs,
        out_specs=out_specs or jax.tree.map(lambda unused: VMEM_SPEC, out_shape),
        scratch_shapes=list(scratch),
        input_output_aliases=aliases or {},
        compiler_params=pltpu.CompilerParams(vmem_limit_bytes=limit << 20),
    )


def in_hbm(x):
    return pltpu.with_memory_space_constraint(x, pltpu.HBM)


def turn_by(x, axis, steps):
    n = lax.axis_size(axis)
    return lax.ppermute(x, axis, [(i, (i + steps) % n) for i in range(n)])


def shift_up(x, axis):
    n = lax.axis_size(axis)
    return lax.ppermute(x, axis, [(i, i + 1) for i in range(n - 1)])


def shift_down(x, axis):
    n = lax.axis_size(axis)
    return lax.ppermute(x, axis, [(i + 1, i) for i in range(n - 1)])


def pack_depth(species, diff, rate, low, high, held, sems):
    copies = []
    for side, first in ((0, 0), (1, 16 - HALO)):
        cut = pl.ds(first, HALO)
        for source, at in (
            (species.at[0, cut], 0),
            (species.at[1, cut], 1),
            (diff.at[cut], 2),
            (rate.at[cut], 3),
        ):
            copies.append(
                pltpu.make_async_copy(source, held.at[side, at], sems.at[4 * side + at])
            )
    for copy in copies:
        copy.start()
    for copy in copies:
        copy.wait()
    low[...] = held[0].astype(BF16)
    high[...] = held[1].astype(BF16)


def load_brick(species, diff, rate, brick, sems):
    copies = [
        pltpu.make_async_copy(
            source, brick.at[f, pl.ds(HALO, 16), pl.ds(0, 32), :], sems.at[f]
        )
        for f, source in enumerate((species.at[0], species.at[1], diff, rate))
    ]
    for copy in copies:
        copy.start()
    for f in range(4):
        brick[f, :, 32:ROWS, :] = jnp.zeros((PLANES, ROWS - 32, 128), F32)
    for copy in copies:
        copy.wait()


def pack_rows(unused, before, after, brick, low, high):
    for f in range(4):
        brick[f, 0:HALO, 0:32, :] = before[f].astype(F32)
        brick[f, HALO + 16 : 22, 0:32, :] = after[f].astype(F32)
    lines = brick.reshape(4 * PLANES * ROWS, 128)
    for r in range(HALO):
        low[r] = lines[pl.ds(r, 4 * PLANES, stride=ROWS), :].astype(BF16)
        high[r] = lines[pl.ds(32 - HALO + r, 4 * PLANES, stride=ROWS), :].astype(BF16)


def column_picker(first_low, first_high):
    j = lax.broadcasted_iota(jnp.int32, (16, 128), 0)
    lane = lax.broadcasted_iota(jnp.int32, (16, 128), 1)
    at = jnp.where(j < 8, first_low + j, first_high + j - 8)
    return ((lane == at) & (j % 8 < EDGE)).astype(F32).astype(BF16)


def pack_columns(place, unused, above, below, brick, low, high):
    has_above = jnp.where(place[1] > 0, 1.0, 0.0).astype(F32)
    has_below = jnp.where(place[1] < place[4], 1.0, 0.0).astype(F32)
    lines = brick.reshape(4 * PLANES * ROWS, 128)
    for r in range(HALO):
        lines[pl.ds(ROWS - HALO + r, 4 * PLANES, stride=ROWS), :] = has_above * above[r].astype(F32)
        lines[pl.ds(32 + r, 4 * PLANES, stride=ROWS), :] = has_below * below[r].astype(F32)
    pick = column_picker(0, 128 - EDGE)
    count = PLANES * ROWS
    blank = jnp.zeros((8, LINES - count), BF16)
    for f in range(4):
        rows = brick[f].reshape(count, 128).astype(BF16)
        edge = lax.dot_general(pick, rows, NT, preferred_element_type=F32).astype(BF16)
        at = f * LINES
        for side, part in ((low, edge[:8]), (high, edge[8:])):
            side[:, at : at + count] = part
            side[:, at + count : at + LINES] = blank


def coefficients(step, diffusivity, reaction):
    spread = step * diffusivity
    return (
        1.0 - (6.0 * spread + (VEL_DEPTH + VEL_ROW + VEL_COL) * step),
        spread + VEL_DEPTH * step,
        spread + VEL_ROW * step,
        spread + VEL_COL * step,
        spread,
        step * reaction,
    )


def stepped(fields, coefs, neighbours):
    fuel, heat = fields
    cell, from_depth, from_row, from_col, from_above, reaction = coefs
    square = heat * heat
    burned = reaction * (fuel * (square / (1.0 + square)))
    results = []
    for f in range(2):
        below_depth, above_depth, below_row, above_row, below_col, above_col = neighbours(f)
        total = (
            (cell * fields[f] + from_depth * below_depth)
            + (from_row * below_row + from_col * below_col)
            + from_above * (above_depth + above_row + above_col)
        )
        results.append(total - burned if f == 0 else total + burned)
    return results


def advance_own(place, brick, shifted, edges, first, second, coefs):
    n = ROWS
    depth_at, row_at = place[0], place[1]
    depth_last, row_last = place[3], place[4]
    row = lax.broadcasted_iota(jnp.int32, (n, 128), 0)
    rows_in = (
        (row < 32)
        | ((row < 32 + HALO) & (row_at < row_last))
        | ((row >= n - HALO) & (row_at > 0))
    )
    step = jnp.where(rows_in, TIME_STEP, 0.0).astype(F32)

    def advanced(source, table, p):
        def neighbours(f):
            centre = source[f, p]
            return (
                source[f, p - 1],
                source[f, p + 1],
                pltpu.roll(centre, 1, 0),
                pltpu.roll(centre, n - 1, 0),
                pltpu.roll(centre, 1, 1),
                pltpu.roll(centre, 127, 1),
            )

        return stepped((source[0, p], source[1, p]), table, neighbours)

    def table_at(p):
        return tuple(coefs[i, p] for i in range(6))

    @pl.loop(1, 21, unroll=4)
    def _(p):
        ok = ((p >= HALO) | (depth_at > 0)) & ((p < HALO + 16) | (depth_at < depth_last))
        scale = jnp.where(ok, 1.0, 0.0).astype(F32)
        table = coefficients(step * scale, brick[2, p], brick[3, p])
        for i in range(6):
            coefs[i, p] = table[i]
        moved = advanced(brick, table, p)
        for f in range(2):
            first[f, p] = moved[f]

    @pl.loop(2, 20, unroll=3)
    def _(p):
        moved = advanced(first, table_at(p), p)
        for f in range(2):
            second[f, p] = 0.75 * brick[f, p] + 0.25 * moved[f]

    def shift_plane(k):
        for f in range(2):
            new = shifted[RIM, f, k]
            for shift in range(-RIM, RIM + 1):
                if shift:
                    shifted[shift + RIM, f, k] = pltpu.roll(new, -shift % 128, 1)

    @pl.loop(0, 16, unroll=2)
    def _(k):
        p = k + HALO
        shift_plane(jnp.maximum(k - 1, 0))
        moved = advanced(second, table_at(p), p)
        for f in range(2):
            shifted[RIM, f, k] = (brick[f, p] * (1.0 / 3.0) + (2.0 / 3.0) * moved[f])[:32]

    shift_plane(15)

    pick = column_picker(0, 128 - EDGE)
    count = PLANES * ROWS
    for f in range(2):
        rows = brick[f].reshape(count, 128)
        rest = (rows - rows.astype(BF16).astype(F32)).astype(BF16)
        edges[:, f * LINES : f * LINES + count] = lax.dot_general(
            pick, rest, NT, preferred_element_type=F32
        )
        edges[:, f * LINES + count : (f + 1) * LINES] = jnp.zeros((16, LINES - count), F32)


def advance_edges(
    place, unused, edges, low, high, left, right, shifted, start, coefs, first, second
):
    row_at, col_at, depth_at = place[1], place[2], place[0]
    depth_last, row_last, col_last = place[3], place[4], place[5]
    shape = (4 * EDGE, 128)
    col = lax.broadcasted_iota(jnp.int32, shape, 0)
    lane = lax.broadcasted_iota(jnp.int32, shape, 1)
    cols_in = ((col >= EDGE) | (col_at > 0)) & ((col < 3 * EDGE) | (col_at < col_last))

    def table(b):
        line = lane + 128 * b
        plane = jnp.floor((line.astype(F32) + 0.5) * (1.0 / ROWS)).astype(jnp.int32)
        row = line - plane * ROWS
        rows_in = (
            (row < 32)
            | ((row < 32 + HALO) & (row_at < row_last))
            | ((row >= ROWS - HALO) & (row_at > 0))
        )
        planes_in = ((plane >= HALO) | (depth_at > 0)) & (
            (plane < HALO + 16) | ((plane < PLANES) & (depth_at < depth_last))
        )
        step = jnp.where(rows_in & cols_in & planes_in, TIME_STEP, 0.0).astype(F32)
        return step, row == 0, row == ROWS - 1

    for f in range(4):
        for b in range(BLOCKS):
            cut = slice(f * LINES + 128 * b, f * LINES + 128 * (b + 1))
            own_low, own_high = low[:, cut].astype(F32), high[:, cut].astype(F32)
            if f < 2:
                own_low = own_low + edges[0:8, cut]
                own_high = own_high + edges[8:16, cut]
            gathered = jnp.concatenate(
                [
                    left[:, cut].astype(F32)[:EDGE],
                    own_low[:EDGE],
                    own_high[:EDGE],
                    right[:, cut].astype(F32)[:EDGE],
                ],
                axis=0,
            )
            if f < 2:
                start[f, b] = gathered
            else:
                first[f - 2, b] = gathered
    masks = []
    for b in range(BLOCKS):
        step, first_row, last_row = table(b)
        masks.append((first_row, last_row))
        made = coefficients(step, first[0, b], first[1, b])
        for i in range(6):
            coefs[i, b] = made[i]

    def stage(source, finish):
        held = {}

        def turn(f, b, by):
            b = b % BLOCKS
            if (f, b, by) not in held:
                held[f, b, by] = pltpu.roll(source[f, b], by, 1)
            return held[f, b, by]

        def from_before(f, b, by):
            return jnp.where(lane < by, turn(f, b - 1, by), turn(f, b, by))

        def from_after(f, b, by):
            return jnp.where(lane >= 128 - by, turn(f, b + 1, 128 - by), turn(f, b, 128 - by))

        for b in range(BLOCKS):
            first_row, last_row = masks[b]

            def neighbours(f):
                x = source[f, b]
                return (
                    from_before(f, b, ROWS),
                    from_after(f, b, ROWS),
                    jnp.where(first_row, from_after(f, b, ROWS - 1), from_before(f, b, 1)),
                    jnp.where(last_row, from_before(f, b, ROWS - 1), from_after(f, b, 1)),
                    pltpu.roll(x, 1, 0),
                    pltpu.roll(x, 4 * EDGE - 1, 0),
                )

            moved = stepped(
                (source[0, b], source[1, b]), tuple(coefs[i, b] for i in range(6)), neighbours
            )
            for f in range(2):
                finish(f, b, moved[f])

    def finish_first(f, b, moved):
        first[f, b] = moved

    def finish_second(f, b, moved):
        second[f, b] = 0.75 * start[f, b] + 0.25 * moved

    def finish_third(f, b, moved):
        first[f, b] = start[f, b] * (1.0 / 3.0) + (2.0 / 3.0) * moved

    stage(start, finish_first)
    stage(first, finish_second)
    stage(second, finish_third)

    m = lax.broadcasted_iota(jnp.int32, (4 * EDGE, 128), 0)
    column = jnp.where(m < 2 * EDGE, m - EDGE, m + 128 - 3 * EDGE)
    used = ((column >= -RIM) & (column < RIM)) | ((column >= 128 - RIM) & (column < 128 + RIM))
    placed = jnp.concatenate(
        [(used & (column == lane + shift)).astype(F32) for shift in range(-RIM, RIM + 1)], axis=1
    )
    placed = jnp.concatenate([placed] * 3, axis=0).astype(BF16)
    lane8 = lax.broadcasted_iota(jnp.int32, (8, 128), 1)
    for f in range(2):
        for b in range(BLOCKS):
            rest = first[f, b]
            parts = []
            for _ in range(3):
                part = rest.astype(BF16).astype(F32)
                parts.append(part)
                rest = rest - part
            patch = lax.dot_general(
                jnp.concatenate(parts, axis=0).astype(BF16), placed, TN, preferred_element_type=F32
            )
            for g in range(16):
                plane, strip = divmod(16 * b + g, ROWS // 8)
                if strip == 4 or not HALO <= plane < HALO + 16:
                    continue
                for i in range(SHIFTS):
                    shift = i - RIM
                    wrong = (lane8 < RIM - shift) | (lane8 >= 128 - RIM - shift)
                    pltpu.store(
                        shifted.at[i, f, plane - HALO, 8 * strip : 8 * strip + 8],
                        patch[8 * g : 8 * g + 8, 128 * i : 128 * (i + 1)],
                        mask=wrong,
                    )


def render_and_save(away, place, shear, weight, bias, shifted, image, out, sem):
    copy = pltpu.make_async_copy(shifted.at[RIM], out, sem.at[0])
    copy.start()
    render(away, place, shear, weight, bias, shifted, image)
    copy.wait()


def render(away, place, shear, weight, bias, shifted, image):
    count = image.shape[0]
    depth_cells = shifted.shape[2]
    depth_at, depth_last = place[0], place[3]
    first = lax.rem(depth_at + away, depth_last + 1) * count
    middle = 0.5 * depth_cells * (depth_last + 1).astype(F32)

    @pl.loop(0, count)
    def _(j):
        v = first + j
        table = [
            tuple(
                (0.5 if c < 3 else 1.0) * value
                for value in (weight[c, 0, v], weight[c, 1, v], bias[c, v])
            )
            for c in range(4)
        ]
        slope = shear[v]

        for part in range(4):
            strip = slice(part * 8, (part + 1) * 8)

            def march(k, state):
                c0, c1, c2, total, through = state
                place_in_depth = (depth_at * depth_cells + k).astype(F32) + 0.5
                offset = slope * (place_in_depth - middle)
                whole = offset.astype(jnp.int32)
                whole = jnp.where(whole.astype(F32) > offset, whole - 1, whole)
                t = offset - whole.astype(F32)
                i = jnp.clip(whole + RIM, 0, SHIFTS - 2)
                s0 = (1.0 - t) * shifted[i, 0, k, strip] + t * shifted[i + 1, 0, k, strip]
                s1 = (1.0 - t) * shifted[i, 1, k, strip] + t * shifted[i + 1, 1, k, strip]
                logits = [table[c][0] * s0 + table[c][1] * s1 + table[c][2] for c in range(4)]
                dense = logits[3]
                total = total + (jnp.maximum(dense, 0.0) + jnp.log(1.0 + jnp.exp(-jnp.abs(dense))))
                after = jnp.exp2((-RAY_STEP * LOG2E) * total)
                part = through - after
                c0 = c0 + part * jnp.tanh(logits[0])
                c1 = c1 + part * jnp.tanh(logits[1])
                c2 = c2 + part * jnp.tanh(logits[2])
                return c0, c1, c2, total, after

            zero = jnp.zeros((8, 128), F32)
            c0, c1, c2, _, through = lax.fori_loop(
                0, depth_cells, march, (zero, zero, zero, zero, zero + 1.0), unroll=16
            )
            opacity = 1.0 - through
            image[j, 0, strip] = 0.5 * (c0 + opacity)
            image[j, 1, strip] = 0.5 * (c1 + opacity)
            image[j, 2, strip] = 0.5 * (c2 + opacity)
            image[j, 3, strip] = opacity


def deal(place, owners, lengths, warp, select, lengths_wide, warp_own, sem):
    views = warp_own.shape[0]
    copy = pltpu.make_async_copy(warp.at[pl.ds(place[0] * views, views)], warp_own, sem.at[0])
    copy.start()
    row = lax.broadcasted_iota(jnp.int32, (128, 128), 0)
    lane = lax.broadcasted_iota(jnp.int32, (128, 128), 1)
    name = jnp.concatenate([owners[v : v + 1, :] for v in range(views)], axis=1)
    length = jnp.concatenate([lengths[v : v + 1, :] for v in range(views)], axis=1)
    along = jnp.broadcast_to(name, (128, 128))
    across = along.T
    earlier = (along == across) & (row < lane) & (row // 32 == lane // 32)
    rank = jnp.sum(earlier.astype(F32), axis=0, keepdims=True).astype(jnp.int32)
    view = lane[0:1] // 32
    half = select.shape[0] // 2
    codes = name * (views * CAPACITY // 2) + view * (CAPACITY // 2) + rank // 2
    codes = codes + (rank % 2) * half
    slot = lax.broadcasted_iota(jnp.int32, select.shape, 0)
    select[...] = (slot == codes).astype(F32).astype(BF16)
    lengths_wide[...] = jnp.broadcast_to(length, (128, 128)).T
    copy.wait()


def composite(place, order, select, lengths, slab0, slab1, slab2, slab3, outgoing, pieces):
    lane = lax.broadcasted_iota(jnp.int32, (32, 128), 1)
    slabs = (slab0, slab1, slab2, slab3)
    depth_at, devices = place[0], place[3] + 1

    def fetch(which, v, c):
        value = slabs[3][v, c]
        for offset in (2, 1, 0):
            value = jnp.where(which == offset, slabs[offset][v, c], value)
        return value

    for v in range(4):
        keep = lane < lengths[32 * v : 32 * (v + 1), :]
        turn = [
            lax.rem(depth_at - order[position, depth_at * 4 + v] + devices, devices)
            for position in range(4)
        ]
        channels = [fetch(turn[0], v, c) for c in range(4)]
        for position in range(1, 4):
            clear = 1.0 - channels[3]
            channels = [channels[c] + clear * fetch(turn[position], v, c) for c in range(4)]
        for c in range(4):
            pieces[32 * v : 32 * (v + 1), 128 * c : 128 * (c + 1)] = jnp.where(
                keep, channels[c], 0.0
            ).astype(BF16)
    row_id = lax.broadcasted_iota(jnp.int32, (128, 128), 0) + 1
    pieces[:, 512:640] = row_id.astype(F32).astype(BF16)
    dealt = jnp.dot(select[...], pieces[...], preferred_element_type=F32).astype(BF16)
    half = outgoing.shape[0]
    outgoing[:, 0:512] = dealt[:half, 0:512]
    outgoing[:, 512:1024] = dealt[half:, 0:512]
    outgoing[:, 1024:1088] = dealt[:half, 512:576]
    outgoing[:, 1088:1152] = dealt[half:, 576:640]


def resample(incoming, warp, frame):
    rows = incoming.shape[0]
    ids = incoming[:, 1024:1152].astype(F32)
    lane = lax.broadcasted_iota(jnp.int32, (rows, 128), 1)
    swapped = pltpu.roll(ids, 64, 1)
    line = (lane + 1).astype(F32)
    total = jnp.zeros((128, 512), F32)
    for odd in range(2):
        names = jnp.where((lane < 64) == (odd == 0), ids, swapped)
        place = (names == line).astype(F32).astype(BF16)
        part = incoming[:, 512 * odd : 512 * (odd + 1)]
        total = total + lax.dot_general(place, part, TN, preferred_element_type=F32)
    for v in range(4):
        rows = jnp.concatenate(
            [total[32 * v : 32 * (v + 1), 128 * c : 128 * (c + 1)] for c in range(4)], axis=0
        )
        warped = jnp.zeros((128, 128), F32)
        for _ in range(3):
            part = rows.astype(BF16)
            warped = warped + jnp.dot(part, warp[v], preferred_element_type=F32)
            rows = rows - part.astype(F32)
        for c in range(4):
            frame[pl.ds(128 * v + c, 32, stride=4), :] = warped[32 * c : 32 * (c + 1)]


def body(
    species,
    diffusivity,
    reaction_rate,
    shear_rate,
    colour_weight,
    colour_bias,
    slab_order,
    lengths,
    owners,
    warp_matrix,
):
    depth_at, row_at, col_at = (lax.axis_index(a) for a in ("depth", "row", "col"))
    depth_devices, row_devices, col_devices = (lax.axis_size(a) for a in ("depth", "row", "col"))
    view_count = shear_rate.shape[0] // depth_devices

    place = jnp.stack(
        [
            depth_at,
            row_at,
            col_at,
            jnp.int32(depth_devices - 1),
            jnp.int32(row_devices - 1),
            jnp.int32(col_devices - 1),
        ]
    ).astype(jnp.int32)
    fields = tuple(in_hbm(x) for x in (species, diffusivity, reaction_rate))

    face = jax.ShapeDtypeStruct((4, HALO, 32, 128), BF16)
    low, high = call(
        pack_depth,
        (face, face),
        [HBM_SPEC] * 3,
        [pltpu.VMEM((2, 4, HALO, 32, 128), F32), pltpu.SemaphoreType.DMA((8,))],
    )(*fields)
    before, after = shift_up(high, "depth"), shift_down(low, "depth")
    brick_type = jax.ShapeDtypeStruct((4, PLANES, ROWS, 128), F32)
    brick = call(load_brick, brick_type, [HBM_SPEC] * 3, [pltpu.SemaphoreType.DMA((4,))])(*fields)
    face = jax.ShapeDtypeStruct((HALO, 4 * PLANES, 128), BF16)
    brick, low, high = call(
        pack_rows, (brick_type, face, face), [VMEM_SPEC] * 3, aliases={0: 0}
    )(brick, before, after)
    above, below = turn_by(high, "row", 1), turn_by(low, "row", -1)
    slots = col_devices * view_count * CAPACITY
    lines = view_count * 32
    select, lengths_wide, warp_own = call(
        deal,
        (
            jax.ShapeDtypeStruct((slots, lines), BF16),
            jax.ShapeDtypeStruct((lines, 128), jnp.int32),
            jax.ShapeDtypeStruct((view_count, 128, 128), BF16),
        ),
        [SMEM_SPEC, VMEM_SPEC, VMEM_SPEC, HBM_SPEC],
        [pltpu.SemaphoreType.DMA((1,))],
    )(place, owners.reshape(view_count, 32), lengths.reshape(view_count, 32), in_hbm(warp_matrix))

    brick, select, lengths_wide, warp_own = lax.optimization_barrier(
        (brick, select, lengths_wide, warp_own)
    )
    face = jax.ShapeDtypeStruct((8, 4 * LINES), BF16)
    brick, low, high = call(
        pack_columns, (brick_type, face, face), [SMEM_SPEC] + [VMEM_SPEC] * 3, aliases={1: 0}
    )(place, brick, above, below)
    left = shift_up(high, "col")
    right = shift_down(low, "col")
    wide = pltpu.VMEM((2, PLANES, ROWS, 128), F32)
    shifted_type = jax.ShapeDtypeStruct((SHIFTS,) + species.shape, F32)
    shifted, edges = call(
        advance_own,
        (shifted_type, jax.ShapeDtypeStruct((16, 2 * LINES), F32)),
        [SMEM_SPEC, VMEM_SPEC],
        [wide, wide, pltpu.VMEM((6, PLANES, ROWS, 128), F32)],
        limit=12,
    )(place, brick)
    shifted = call(
        advance_edges,
        shifted_type,
        [SMEM_SPEC] + [VMEM_SPEC] * 6,
        [pltpu.VMEM((n, BLOCKS, 4 * EDGE, 128), F32) for n in (2, 6, 2, 2)],
        aliases={1: 0},
    )(place, shifted, edges, low, high, left, right)

    image = jax.ShapeDtypeStruct((view_count, 4, 32, 128), F32)
    weight, bias = jnp.transpose(colour_weight, (1, 2, 0)), colour_bias.T
    slabs = [None] * 4
    for away in (2, 1, 3, 0):
        if away == SAVER:
            drawn, species_out = call(
                functools.partial(render_and_save, away),
                (image, jax.ShapeDtypeStruct(species.shape, F32)),
                [SMEM_SPEC] * 4 + [VMEM_SPEC],
                [pltpu.SemaphoreType.DMA((1,))],
                out_specs=(VMEM_SPEC, HBM_SPEC),
            )(place, shear_rate, weight, bias, shifted)
        else:
            drawn = call(
                functools.partial(render, away), image, [SMEM_SPEC] * 4 + [VMEM_SPEC]
            )(place, shear_rate, weight, bias, shifted)
        if away:
            drawn = turn_by(drawn, "depth", away)
        slabs[away] = drawn
    outgoing = call(
        composite,
        jax.ShapeDtypeStruct((slots // 2, 1152), BF16),
        [SMEM_SPEC] * 2 + [VMEM_SPEC] * 6,
        [pltpu.VMEM((lines, 640), BF16)],
    )(place, slab_order.T, select, lengths_wide, *slabs)
    incoming = lax.all_to_all(
        outgoing.reshape(col_devices, -1, 1152),
        "col",
        split_axis=0,
        concat_axis=0,
        tiled=True,
    ).reshape(slots // 2, 1152)
    frame = call(resample, jax.ShapeDtypeStruct((4 * lines, 128), F32), [VMEM_SPEC] * 2)(
        incoming, warp_own
    )
    return species_out, frame.reshape(view_count, 32, 4, 128)


def solution(mesh):
    in_specs = (
        P(None, "depth", "row", "col"),
        P("depth", "row", "col"),
        P("depth", "row", "col"),
        P(),
        P(),
        P(),
        P(),
        P("depth", "col", "row"),
        P("depth", "col", "row", None),
        P(),
    )
    out_specs = (P(None, "depth", "row", "col"), P("depth", "row", None, "col"))
    return jax.shard_map(body, mesh=mesh, in_specs=in_specs, out_specs=out_specs, check_vma=False)
```

```python
import functools

import jax
import jax.numpy as jnp
from jax import lax
from jax.experimental import pallas as pl
from jax.experimental.pallas import tpu as pltpu
from jax.sharding import PartitionSpec as P

TIME_STEP = 0.1
RAY_STEP = 0.02
LOG2E = 1.4426950408889634
VEL_DEPTH = 0.3
VEL_ROW = 0.2
VEL_COL = 0.4

HALO = 3
RIM = 3
EDGE = 6
PLANES = 22
ROWS = 40
LINES = 896
BLOCKS = LINES // 128
SHIFTS = 2 * RIM + 1
CAPACITY = 4
SAVER = 1

F32 = jnp.float32
BF16 = jnp.bfloat16
VMEM_SPEC = pl.BlockSpec(memory_space=pltpu.VMEM)
SMEM_SPEC = pl.BlockSpec(memory_space=pltpu.SMEM)
HBM_SPEC = pl.BlockSpec(memory_space=pltpu.HBM)
NT = (((1,), (1,)), ((), ()))
TN = (((0,), (0,)), ((), ()))


def call(kernel, out_shape, in_specs, scratch=(), limit=8, aliases=None, out_specs=None):
    return pl.pallas_call(
        kernel,
        out_shape=out_shape,
        in_specs=in_specs,
        out_specs=out_specs or jax.tree.map(lambda unused: VMEM_SPEC, out_shape),
        scratch_shapes=list(scratch),
        input_output_aliases=aliases or {},
        compiler_params=pltpu.CompilerParams(vmem_limit_bytes=limit << 20),
    )


def in_hbm(x):
    return pltpu.with_memory_space_constraint(x, pltpu.HBM)


def turn_by(x, axis, steps):
    n = lax.axis_size(axis)
    return lax.ppermute(x, axis, [(i, (i + steps) % n) for i in range(n)])


def shift_up(x, axis):
    n = lax.axis_size(axis)
    return lax.ppermute(x, axis, [(i, i + 1) for i in range(n - 1)])


def shift_down(x, axis):
    n = lax.axis_size(axis)
    return lax.ppermute(x, axis, [(i + 1, i) for i in range(n - 1)])


def pack_depth(species, diff, rate, low, high, held, sems):
    copies = []
    for side, first in ((0, 0), (1, 16 - HALO)):
        cut = pl.ds(first, HALO)
        for source, at in (
            (species.at[0, cut], 0),
            (species.at[1, cut], 1),
            (diff.at[cut], 2),
            (rate.at[cut], 3),
        ):
            copies.append(
                pltpu.make_async_copy(source, held.at[side, at], sems.at[4 * side + at])
            )
    for copy in copies:
        copy.start()
    for copy in copies:
        copy.wait()
    low[...] = held[0].astype(BF16)
    high[...] = held[1].astype(BF16)


def load_brick(species, diff, rate, brick, sems):
    copies = [
        pltpu.make_async_copy(
            source, brick.at[f, pl.ds(HALO, 16), pl.ds(0, 32), :], sems.at[f]
        )
        for f, source in enumerate((species.at[0], species.at[1], diff, rate))
    ]
    for copy in copies:
        copy.start()
    for f in range(4):
        brick[f, :, 32:ROWS, :] = jnp.zeros((PLANES, ROWS - 32, 128), F32)
    for copy in copies:
        copy.wait()


def pack_rows(unused, before, after, brick, low, high):
    for f in range(4):
        brick[f, 0:HALO, 0:32, :] = before[f].astype(F32)
        brick[f, HALO + 16 : 22, 0:32, :] = after[f].astype(F32)
    lines = brick.reshape(4 * PLANES * ROWS, 128)
    for r in range(HALO):
        low[r] = lines[pl.ds(r, 4 * PLANES, stride=ROWS), :].astype(BF16)
        high[r] = lines[pl.ds(32 - HALO + r, 4 * PLANES, stride=ROWS), :].astype(BF16)


def column_picker(first_low, first_high):
    j = lax.broadcasted_iota(jnp.int32, (16, 128), 0)
    lane = lax.broadcasted_iota(jnp.int32, (16, 128), 1)
    at = jnp.where(j < 8, first_low + j, first_high + j - 8)
    return ((lane == at) & (j % 8 < EDGE)).astype(F32).astype(BF16)


def pack_columns(place, unused, above, below, brick, low, high):
    has_above = jnp.where(place[1] > 0, 1.0, 0.0).astype(F32)
    has_below = jnp.where(place[1] < place[4], 1.0, 0.0).astype(F32)
    lines = brick.reshape(4 * PLANES * ROWS, 128)
    for r in range(HALO):
        lines[pl.ds(ROWS - HALO + r, 4 * PLANES, stride=ROWS), :] = has_above * above[r].astype(F32)
        lines[pl.ds(32 + r, 4 * PLANES, stride=ROWS), :] = has_below * below[r].astype(F32)
    pick = column_picker(0, 128 - EDGE)
    count = PLANES * ROWS
    blank = jnp.zeros((8, LINES - count), BF16)
    for f in range(4):
        rows = brick[f].reshape(count, 128).astype(BF16)
        edge = lax.dot_general(pick, rows, NT, preferred_element_type=F32).astype(BF16)
        at = f * LINES
        for side, part in ((low, edge[:8]), (high, edge[8:])):
            side[:, at : at + count] = part
            side[:, at + count : at + LINES] = blank


def coefficients(step, diffusivity, reaction):
    spread = step * diffusivity
    return (
        1.0 - (6.0 * spread + (VEL_DEPTH + VEL_ROW + VEL_COL) * step),
        spread + VEL_DEPTH * step,
        spread + VEL_ROW * step,
        spread + VEL_COL * step,
        spread,
        step * reaction,
    )


def stepped(fields, coefs, neighbours):
    fuel, heat = fields
    cell, from_depth, from_row, from_col, from_above, reaction = coefs
    square = heat * heat
    burned = reaction * (fuel * (square / (1.0 + square)))
    results = []
    for f in range(2):
        below_depth, above_depth, below_row, above_row, below_col, above_col = neighbours(f)
        total = (
            (cell * fields[f] + from_depth * below_depth)
            + (from_row * below_row + from_col * below_col)
            + from_above * (above_depth + above_row + above_col)
        )
        results.append(total - burned if f == 0 else total + burned)
    return results


def advance_own(place, brick, shifted, edges, first, second, coefs):
    n = ROWS
    depth_at, row_at = place[0], place[1]
    depth_last, row_last = place[3], place[4]
    row = lax.broadcasted_iota(jnp.int32, (n, 128), 0)
    rows_in = (
        (row < 32)
        | ((row < 32 + HALO) & (row_at < row_last))
        | ((row >= n - HALO) & (row_at > 0))
    )
    step = jnp.where(rows_in, TIME_STEP, 0.0).astype(F32)

    def advanced(source, table, p):
        def neighbours(f):
            centre = source[f, p]
            return (
                source[f, p - 1],
                source[f, p + 1],
                pltpu.roll(centre, 1, 0),
                pltpu.roll(centre, n - 1, 0),
                pltpu.roll(centre, 1, 1),
                pltpu.roll(centre, 127, 1),
            )

        return stepped((source[0, p], source[1, p]), table, neighbours)

    def table_at(p):
        return tuple(coefs[i, p] for i in range(6))

    @pl.loop(1, 21, unroll=4)
    def _(p):
        ok = ((p >= HALO) | (depth_at > 0)) & ((p < HALO + 16) | (depth_at < depth_last))
        scale = jnp.where(ok, 1.0, 0.0).astype(F32)
        table = coefficients(step * scale, brick[2, p], brick[3, p])
        for i in range(6):
            coefs[i, p] = table[i]
        moved = advanced(brick, table, p)
        for f in range(2):
            first[f, p] = moved[f]

    @pl.loop(2, 20, unroll=3)
    def _(p):
        moved = advanced(first, table_at(p), p)
        for f in range(2):
            second[f, p] = 0.75 * brick[f, p] + 0.25 * moved[f]

    def shift_plane(k):
        for f in range(2):
            new = shifted[RIM, f, k]
            for shift in range(-RIM, RIM + 1):
                if shift:
                    shifted[shift + RIM, f, k] = pltpu.roll(new, -shift % 128, 1)

    @pl.loop(0, 16, unroll=2)
    def _(k):
        p = k + HALO
        shift_plane(jnp.maximum(k - 1, 0))
        moved = advanced(second, table_at(p), p)
        for f in range(2):
            shifted[RIM, f, k] = (brick[f, p] * (1.0 / 3.0) + (2.0 / 3.0) * moved[f])[:32]

    shift_plane(15)

    pick = column_picker(0, 128 - EDGE)
    count = PLANES * ROWS
    for f in range(2):
        rows = brick[f].reshape(count, 128)
        rest = (rows - rows.astype(BF16).astype(F32)).astype(BF16)
        edges[:, f * LINES : f * LINES + count] = lax.dot_general(
            pick, rest, NT, preferred_element_type=F32
        )
        edges[:, f * LINES + count : (f + 1) * LINES] = jnp.zeros((16, LINES - count), F32)


def advance_edges(
    place, unused, edges, low, high, left, right, shifted, start, coefs, first, second
):
    row_at, col_at, depth_at = place[1], place[2], place[0]
    depth_last, row_last, col_last = place[3], place[4], place[5]
    shape = (4 * EDGE, 128)
    col = lax.broadcasted_iota(jnp.int32, shape, 0)
    lane = lax.broadcasted_iota(jnp.int32, shape, 1)
    cols_in = ((col >= EDGE) | (col_at > 0)) & ((col < 3 * EDGE) | (col_at < col_last))

    def table(b):
        line = lane + 128 * b
        plane = jnp.floor((line.astype(F32) + 0.5) * (1.0 / ROWS)).astype(jnp.int32)
        row = line - plane * ROWS
        rows_in = (
            (row < 32)
            | ((row < 32 + HALO) & (row_at < row_last))
            | ((row >= ROWS - HALO) & (row_at > 0))
        )
        planes_in = ((plane >= HALO) | (depth_at > 0)) & (
            (plane < HALO + 16) | ((plane < PLANES) & (depth_at < depth_last))
        )
        step = jnp.where(rows_in & cols_in & planes_in, TIME_STEP, 0.0).astype(F32)
        return step, row == 0, row == ROWS - 1

    for f in range(4):
        for b in range(BLOCKS):
            cut = slice(f * LINES + 128 * b, f * LINES + 128 * (b + 1))
            own_low, own_high = low[:, cut].astype(F32), high[:, cut].astype(F32)
            if f < 2:
                own_low = own_low + edges[0:8, cut]
                own_high = own_high + edges[8:16, cut]
            gathered = jnp.concatenate(
                [
                    left[:, cut].astype(F32)[:EDGE],
                    own_low[:EDGE],
                    own_high[:EDGE],
                    right[:, cut].astype(F32)[:EDGE],
                ],
                axis=0,
            )
            if f < 2:
                start[f, b] = gathered
            else:
                first[f - 2, b] = gathered
    masks = []
    for b in range(BLOCKS):
        step, first_row, last_row = table(b)
        masks.append((first_row, last_row))
        made = coefficients(step, first[0, b], first[1, b])
        for i in range(6):
            coefs[i, b] = made[i]

    def stage(source, finish):
        held = {}

        def turn(f, b, by):
            b = b % BLOCKS
            if (f, b, by) not in held:
                held[f, b, by] = pltpu.roll(source[f, b], by, 1)
            return held[f, b, by]

        def from_before(f, b, by):
            return jnp.where(lane < by, turn(f, b - 1, by), turn(f, b, by))

        def from_after(f, b, by):
            return jnp.where(lane >= 128 - by, turn(f, b + 1, 128 - by), turn(f, b, 128 - by))

        for b in range(BLOCKS):
            first_row, last_row = masks[b]

            def neighbours(f):
                x = source[f, b]
                return (
                    from_before(f, b, ROWS),
                    from_after(f, b, ROWS),
                    jnp.where(first_row, from_after(f, b, ROWS - 1), from_before(f, b, 1)),
                    jnp.where(last_row, from_before(f, b, ROWS - 1), from_after(f, b, 1)),
                    pltpu.roll(x, 1, 0),
                    pltpu.roll(x, 4 * EDGE - 1, 0),
                )

            moved = stepped(
                (source[0, b], source[1, b]), tuple(coefs[i, b] for i in range(6)), neighbours
            )
            for f in range(2):
                finish(f, b, moved[f])

    def finish_first(f, b, moved):
        first[f, b] = moved

    def finish_second(f, b, moved):
        second[f, b] = 0.75 * start[f, b] + 0.25 * moved

    def finish_third(f, b, moved):
        first[f, b] = start[f, b] * (1.0 / 3.0) + (2.0 / 3.0) * moved

    stage(start, finish_first)
    stage(first, finish_second)
    stage(second, finish_third)

    m = lax.broadcasted_iota(jnp.int32, (4 * EDGE, 128), 0)
    column = jnp.where(m < 2 * EDGE, m - EDGE, m + 128 - 3 * EDGE)
    used = ((column >= -RIM) & (column < RIM)) | ((column >= 128 - RIM) & (column < 128 + RIM))
    placed = jnp.concatenate(
        [(used & (column == lane + shift)).astype(F32) for shift in range(-RIM, RIM + 1)], axis=1
    )
    placed = jnp.concatenate([placed] * 3, axis=0).astype(BF16)
    lane8 = lax.broadcasted_iota(jnp.int32, (8, 128), 1)
    for f in range(2):
        for b in range(BLOCKS):
            rest = first[f, b]
            parts = []
            for _ in range(3):
                part = rest.astype(BF16).astype(F32)
                parts.append(part)
                rest = rest - part
            patch = lax.dot_general(
                jnp.concatenate(parts, axis=0).astype(BF16), placed, TN, preferred_element_type=F32
            )
            for g in range(16):
                plane, strip = divmod(16 * b + g, ROWS // 8)
                if strip == 4 or not HALO <= plane < HALO + 16:
                    continue
                for i in range(SHIFTS):
                    shift = i - RIM
                    wrong = (lane8 < RIM - shift) | (lane8 >= 128 - RIM - shift)
                    pltpu.store(
                        shifted.at[i, f, plane - HALO, 8 * strip : 8 * strip + 8],
                        patch[8 * g : 8 * g + 8, 128 * i : 128 * (i + 1)],
                        mask=wrong,
                    )


def render_and_save(away, place, shear, weight, bias, shifted, image, out, sem):
    copy = pltpu.make_async_copy(shifted.at[RIM], out, sem.at[0])
    copy.start()
    render(away, place, shear, weight, bias, shifted, image)
    copy.wait()


def render(away, place, shear, weight, bias, shifted, image):
    count = image.shape[0]
    depth_cells = shifted.shape[2]
    depth_at, depth_last = place[0], place[3]
    first = lax.rem(depth_at + away, depth_last + 1) * count
    middle = 0.5 * depth_cells * (depth_last + 1).astype(F32)

    @pl.loop(0, count)
    def _(j):
        v = first + j
        table = [
            tuple(
                (0.5 if c < 3 else LOG2E) * value
                for value in (weight[c, 0, v], weight[c, 1, v], bias[c, v])
            )
            for c in range(4)
        ]
        slope = shear[v]

        for part in range(4):
            strip = slice(part * 8, (part + 1) * 8)

            def march(k, state):
                c0, c1, c2, total, through = state
                place_in_depth = (depth_at * depth_cells + k).astype(F32) + 0.5
                offset = slope * (place_in_depth - middle)
                whole = offset.astype(jnp.int32)
                whole = jnp.where(whole.astype(F32) > offset, whole - 1, whole)
                t = offset - whole.astype(F32)
                i = jnp.clip(whole + RIM, 0, SHIFTS - 2)
                s0 = (1.0 - t) * shifted[i, 0, k, strip] + t * shifted[i + 1, 0, k, strip]
                s1 = (1.0 - t) * shifted[i, 1, k, strip] + t * shifted[i + 1, 1, k, strip]
                logits = [table[c][0] * s0 + table[c][1] * s1 + table[c][2] for c in range(4)]
                total = total + jnp.log(1.0 + jnp.exp2(logits[3]))
                after = jnp.exp2((-RAY_STEP * LOG2E) * total)
                part = through - after
                c0 = c0 + part * jnp.tanh(logits[0])
                c1 = c1 + part * jnp.tanh(logits[1])
                c2 = c2 + part * jnp.tanh(logits[2])
                return c0, c1, c2, total, after

            zero = jnp.zeros((8, 128), F32)
            c0, c1, c2, _, through = lax.fori_loop(
                0, depth_cells, march, (zero, zero, zero, zero, zero + 1.0), unroll=16
            )
            opacity = 1.0 - through
            image[j, 0, strip] = 0.5 * (c0 + opacity)
            image[j, 1, strip] = 0.5 * (c1 + opacity)
            image[j, 2, strip] = 0.5 * (c2 + opacity)
            image[j, 3, strip] = opacity


def deal(place, owners, lengths, warp, select, lengths_wide, warp_own, sem):
    views = warp_own.shape[0]
    copy = pltpu.make_async_copy(warp.at[pl.ds(place[0] * views, views)], warp_own, sem.at[0])
    copy.start()
    row = lax.broadcasted_iota(jnp.int32, (128, 128), 0)
    lane = lax.broadcasted_iota(jnp.int32, (128, 128), 1)
    name = jnp.concatenate([owners[v : v + 1, :] for v in range(views)], axis=1)
    length = jnp.concatenate([lengths[v : v + 1, :] for v in range(views)], axis=1)
    along = jnp.broadcast_to(name, (128, 128))
    across = along.T
    earlier = (along == across) & (row < lane) & (row // 32 == lane // 32)
    rank = jnp.sum(earlier.astype(F32), axis=0, keepdims=True).astype(jnp.int32)
    view = lane[0:1] // 32
    half = select.shape[0] // 2
    codes = name * (views * CAPACITY // 2) + view * (CAPACITY // 2) + rank // 2
    codes = codes + (rank % 2) * half
    slot = lax.broadcasted_iota(jnp.int32, select.shape, 0)
    select[...] = (slot == codes).astype(F32).astype(BF16)
    lengths_wide[...] = jnp.broadcast_to(length, (128, 128)).T
    copy.wait()


def composite(place, order, select, lengths, slab0, slab1, slab2, slab3, outgoing, pieces):
    lane = lax.broadcasted_iota(jnp.int32, (32, 128), 1)
    slabs = (slab0, slab1, slab2, slab3)
    depth_at, devices = place[0], place[3] + 1

    for v in range(4):
        keep = lane < lengths[32 * v : 32 * (v + 1), :]
        when = [jnp.int32(0)] * 4
        for position in range(4):
            turn = lax.rem(depth_at - order[position, depth_at * 4 + v] + devices, devices)
            when = [jnp.where(turn == i, position, when[i]) for i in range(4)]
        opacity = [slabs[i][v, 3] for i in range(4)]
        weight = [None] * 4
        for i in range(4):
            for j in range(4):
                if i != j:
                    ahead = jnp.where(when[j] < when[i], 1.0, 0.0).astype(F32)
                    clear = 1.0 - ahead * opacity[j]
                    weight[i] = clear if weight[i] is None else weight[i] * clear
        for c in range(4):
            value = sum(weight[i] * (slabs[i][v, c] if c < 3 else opacity[i]) for i in range(4))
            pieces[32 * v : 32 * (v + 1), 128 * c : 128 * (c + 1)] = jnp.where(
                keep, value, 0.0
            ).astype(BF16)
    row_id = lax.broadcasted_iota(jnp.int32, (128, 128), 0) + 1
    pieces[:, 512:640] = row_id.astype(F32).astype(BF16)
    dealt = jnp.dot(select[...], pieces[...], preferred_element_type=F32).astype(BF16)
    half = outgoing.shape[0]
    outgoing[:, 0:512] = dealt[:half, 0:512]
    outgoing[:, 512:1024] = dealt[half:, 0:512]
    outgoing[:, 1024:1088] = dealt[:half, 512:576]
    outgoing[:, 1088:1152] = dealt[half:, 576:640]


def resample(incoming, warp, frame):
    rows = incoming.shape[0]
    ids = incoming[:, 1024:1152].astype(F32)
    lane = lax.broadcasted_iota(jnp.int32, (rows, 128), 1)
    swapped = pltpu.roll(ids, 64, 1)
    line = (lane + 1).astype(F32)
    total = jnp.zeros((128, 512), F32)
    for odd in range(2):
        names = jnp.where((lane < 64) == (odd == 0), ids, swapped)
        place = (names == line).astype(F32).astype(BF16)
        part = incoming[:, 512 * odd : 512 * (odd + 1)]
        total = total + lax.dot_general(place, part, TN, preferred_element_type=F32)
    for v in range(4):
        rows = jnp.concatenate(
            [total[32 * v : 32 * (v + 1), 128 * c : 128 * (c + 1)] for c in range(4)], axis=0
        )
        warped = jnp.zeros((128, 128), F32)
        for _ in range(3):
            part = rows.astype(BF16)
            warped = warped + jnp.dot(part, warp[v], preferred_element_type=F32)
            rows = rows - part.astype(F32)
        for c in range(4):
            frame[pl.ds(128 * v + c, 32, stride=4), :] = warped[32 * c : 32 * (c + 1)]


def body(
    species,
    diffusivity,
    reaction_rate,
    shear_rate,
    colour_weight,
    colour_bias,
    slab_order,
    lengths,
    owners,
    warp_matrix,
):
    depth_at, row_at, col_at = (lax.axis_index(a) for a in ("depth", "row", "col"))
    depth_devices, row_devices, col_devices = (lax.axis_size(a) for a in ("depth", "row", "col"))
    view_count = shear_rate.shape[0] // depth_devices

    place = jnp.stack(
        [
            depth_at,
            row_at,
            col_at,
            jnp.int32(depth_devices - 1),
            jnp.int32(row_devices - 1),
            jnp.int32(col_devices - 1),
        ]
    ).astype(jnp.int32)
    fields = tuple(in_hbm(x) for x in (species, diffusivity, reaction_rate))

    face = jax.ShapeDtypeStruct((4, HALO, 32, 128), BF16)
    low, high = call(
        pack_depth,
        (face, face),
        [HBM_SPEC] * 3,
        [pltpu.VMEM((2, 4, HALO, 32, 128), F32), pltpu.SemaphoreType.DMA((8,))],
    )(*fields)
    before, after = shift_up(high, "depth"), shift_down(low, "depth")
    brick_type = jax.ShapeDtypeStruct((4, PLANES, ROWS, 128), F32)
    brick = call(load_brick, brick_type, [HBM_SPEC] * 3, [pltpu.SemaphoreType.DMA((4,))])(*fields)
    face = jax.ShapeDtypeStruct((HALO, 4 * PLANES, 128), BF16)
    brick, low, high = call(
        pack_rows, (brick_type, face, face), [VMEM_SPEC] * 3, aliases={0: 0}
    )(brick, before, after)
    above, below = turn_by(high, "row", 1), turn_by(low, "row", -1)
    slots = col_devices * view_count * CAPACITY
    lines = view_count * 32
    select, lengths_wide, warp_own = call(
        deal,
        (
            jax.ShapeDtypeStruct((slots, lines), BF16),
            jax.ShapeDtypeStruct((lines, 128), jnp.int32),
            jax.ShapeDtypeStruct((view_count, 128, 128), BF16),
        ),
        [SMEM_SPEC, VMEM_SPEC, VMEM_SPEC, HBM_SPEC],
        [pltpu.SemaphoreType.DMA((1,))],
    )(place, owners.reshape(view_count, 32), lengths.reshape(view_count, 32), in_hbm(warp_matrix))

    brick, select, lengths_wide, warp_own = lax.optimization_barrier(
        (brick, select, lengths_wide, warp_own)
    )
    face = jax.ShapeDtypeStruct((8, 4 * LINES), BF16)
    brick, low, high = call(
        pack_columns, (brick_type, face, face), [SMEM_SPEC] + [VMEM_SPEC] * 3, aliases={1: 0}
    )(place, brick, above, below)
    left = shift_up(high, "col")
    right = shift_down(low, "col")
    wide = pltpu.VMEM((2, PLANES, ROWS, 128), F32)
    shifted_type = jax.ShapeDtypeStruct((SHIFTS,) + species.shape, F32)
    shifted, edges = call(
        advance_own,
        (shifted_type, jax.ShapeDtypeStruct((16, 2 * LINES), F32)),
        [SMEM_SPEC, VMEM_SPEC],
        [wide, wide, pltpu.VMEM((6, PLANES, ROWS, 128), F32)],
        limit=12,
    )(place, brick)
    shifted = call(
        advance_edges,
        shifted_type,
        [SMEM_SPEC] + [VMEM_SPEC] * 6,
        [pltpu.VMEM((n, BLOCKS, 4 * EDGE, 128), F32) for n in (2, 6, 2, 2)],
        aliases={1: 0},
    )(place, shifted, edges, low, high, left, right)

    image = jax.ShapeDtypeStruct((view_count, 4, 32, 128), F32)
    weight, bias = jnp.transpose(colour_weight, (1, 2, 0)), colour_bias.T
    slabs = [None] * 4
    for away in (2, 1, 3, 0):
        if away == SAVER:
            drawn, species_out = call(
                functools.partial(render_and_save, away),
                (image, jax.ShapeDtypeStruct(species.shape, F32)),
                [SMEM_SPEC] * 4 + [VMEM_SPEC],
                [pltpu.SemaphoreType.DMA((1,))],
                out_specs=(VMEM_SPEC, HBM_SPEC),
            )(place, shear_rate, weight, bias, shifted)
        else:
            drawn = call(
                functools.partial(render, away), image, [SMEM_SPEC] * 4 + [VMEM_SPEC]
            )(place, shear_rate, weight, bias, shifted)
        if away:
            drawn = turn_by(drawn, "depth", away)
        slabs[away] = drawn
    outgoing = call(
        composite,
        jax.ShapeDtypeStruct((slots // 2, 1152), BF16),
        [SMEM_SPEC] * 2 + [VMEM_SPEC] * 6,
        [pltpu.VMEM((lines, 640), BF16)],
    )(place, slab_order.T, select, lengths_wide, *slabs)
    incoming = lax.all_to_all(
        outgoing.reshape(col_devices, -1, 1152),
        "col",
        split_axis=0,
        concat_axis=0,
        tiled=True,
    ).reshape(slots // 2, 1152)
    frame = call(resample, jax.ShapeDtypeStruct((4 * lines, 128), F32), [VMEM_SPEC] * 2)(
        incoming, warp_own
    )
    return species_out, frame.reshape(view_count, 32, 4, 128)


def solution(mesh):
    in_specs = (
        P(None, "depth", "row", "col"),
        P("depth", "row", "col"),
        P("depth", "row", "col"),
        P(),
        P(),
        P(),
        P(),
        P("depth", "col", "row"),
        P("depth", "col", "row", None),
        P(),
    )
    out_specs = (P(None, "depth", "row", "col"), P("depth", "row", None, "col"))
    return jax.shard_map(body, mesh=mesh, in_specs=in_specs, out_specs=out_specs, check_vma=False)
```

```python
import functools

import jax
import jax.numpy as jnp
from jax import lax
from jax.experimental import pallas as pl
from jax.experimental.pallas import tpu as pltpu
from jax.sharding import PartitionSpec as P

TIME_STEP = 0.1
RAY_STEP = 0.02
LOG2E = 1.4426950408889634
VEL_DEPTH = 0.3
VEL_ROW = 0.2
VEL_COL = 0.4

HALO = 3
RIM = 3
EDGE = 6
PLANES = 22
ROWS = 40
LINES = 896
BLOCKS = LINES // 128
SHIFTS = 2 * RIM + 1
CAPACITY = 4
SAVER = 1

F32 = jnp.float32
BF16 = jnp.bfloat16
VMEM_SPEC = pl.BlockSpec(memory_space=pltpu.VMEM)
SMEM_SPEC = pl.BlockSpec(memory_space=pltpu.SMEM)
HBM_SPEC = pl.BlockSpec(memory_space=pltpu.HBM)
NT = (((1,), (1,)), ((), ()))
TN = (((0,), (0,)), ((), ()))


def call(kernel, out_shape, in_specs, scratch=(), limit=8, aliases=None, out_specs=None):
    return pl.pallas_call(
        kernel,
        out_shape=out_shape,
        in_specs=in_specs,
        out_specs=out_specs or jax.tree.map(lambda unused: VMEM_SPEC, out_shape),
        scratch_shapes=list(scratch),
        input_output_aliases=aliases or {},
        compiler_params=pltpu.CompilerParams(vmem_limit_bytes=limit << 20),
    )


def in_hbm(x):
    return pltpu.with_memory_space_constraint(x, pltpu.HBM)


def turn_by(x, axis, steps):
    n = lax.axis_size(axis)
    return lax.ppermute(x, axis, [(i, (i + steps) % n) for i in range(n)])


def shift_up(x, axis):
    n = lax.axis_size(axis)
    return lax.ppermute(x, axis, [(i, i + 1) for i in range(n - 1)])


def shift_down(x, axis):
    n = lax.axis_size(axis)
    return lax.ppermute(x, axis, [(i + 1, i) for i in range(n - 1)])


def pack_depth(species, diff, rate, low, high, held, sems):
    copies = []
    for side, first in ((0, 0), (1, 16 - HALO)):
        cut = pl.ds(first, HALO)
        for source, at in (
            (species.at[0, cut], 0),
            (species.at[1, cut], 1),
            (diff.at[cut], 2),
            (rate.at[cut], 3),
        ):
            copies.append(
                pltpu.make_async_copy(source, held.at[side, at], sems.at[4 * side + at])
            )
    for copy in copies:
        copy.start()
    for copy in copies:
        copy.wait()
    low[...] = held[0].astype(BF16)
    high[...] = held[1].astype(BF16)


def load_brick(species, diff, rate, brick, edges, sems):
    copies = [
        pltpu.make_async_copy(
            source, brick.at[f, pl.ds(HALO, 16), pl.ds(0, 32), :], sems.at[f]
        )
        for f, source in enumerate((species.at[0], species.at[1], diff, rate))
    ]
    for copy in copies:
        copy.start()
    for f in range(4):
        brick[f, :, 32:ROWS, :] = jnp.zeros((PLANES, ROWS - 32, 128), F32)
        brick[f, 0:HALO, 0:32, :] = jnp.zeros((HALO, 32, 128), F32)
        brick[f, HALO + 16 :, 0:32, :] = jnp.zeros((HALO, 32, 128), F32)
    for copy in copies:
        copy.wait()
    pick = column_picker(0, 128 - EDGE)
    count = PLANES * ROWS
    for f in range(2):
        rows = brick[f].reshape(count, 128)
        rest = (rows - rows.astype(BF16).astype(F32)).astype(BF16)
        edges[:, f * LINES : f * LINES + count] = lax.dot_general(
            pick, rest, NT, preferred_element_type=F32
        )
        edges[:, f * LINES + count : (f + 1) * LINES] = jnp.zeros((16, LINES - count), F32)


def pack_rows(unused, before, after, brick, low, high):
    for f in range(4):
        brick[f, 0:HALO, 0:32, :] = before[f].astype(F32)
        brick[f, HALO + 16 : 22, 0:32, :] = after[f].astype(F32)
    lines = brick.reshape(4 * PLANES * ROWS, 128)
    for r in range(HALO):
        low[r] = lines[pl.ds(r, 4 * PLANES, stride=ROWS), :].astype(BF16)
        high[r] = lines[pl.ds(32 - HALO + r, 4 * PLANES, stride=ROWS), :].astype(BF16)


def column_picker(first_low, first_high):
    j = lax.broadcasted_iota(jnp.int32, (16, 128), 0)
    lane = lax.broadcasted_iota(jnp.int32, (16, 128), 1)
    at = jnp.where(j < 8, first_low + j, first_high + j - 8)
    return ((lane == at) & (j % 8 < EDGE)).astype(F32).astype(BF16)


def pack_columns(place, unused, above, below, brick, low, high):
    has_above = jnp.where(place[1] > 0, 1.0, 0.0).astype(F32)
    has_below = jnp.where(place[1] < place[4], 1.0, 0.0).astype(F32)
    lines = brick.reshape(4 * PLANES * ROWS, 128)
    for r in range(HALO):
        lines[pl.ds(ROWS - HALO + r, 4 * PLANES, stride=ROWS), :] = has_above * above[r].astype(F32)
        lines[pl.ds(32 + r, 4 * PLANES, stride=ROWS), :] = has_below * below[r].astype(F32)
    pick = column_picker(0, 128 - EDGE)
    count = PLANES * ROWS
    blank = jnp.zeros((8, LINES - count), BF16)
    for f in range(4):
        rows = brick[f].reshape(count, 128).astype(BF16)
        edge = lax.dot_general(pick, rows, NT, preferred_element_type=F32).astype(BF16)
        at = f * LINES
        for side, part in ((low, edge[:8]), (high, edge[8:])):
            side[:, at : at + count] = part
            side[:, at + count : at + LINES] = blank


def coefficients(step, diffusivity, reaction):
    spread = step * diffusivity
    return (
        1.0 - (6.0 * spread + (VEL_DEPTH + VEL_ROW + VEL_COL) * step),
        spread + VEL_DEPTH * step,
        spread + VEL_ROW * step,
        spread + VEL_COL * step,
        spread,
        step * reaction,
    )


def stepped(fields, coefs, neighbours):
    fuel, heat = fields
    cell, from_depth, from_row, from_col, from_above, reaction = coefs
    square = heat * heat
    burned = reaction * (fuel * (square / (1.0 + square)))
    results = []
    for f in range(2):
        below_depth, above_depth, below_row, above_row, below_col, above_col = neighbours(f)
        total = (
            (cell * fields[f] + from_depth * below_depth)
            + (from_row * below_row + from_col * below_col)
            + from_above * (above_depth + above_row + above_col)
        )
        results.append(total - burned if f == 0 else total + burned)
    return results


def advance_own(place, brick, shifted, first, second, coefs):
    n = ROWS
    depth_at, row_at = place[0], place[1]
    depth_last, row_last = place[3], place[4]
    row = lax.broadcasted_iota(jnp.int32, (n, 128), 0)
    rows_in = (
        (row < 32)
        | ((row < 32 + HALO) & (row_at < row_last))
        | ((row >= n - HALO) & (row_at > 0))
    )
    step = jnp.where(rows_in, TIME_STEP, 0.0).astype(F32)

    def advanced(source, table, p):
        def neighbours(f):
            centre = source[f, p]
            return (
                source[f, p - 1],
                source[f, p + 1],
                pltpu.roll(centre, 1, 0),
                pltpu.roll(centre, n - 1, 0),
                pltpu.roll(centre, 1, 1),
                pltpu.roll(centre, 127, 1),
            )

        return stepped((source[0, p], source[1, p]), table, neighbours)

    def table_at(p):
        return tuple(coefs[i, p] for i in range(6))

    @pl.loop(1, 21, unroll=4)
    def _(p):
        ok = ((p >= HALO) | (depth_at > 0)) & ((p < HALO + 16) | (depth_at < depth_last))
        scale = jnp.where(ok, 1.0, 0.0).astype(F32)
        table = coefficients(step * scale, brick[2, p], brick[3, p])
        for i in range(6):
            coefs[i, p] = table[i]
        moved = advanced(brick, table, p)
        for f in range(2):
            first[f, p] = moved[f]

    @pl.loop(2, 20, unroll=3)
    def _(p):
        moved = advanced(first, table_at(p), p)
        for f in range(2):
            second[f, p] = 0.75 * brick[f, p] + 0.25 * moved[f]

    def shift_plane(k):
        for f in range(2):
            new = shifted[RIM, f, k]
            for shift in range(-RIM, RIM + 1):
                if shift:
                    shifted[shift + RIM, f, k] = pltpu.roll(new, -shift % 128, 1)

    @pl.loop(0, 16, unroll=2)
    def _(k):
        p = k + HALO
        shift_plane(jnp.maximum(k - 1, 0))
        moved = advanced(second, table_at(p), p)
        for f in range(2):
            shifted[RIM, f, k] = (brick[f, p] * (1.0 / 3.0) + (2.0 / 3.0) * moved[f])[:32]

    shift_plane(15)


def advance_edges(
    place, unused, edges, low, high, left, right, shifted, start, coefs, first, second
):
    row_at, col_at, depth_at = place[1], place[2], place[0]
    depth_last, row_last, col_last = place[3], place[4], place[5]
    shape = (4 * EDGE, 128)
    col = lax.broadcasted_iota(jnp.int32, shape, 0)
    lane = lax.broadcasted_iota(jnp.int32, shape, 1)
    cols_in = ((col >= EDGE) | (col_at > 0)) & ((col < 3 * EDGE) | (col_at < col_last))

    def table(b):
        line = lane + 128 * b
        plane = jnp.floor((line.astype(F32) + 0.5) * (1.0 / ROWS)).astype(jnp.int32)
        row = line - plane * ROWS
        rows_in = (
            (row < 32)
            | ((row < 32 + HALO) & (row_at < row_last))
            | ((row >= ROWS - HALO) & (row_at > 0))
        )
        planes_in = ((plane >= HALO) | (depth_at > 0)) & (
            (plane < HALO + 16) | ((plane < PLANES) & (depth_at < depth_last))
        )
        step = jnp.where(rows_in & cols_in & planes_in, TIME_STEP, 0.0).astype(F32)
        return step, row == 0, row == ROWS - 1

    for f in range(4):
        for b in range(BLOCKS):
            cut = slice(f * LINES + 128 * b, f * LINES + 128 * (b + 1))
            own_low, own_high = low[:, cut].astype(F32), high[:, cut].astype(F32)
            if f < 2:
                own_low = own_low + edges[0:8, cut]
                own_high = own_high + edges[8:16, cut]
            gathered = jnp.concatenate(
                [
                    left[:, cut].astype(F32)[:EDGE],
                    own_low[:EDGE],
                    own_high[:EDGE],
                    right[:, cut].astype(F32)[:EDGE],
                ],
                axis=0,
            )
            if f < 2:
                start[f, b] = gathered
            else:
                first[f - 2, b] = gathered
    masks = []
    for b in range(BLOCKS):
        step, first_row, last_row = table(b)
        masks.append((first_row, last_row))
        made = coefficients(step, first[0, b], first[1, b])
        for i in range(6):
            coefs[i, b] = made[i]

    def stage(source, finish):
        held = {}

        def turn(f, b, by):
            b = b % BLOCKS
            if (f, b, by) not in held:
                held[f, b, by] = pltpu.roll(source[f, b], by, 1)
            return held[f, b, by]

        def from_before(f, b, by):
            return jnp.where(lane < by, turn(f, b - 1, by), turn(f, b, by))

        def from_after(f, b, by):
            return jnp.where(lane >= 128 - by, turn(f, b + 1, 128 - by), turn(f, b, 128 - by))

        for b in range(BLOCKS):
            first_row, last_row = masks[b]

            def neighbours(f):
                x = source[f, b]
                return (
                    from_before(f, b, ROWS),
                    from_after(f, b, ROWS),
                    jnp.where(first_row, from_after(f, b, ROWS - 1), from_before(f, b, 1)),
                    jnp.where(last_row, from_before(f, b, ROWS - 1), from_after(f, b, 1)),
                    pltpu.roll(x, 1, 0),
                    pltpu.roll(x, 4 * EDGE - 1, 0),
                )

            moved = stepped(
                (source[0, b], source[1, b]), tuple(coefs[i, b] for i in range(6)), neighbours
            )
            for f in range(2):
                finish(f, b, moved[f])

    def finish_first(f, b, moved):
        first[f, b] = moved

    def finish_second(f, b, moved):
        second[f, b] = 0.75 * start[f, b] + 0.25 * moved

    def finish_third(f, b, moved):
        first[f, b] = start[f, b] * (1.0 / 3.0) + (2.0 / 3.0) * moved

    stage(start, finish_first)
    stage(first, finish_second)
    stage(second, finish_third)

    m = lax.broadcasted_iota(jnp.int32, (4 * EDGE, 128), 0)
    column = jnp.where(m < 2 * EDGE, m - EDGE, m + 128 - 3 * EDGE)
    used = ((column >= -RIM) & (column < RIM)) | ((column >= 128 - RIM) & (column < 128 + RIM))
    placed = jnp.concatenate(
        [(used & (column == lane + shift)).astype(F32) for shift in range(-RIM, RIM + 1)], axis=1
    )
    placed = jnp.concatenate([placed] * 3, axis=0).astype(BF16)
    lane8 = lax.broadcasted_iota(jnp.int32, (8, 128), 1)
    for f in range(2):
        for b in range(BLOCKS):
            rest = first[f, b]
            parts = []
            for _ in range(3):
                part = rest.astype(BF16).astype(F32)
                parts.append(part)
                rest = rest - part
            patch = lax.dot_general(
                jnp.concatenate(parts, axis=0).astype(BF16), placed, TN, preferred_element_type=F32
            )
            for g in range(16):
                plane, strip = divmod(16 * b + g, ROWS // 8)
                if strip == 4 or not HALO <= plane < HALO + 16:
                    continue
                for i in range(SHIFTS):
                    shift = i - RIM
                    wrong = (lane8 < RIM - shift) | (lane8 >= 128 - RIM - shift)
                    pltpu.store(
                        shifted.at[i, f, plane - HALO, 8 * strip : 8 * strip + 8],
                        patch[8 * g : 8 * g + 8, 128 * i : 128 * (i + 1)],
                        mask=wrong,
                    )


def render_and_save(away, place, shear, weight, bias, shifted, image, out, sem):
    copy = pltpu.make_async_copy(shifted.at[RIM], out, sem.at[0])
    copy.start()
    render(away, place, shear, weight, bias, shifted, image)
    copy.wait()


def render(away, place, shear, weight, bias, shifted, image):
    count = image.shape[0]
    depth_cells = shifted.shape[2]
    depth_at, depth_last = place[0], place[3]
    first = lax.rem(depth_at + away, depth_last + 1) * count
    middle = 0.5 * depth_cells * (depth_last + 1).astype(F32)

    @pl.loop(0, count)
    def _(j):
        v = first + j
        table = [
            tuple(
                (0.5 if c < 3 else LOG2E) * value
                for value in (weight[c, 0, v], weight[c, 1, v], bias[c, v])
            )
            for c in range(4)
        ]
        slope = shear[v]

        for part in range(4):
            strip = slice(part * 8, (part + 1) * 8)

            def march(k, state):
                c0, c1, c2, total, through = state
                place_in_depth = (depth_at * depth_cells + k).astype(F32) + 0.5
                offset = slope * (place_in_depth - middle)
                whole = offset.astype(jnp.int32)
                whole = jnp.where(whole.astype(F32) > offset, whole - 1, whole)
                t = offset - whole.astype(F32)
                i = jnp.clip(whole + RIM, 0, SHIFTS - 2)
                s0 = (1.0 - t) * shifted[i, 0, k, strip] + t * shifted[i + 1, 0, k, strip]
                s1 = (1.0 - t) * shifted[i, 1, k, strip] + t * shifted[i + 1, 1, k, strip]
                logits = [table[c][0] * s0 + table[c][1] * s1 + table[c][2] for c in range(4)]
                total = total + jnp.log(1.0 + jnp.exp2(logits[3]))
                after = jnp.exp2((-RAY_STEP * LOG2E) * total)
                part = through - after
                c0 = c0 + part * jnp.tanh(logits[0])
                c1 = c1 + part * jnp.tanh(logits[1])
                c2 = c2 + part * jnp.tanh(logits[2])
                return c0, c1, c2, total, after

            zero = jnp.zeros((8, 128), F32)
            c0, c1, c2, _, through = lax.fori_loop(
                0, depth_cells, march, (zero, zero, zero, zero, zero + 1.0), unroll=16
            )
            opacity = 1.0 - through
            image[j, 0, strip] = 0.5 * (c0 + opacity)
            image[j, 1, strip] = 0.5 * (c1 + opacity)
            image[j, 2, strip] = 0.5 * (c2 + opacity)
            image[j, 3, strip] = opacity


def deal(place, owners, lengths, warp, select, lengths_wide, warp_own, sem):
    views = warp_own.shape[0]
    copy = pltpu.make_async_copy(warp.at[pl.ds(place[0] * views, views)], warp_own, sem.at[0])
    copy.start()
    row = lax.broadcasted_iota(jnp.int32, (128, 128), 0)
    lane = lax.broadcasted_iota(jnp.int32, (128, 128), 1)
    name = jnp.concatenate([owners[v : v + 1, :] for v in range(views)], axis=1)
    length = jnp.concatenate([lengths[v : v + 1, :] for v in range(views)], axis=1)
    along = jnp.broadcast_to(name, (128, 128))
    across = along.T
    earlier = (along == across) & (row < lane) & (row // 32 == lane // 32)
    rank = jnp.sum(earlier.astype(F32), axis=0, keepdims=True).astype(jnp.int32)
    view = lane[0:1] // 32
    half = select.shape[0] // 2
    codes = name * (views * CAPACITY // 2) + view * (CAPACITY // 2) + rank // 2
    codes = codes + (rank % 2) * half
    slot = lax.broadcasted_iota(jnp.int32, select.shape, 0)
    select[...] = (slot == codes).astype(F32).astype(BF16)
    lengths_wide[...] = jnp.broadcast_to(length, (128, 128)).T
    copy.wait()


def composite(place, order, select, lengths, slab0, slab1, slab2, slab3, outgoing, pieces):
    lane = lax.broadcasted_iota(jnp.int32, (32, 128), 1)
    slabs = (slab0, slab1, slab2, slab3)
    depth_at, devices = place[0], place[3] + 1

    for v in range(4):
        keep = lane < lengths[32 * v : 32 * (v + 1), :]
        when = [jnp.int32(0)] * 4
        for position in range(4):
            turn = lax.rem(depth_at - order[position, depth_at * 4 + v] + devices, devices)
            when = [jnp.where(turn == i, position, when[i]) for i in range(4)]
        opacity = [slabs[i][v, 3] for i in range(4)]
        weight = [None] * 4
        for i in range(4):
            for j in range(4):
                if i != j:
                    ahead = jnp.where(when[j] < when[i], 1.0, 0.0).astype(F32)
                    clear = 1.0 - ahead * opacity[j]
                    weight[i] = clear if weight[i] is None else weight[i] * clear
        for c in range(4):
            value = sum(weight[i] * (slabs[i][v, c] if c < 3 else opacity[i]) for i in range(4))
            pieces[32 * v : 32 * (v + 1), 128 * c : 128 * (c + 1)] = jnp.where(
                keep, value, 0.0
            ).astype(BF16)
    row_id = lax.broadcasted_iota(jnp.int32, (128, 128), 0) + 1
    pieces[:, 512:640] = row_id.astype(F32).astype(BF16)
    dealt = jnp.dot(select[...], pieces[...], preferred_element_type=F32).astype(BF16)
    half = outgoing.shape[0]
    outgoing[:, 0:512] = dealt[:half, 0:512]
    outgoing[:, 512:1024] = dealt[half:, 0:512]
    outgoing[:, 1024:1088] = dealt[:half, 512:576]
    outgoing[:, 1088:1152] = dealt[half:, 576:640]


def resample(incoming, warp, frame, done, sems):
    rows = incoming.shape[0]
    ids = incoming[:, 1024:1152].astype(F32)
    lane = lax.broadcasted_iota(jnp.int32, (rows, 128), 1)
    swapped = pltpu.roll(ids, 64, 1)
    line = (lane + 1).astype(F32)
    total = jnp.zeros((128, 512), F32)
    for odd in range(2):
        names = jnp.where((lane < 64) == (odd == 0), ids, swapped)
        place = (names == line).astype(F32).astype(BF16)
        part = incoming[:, 512 * odd : 512 * (odd + 1)]
        total = total + lax.dot_general(place, part, TN, preferred_element_type=F32)
    copies = []
    for v in range(4):
        rows = jnp.concatenate(
            [total[32 * v : 32 * (v + 1), 128 * c : 128 * (c + 1)] for c in range(4)], axis=0
        )
        warped = jnp.zeros((128, 128), F32)
        for _ in range(3):
            part = rows.astype(BF16)
            warped = warped + jnp.dot(part, warp[v], preferred_element_type=F32)
            rows = rows - part.astype(F32)
        for c in range(4):
            done[pl.ds(128 * v + c, 32, stride=4), :] = warped[32 * c : 32 * (c + 1)]
        cut = pl.ds(128 * v, 128)
        copies.append(pltpu.make_async_copy(done.at[cut], frame.at[cut], sems.at[v]))
        copies[-1].start()
    for copy in copies:
        copy.wait()


def body(
    species,
    diffusivity,
    reaction_rate,
    shear_rate,
    colour_weight,
    colour_bias,
    slab_order,
    lengths,
    owners,
    warp_matrix,
):
    depth_at, row_at, col_at = (lax.axis_index(a) for a in ("depth", "row", "col"))
    depth_devices, row_devices, col_devices = (lax.axis_size(a) for a in ("depth", "row", "col"))
    view_count = shear_rate.shape[0] // depth_devices

    place = jnp.stack(
        [
            depth_at,
            row_at,
            col_at,
            jnp.int32(depth_devices - 1),
            jnp.int32(row_devices - 1),
            jnp.int32(col_devices - 1),
        ]
    ).astype(jnp.int32)
    fields = tuple(in_hbm(x) for x in (species, diffusivity, reaction_rate))

    face = jax.ShapeDtypeStruct((4, HALO, 32, 128), BF16)
    low, high = call(
        pack_depth,
        (face, face),
        [HBM_SPEC] * 3,
        [pltpu.VMEM((2, 4, HALO, 32, 128), F32), pltpu.SemaphoreType.DMA((8,))],
    )(*fields)
    before, after = shift_up(high, "depth"), shift_down(low, "depth")
    brick_type = jax.ShapeDtypeStruct((4, PLANES, ROWS, 128), F32)
    brick, edges = call(
        load_brick,
        (brick_type, jax.ShapeDtypeStruct((16, 2 * LINES), F32)),
        [HBM_SPEC] * 3,
        [pltpu.SemaphoreType.DMA((4,))],
    )(*fields)
    face = jax.ShapeDtypeStruct((HALO, 4 * PLANES, 128), BF16)
    brick, low, high = call(
        pack_rows, (brick_type, face, face), [VMEM_SPEC] * 3, aliases={0: 0}
    )(brick, before, after)
    above, below = turn_by(high, "row", 1), turn_by(low, "row", -1)
    slots = col_devices * view_count * CAPACITY
    lines = view_count * 32
    select, lengths_wide, warp_own = call(
        deal,
        (
            jax.ShapeDtypeStruct((slots, lines), BF16),
            jax.ShapeDtypeStruct((lines, 128), jnp.int32),
            jax.ShapeDtypeStruct((view_count, 128, 128), BF16),
        ),
        [SMEM_SPEC, VMEM_SPEC, VMEM_SPEC, HBM_SPEC],
        [pltpu.SemaphoreType.DMA((1,))],
    )(place, owners.reshape(view_count, 32), lengths.reshape(view_count, 32), in_hbm(warp_matrix))

    brick, select, lengths_wide, warp_own = lax.optimization_barrier(
        (brick, select, lengths_wide, warp_own)
    )
    face = jax.ShapeDtypeStruct((8, 4 * LINES), BF16)
    brick, low, high = call(
        pack_columns, (brick_type, face, face), [SMEM_SPEC] + [VMEM_SPEC] * 3, aliases={1: 0}
    )(place, brick, above, below)
    left = shift_up(high, "col")
    right = shift_down(low, "col")
    wide = pltpu.VMEM((2, PLANES, ROWS, 128), F32)
    shifted_type = jax.ShapeDtypeStruct((SHIFTS,) + species.shape, F32)
    shifted = call(
        advance_own,
        shifted_type,
        [SMEM_SPEC, VMEM_SPEC],
        [wide, wide, pltpu.VMEM((6, PLANES, ROWS, 128), F32)],
        limit=12,
    )(place, brick)
    shifted = call(
        advance_edges,
        shifted_type,
        [SMEM_SPEC] + [VMEM_SPEC] * 6,
        [pltpu.VMEM((n, BLOCKS, 4 * EDGE, 128), F32) for n in (2, 6, 2, 2)],
        aliases={1: 0},
    )(place, shifted, edges, low, high, left, right)

    image = jax.ShapeDtypeStruct((view_count, 4, 32, 128), F32)
    weight, bias = jnp.transpose(colour_weight, (1, 2, 0)), colour_bias.T
    slabs = [None] * 4
    for away in (2, 1, 3, 0):
        if away == SAVER:
            drawn, species_out = call(
                functools.partial(render_and_save, away),
                (image, jax.ShapeDtypeStruct(species.shape, F32)),
                [SMEM_SPEC] * 4 + [VMEM_SPEC],
                [pltpu.SemaphoreType.DMA((1,))],
                out_specs=(VMEM_SPEC, HBM_SPEC),
            )(place, shear_rate, weight, bias, shifted)
        else:
            drawn = call(
                functools.partial(render, away), image, [SMEM_SPEC] * 4 + [VMEM_SPEC]
            )(place, shear_rate, weight, bias, shifted)
        if away:
            drawn = turn_by(drawn, "depth", away)
        slabs[away] = drawn
    outgoing = call(
        composite,
        jax.ShapeDtypeStruct((slots // 2, 1152), BF16),
        [SMEM_SPEC] * 2 + [VMEM_SPEC] * 6,
        [pltpu.VMEM((lines, 640), BF16)],
    )(place, slab_order.T, select, lengths_wide, *slabs)
    incoming = lax.all_to_all(
        outgoing.reshape(col_devices, -1, 1152),
        "col",
        split_axis=0,
        concat_axis=0,
        tiled=True,
    ).reshape(slots // 2, 1152)
    frame = call(
        resample,
        jax.ShapeDtypeStruct((4 * lines, 128), F32),
        [VMEM_SPEC] * 2,
        [pltpu.VMEM((4 * lines, 128), F32), pltpu.SemaphoreType.DMA((4,))],
        out_specs=HBM_SPEC,
    )(incoming, warp_own)
    return species_out, frame.reshape(view_count, 32, 4, 128)


def solution(mesh):
    in_specs = (
        P(None, "depth", "row", "col"),
        P("depth", "row", "col"),
        P("depth", "row", "col"),
        P(),
        P(),
        P(),
        P(),
        P("depth", "col", "row"),
        P("depth", "col", "row", None),
        P(),
    )
    out_specs = (P(None, "depth", "row", "col"), P("depth", "row", None, "col"))
    return jax.shard_map(body, mesh=mesh, in_specs=in_specs, out_specs=out_specs, check_vma=False)
```

```python
import functools

import jax
import jax.numpy as jnp
from jax import lax
from jax.experimental import pallas as pl
from jax.experimental.pallas import tpu as pltpu
from jax.sharding import PartitionSpec as P

TIME_STEP = 0.1
RAY_STEP = 0.02
LOG2E = 1.4426950408889634
VEL_DEPTH = 0.3
VEL_ROW = 0.2
VEL_COL = 0.4

HALO = 3
RIM = 3
EDGE = 6
PLANES = 22
ROWS = 40
LINES = 896
BLOCKS = LINES // 128
SHIFTS = 2 * RIM + 1
CAPACITY = 4
SAVER = 1

F32 = jnp.float32
BF16 = jnp.bfloat16
VMEM_SPEC = pl.BlockSpec(memory_space=pltpu.VMEM)
SMEM_SPEC = pl.BlockSpec(memory_space=pltpu.SMEM)
HBM_SPEC = pl.BlockSpec(memory_space=pltpu.HBM)
NT = (((1,), (1,)), ((), ()))
TN = (((0,), (0,)), ((), ()))


def call(kernel, out_shape, in_specs, scratch=(), limit=8, aliases=None, out_specs=None):
    return pl.pallas_call(
        kernel,
        out_shape=out_shape,
        in_specs=in_specs,
        out_specs=out_specs or jax.tree.map(lambda unused: VMEM_SPEC, out_shape),
        scratch_shapes=list(scratch),
        input_output_aliases=aliases or {},
        compiler_params=pltpu.CompilerParams(vmem_limit_bytes=limit << 20),
    )


def in_hbm(x):
    return pltpu.with_memory_space_constraint(x, pltpu.HBM)


def turn_by(x, axis, steps):
    n = lax.axis_size(axis)
    return lax.ppermute(x, axis, [(i, (i + steps) % n) for i in range(n)])


def shift_up(x, axis):
    n = lax.axis_size(axis)
    return lax.ppermute(x, axis, [(i, i + 1) for i in range(n - 1)])


def shift_down(x, axis):
    n = lax.axis_size(axis)
    return lax.ppermute(x, axis, [(i + 1, i) for i in range(n - 1)])


def pack_depth(species, diff, rate, low, high, held, sems):
    copies = []
    for side, first in ((0, 0), (1, 16 - HALO)):
        cut = pl.ds(first, HALO)
        for source, at in (
            (species.at[0, cut], 0),
            (species.at[1, cut], 1),
            (diff.at[cut], 2),
            (rate.at[cut], 3),
        ):
            copies.append(
                pltpu.make_async_copy(source, held.at[side, at], sems.at[4 * side + at])
            )
    for copy in copies:
        copy.start()
    for copy in copies:
        copy.wait()
    low[...] = held[0].astype(BF16)
    high[...] = held[1].astype(BF16)


def load_brick(species, diff, rate, brick, sems):
    copies = [
        pltpu.make_async_copy(
            source, brick.at[f, pl.ds(HALO, 16), pl.ds(0, 32), :], sems.at[f]
        )
        for f, source in enumerate((species.at[0], species.at[1], diff, rate))
    ]
    for copy in copies:
        copy.start()
    for f in range(4):
        brick[f, :, 32:ROWS, :] = jnp.zeros((PLANES, ROWS - 32, 128), F32)
    for copy in copies:
        copy.wait()


def pack_rows(unused, before, after, brick, low, high):
    for f in range(4):
        brick[f, 0:HALO, 0:32, :] = before[f].astype(F32)
        brick[f, HALO + 16 : 22, 0:32, :] = after[f].astype(F32)
    lines = brick.reshape(4 * PLANES * ROWS, 128)
    for r in range(HALO):
        low[r] = lines[pl.ds(r, 4 * PLANES, stride=ROWS), :].astype(BF16)
        high[r] = lines[pl.ds(32 - HALO + r, 4 * PLANES, stride=ROWS), :].astype(BF16)


def column_picker(first_low, first_high):
    j = lax.broadcasted_iota(jnp.int32, (16, 128), 0)
    lane = lax.broadcasted_iota(jnp.int32, (16, 128), 1)
    at = jnp.where(j < 8, first_low + j, first_high + j - 8)
    return ((lane == at) & (j % 8 < EDGE)).astype(F32).astype(BF16)


def pack_columns(place, unused, above, below, brick, low, high):
    has_above = jnp.where(place[1] > 0, 1.0, 0.0).astype(F32)
    has_below = jnp.where(place[1] < place[4], 1.0, 0.0).astype(F32)
    lines = brick.reshape(4 * PLANES * ROWS, 128)
    for r in range(HALO):
        lines[pl.ds(ROWS - HALO + r, 4 * PLANES, stride=ROWS), :] = has_above * above[r].astype(F32)
        lines[pl.ds(32 + r, 4 * PLANES, stride=ROWS), :] = has_below * below[r].astype(F32)
    pick = column_picker(0, 128 - EDGE)
    count = PLANES * ROWS
    blank = jnp.zeros((8, LINES - count), BF16)
    for f in range(4):
        rows = brick[f].reshape(count, 128).astype(BF16)
        edge = lax.dot_general(pick, rows, NT, preferred_element_type=F32).astype(BF16)
        at = f * LINES
        for side, part in ((low, edge[:8]), (high, edge[8:])):
            side[:, at : at + count] = part
            side[:, at + count : at + LINES] = blank


def coefficients(step, diffusivity, reaction):
    spread = step * diffusivity
    return (
        1.0 - (6.0 * spread + (VEL_DEPTH + VEL_ROW + VEL_COL) * step),
        spread + VEL_DEPTH * step,
        spread + VEL_ROW * step,
        spread + VEL_COL * step,
        spread,
        step * reaction,
    )


def stepped(fields, coefs, neighbours):
    fuel, heat = fields
    cell, from_depth, from_row, from_col, from_above, reaction = coefs
    square = heat * heat
    burned = reaction * (fuel * (square / (1.0 + square)))
    results = []
    for f in range(2):
        below_depth, above_depth, below_row, above_row, below_col, above_col = neighbours(f)
        total = (
            (cell * fields[f] + from_depth * below_depth)
            + (from_row * below_row + from_col * below_col)
            + from_above * (above_depth + above_row + above_col)
        )
        results.append(total - burned if f == 0 else total + burned)
    return results


def advance_own(place, brick, shifted, edges, first, second, coefs):
    n = ROWS
    depth_at, row_at = place[0], place[1]
    depth_last, row_last = place[3], place[4]
    row = lax.broadcasted_iota(jnp.int32, (n, 128), 0)
    rows_in = (
        (row < 32)
        | ((row < 32 + HALO) & (row_at < row_last))
        | ((row >= n - HALO) & (row_at > 0))
    )
    step = jnp.where(rows_in, TIME_STEP, 0.0).astype(F32)

    def advanced(source, table, p):
        def neighbours(f):
            centre = source[f, p]
            return (
                source[f, p - 1],
                source[f, p + 1],
                pltpu.roll(centre, 1, 0),
                pltpu.roll(centre, n - 1, 0),
                pltpu.roll(centre, 1, 1),
                pltpu.roll(centre, 127, 1),
            )

        return stepped((source[0, p], source[1, p]), table, neighbours)

    def table_at(p):
        return tuple(coefs[i, p] for i in range(6))

    @pl.loop(1, 21, unroll=4)
    def _(p):
        ok = ((p >= HALO) | (depth_at > 0)) & ((p < HALO + 16) | (depth_at < depth_last))
        scale = jnp.where(ok, 1.0, 0.0).astype(F32)
        table = coefficients(step * scale, brick[2, p], brick[3, p])
        for i in range(6):
            coefs[i, p] = table[i]
        moved = advanced(brick, table, p)
        for f in range(2):
            first[f, p] = moved[f]

    @pl.loop(2, 20, unroll=3)
    def _(p):
        moved = advanced(first, table_at(p), p)
        for f in range(2):
            second[f, p] = 0.75 * brick[f, p] + 0.25 * moved[f]

    def shift_plane(k):
        for f in range(2):
            new = shifted[RIM, f, k]
            for shift in range(-RIM, RIM + 1):
                if shift:
                    shifted[shift + RIM, f, k] = pltpu.roll(new, -shift % 128, 1)

    @pl.loop(0, 16, unroll=2)
    def _(k):
        p = k + HALO
        shift_plane(jnp.maximum(k - 1, 0))
        moved = advanced(second, table_at(p), p)
        for f in range(2):
            shifted[RIM, f, k] = (brick[f, p] * (1.0 / 3.0) + (2.0 / 3.0) * moved[f])[:32]

    shift_plane(15)

    pick = column_picker(0, 128 - EDGE)
    count = PLANES * ROWS
    for f in range(2):
        rows = brick[f].reshape(count, 128)
        rest = (rows - rows.astype(BF16).astype(F32)).astype(BF16)
        edges[:, f * LINES : f * LINES + count] = lax.dot_general(
            pick, rest, NT, preferred_element_type=F32
        )
        edges[:, f * LINES + count : (f + 1) * LINES] = jnp.zeros((16, LINES - count), F32)


def advance_edges(
    place, unused, edges, low, high, left, right, shifted, start, coefs, first, second
):
    row_at, col_at, depth_at = place[1], place[2], place[0]
    depth_last, row_last, col_last = place[3], place[4], place[5]
    shape = (4 * EDGE, 128)
    col = lax.broadcasted_iota(jnp.int32, shape, 0)
    lane = lax.broadcasted_iota(jnp.int32, shape, 1)
    cols_in = ((col >= EDGE) | (col_at > 0)) & ((col < 3 * EDGE) | (col_at < col_last))

    def table(b):
        line = lane + 128 * b
        plane = jnp.floor((line.astype(F32) + 0.5) * (1.0 / ROWS)).astype(jnp.int32)
        row = line - plane * ROWS
        rows_in = (
            (row < 32)
            | ((row < 32 + HALO) & (row_at < row_last))
            | ((row >= ROWS - HALO) & (row_at > 0))
        )
        planes_in = ((plane >= HALO) | (depth_at > 0)) & (
            (plane < HALO + 16) | ((plane < PLANES) & (depth_at < depth_last))
        )
        step = jnp.where(rows_in & cols_in & planes_in, TIME_STEP, 0.0).astype(F32)
        return step, row == 0, row == ROWS - 1

    for f in range(4):
        for b in range(BLOCKS):
            cut = slice(f * LINES + 128 * b, f * LINES + 128 * (b + 1))
            own_low, own_high = low[:, cut].astype(F32), high[:, cut].astype(F32)
            if f < 2:
                own_low = own_low + edges[0:8, cut]
                own_high = own_high + edges[8:16, cut]
            gathered = jnp.concatenate(
                [
                    left[:, cut].astype(F32)[:EDGE],
                    own_low[:EDGE],
                    own_high[:EDGE],
                    right[:, cut].astype(F32)[:EDGE],
                ],
                axis=0,
            )
            if f < 2:
                start[f, b] = gathered
            else:
                first[f - 2, b] = gathered
    masks = []
    for b in range(BLOCKS):
        step, first_row, last_row = table(b)
        masks.append((first_row, last_row))
        made = coefficients(step, first[0, b], first[1, b])
        for i in range(6):
            coefs[i, b] = made[i]

    def stage(source, finish):
        held = {}

        def turn(f, b, by):
            b = b % BLOCKS
            if (f, b, by) not in held:
                held[f, b, by] = pltpu.roll(source[f, b], by, 1)
            return held[f, b, by]

        def from_before(f, b, by):
            return jnp.where(lane < by, turn(f, b - 1, by), turn(f, b, by))

        def from_after(f, b, by):
            return jnp.where(lane >= 128 - by, turn(f, b + 1, 128 - by), turn(f, b, 128 - by))

        for b in range(BLOCKS):
            first_row, last_row = masks[b]

            def neighbours(f):
                x = source[f, b]
                return (
                    from_before(f, b, ROWS),
                    from_after(f, b, ROWS),
                    jnp.where(first_row, from_after(f, b, ROWS - 1), from_before(f, b, 1)),
                    jnp.where(last_row, from_before(f, b, ROWS - 1), from_after(f, b, 1)),
                    pltpu.roll(x, 1, 0),
                    pltpu.roll(x, 4 * EDGE - 1, 0),
                )

            moved = stepped(
                (source[0, b], source[1, b]), tuple(coefs[i, b] for i in range(6)), neighbours
            )
            for f in range(2):
                finish(f, b, moved[f])

    def finish_first(f, b, moved):
        first[f, b] = moved

    def finish_second(f, b, moved):
        second[f, b] = 0.75 * start[f, b] + 0.25 * moved

    def finish_third(f, b, moved):
        first[f, b] = start[f, b] * (1.0 / 3.0) + (2.0 / 3.0) * moved

    stage(start, finish_first)
    stage(first, finish_second)
    stage(second, finish_third)

    m = lax.broadcasted_iota(jnp.int32, (4 * EDGE, 128), 0)
    column = jnp.where(m < 2 * EDGE, m - EDGE, m + 128 - 3 * EDGE)
    used = ((column >= -RIM) & (column < RIM)) | ((column >= 128 - RIM) & (column < 128 + RIM))
    placed = jnp.concatenate(
        [(used & (column == lane + shift)).astype(F32) for shift in range(-RIM, RIM + 1)], axis=1
    )
    placed = jnp.concatenate([placed] * 3, axis=0).astype(BF16)
    lane8 = lax.broadcasted_iota(jnp.int32, (8, 128), 1)
    for f in range(2):
        for b in range(BLOCKS):
            rest = first[f, b]
            parts = []
            for _ in range(3):
                part = rest.astype(BF16).astype(F32)
                parts.append(part)
                rest = rest - part
            patch = lax.dot_general(
                jnp.concatenate(parts, axis=0).astype(BF16), placed, TN, preferred_element_type=F32
            )
            for g in range(16):
                plane, strip = divmod(16 * b + g, ROWS // 8)
                if strip == 4 or not HALO <= plane < HALO + 16:
                    continue
                for i in range(SHIFTS):
                    shift = i - RIM
                    wrong = (lane8 < RIM - shift) | (lane8 >= 128 - RIM - shift)
                    pltpu.store(
                        shifted.at[i, f, plane - HALO, 8 * strip : 8 * strip + 8],
                        patch[8 * g : 8 * g + 8, 128 * i : 128 * (i + 1)],
                        mask=wrong,
                    )


def render_and_save(away, place, shear, weight, bias, shifted, image, out, sem):
    copy = pltpu.make_async_copy(shifted.at[RIM], out, sem.at[0])
    copy.start()
    render(away, place, shear, weight, bias, shifted, image)
    copy.wait()


def render(away, place, shear, weight, bias, shifted, image):
    count = image.shape[0]
    depth_cells = shifted.shape[2]
    depth_at, depth_last = place[0], place[3]
    first = lax.rem(depth_at + away, depth_last + 1) * count
    middle = 0.5 * depth_cells * (depth_last + 1).astype(F32)

    @pl.loop(0, count)
    def _(j):
        v = first + j
        table = [
            tuple(
                (0.5 if c < 3 else LOG2E) * value
                for value in (weight[c, 0, v], weight[c, 1, v], bias[c, v])
            )
            for c in range(4)
        ]
        slope = shear[v]

        for part in range(2):
            strip = slice(part * 16, (part + 1) * 16)

            def march(k, state):
                c0, c1, c2, total, through = state
                place_in_depth = (depth_at * depth_cells + k).astype(F32) + 0.5
                offset = slope * (place_in_depth - middle)
                whole = offset.astype(jnp.int32)
                whole = jnp.where(whole.astype(F32) > offset, whole - 1, whole)
                t = offset - whole.astype(F32)
                i = jnp.clip(whole + RIM, 0, SHIFTS - 2)
                s0 = (1.0 - t) * shifted[i, 0, k, strip] + t * shifted[i + 1, 0, k, strip]
                s1 = (1.0 - t) * shifted[i, 1, k, strip] + t * shifted[i + 1, 1, k, strip]
                logits = [table[c][0] * s0 + table[c][1] * s1 + table[c][2] for c in range(4)]
                total = total + jnp.log(1.0 + jnp.exp2(logits[3]))
                after = jnp.exp2((-RAY_STEP * LOG2E) * total)
                part = through - after
                c0 = c0 + part * jnp.tanh(logits[0])
                c1 = c1 + part * jnp.tanh(logits[1])
                c2 = c2 + part * jnp.tanh(logits[2])
                return c0, c1, c2, total, after

            zero = jnp.zeros((16, 128), F32)
            c0, c1, c2, _, through = lax.fori_loop(
                0, depth_cells, march, (zero, zero, zero, zero, zero + 1.0), unroll=16
            )
            opacity = 1.0 - through
            image[j, 0, strip] = 0.5 * (c0 + opacity)
            image[j, 1, strip] = 0.5 * (c1 + opacity)
            image[j, 2, strip] = 0.5 * (c2 + opacity)
            image[j, 3, strip] = opacity


def deal(place, owners, lengths, warp, select, lengths_wide, warp_own, sem):
    views = warp_own.shape[0]
    copy = pltpu.make_async_copy(warp.at[pl.ds(place[0] * views, views)], warp_own, sem.at[0])
    copy.start()
    row = lax.broadcasted_iota(jnp.int32, (128, 128), 0)
    lane = lax.broadcasted_iota(jnp.int32, (128, 128), 1)
    name = jnp.concatenate([owners[v : v + 1, :] for v in range(views)], axis=1)
    length = jnp.concatenate([lengths[v : v + 1, :] for v in range(views)], axis=1)
    along = jnp.broadcast_to(name, (128, 128))
    across = along.T
    earlier = (along == across) & (row < lane) & (row // 32 == lane // 32)
    rank = jnp.sum(earlier.astype(F32), axis=0, keepdims=True).astype(jnp.int32)
    view = lane[0:1] // 32
    half = select.shape[0] // 2
    codes = name * (views * CAPACITY // 2) + view * (CAPACITY // 2) + rank // 2
    codes = codes + (rank % 2) * half
    slot = lax.broadcasted_iota(jnp.int32, select.shape, 0)
    select[...] = (slot == codes).astype(F32).astype(BF16)
    lengths_wide[...] = jnp.broadcast_to(length, (128, 128)).T
    copy.wait()


def composite(place, order, select, lengths, slab0, slab1, slab2, slab3, outgoing, pieces):
    lane = lax.broadcasted_iota(jnp.int32, (32, 128), 1)
    slabs = (slab0, slab1, slab2, slab3)
    depth_at, devices = place[0], place[3] + 1

    for v in range(4):
        keep = lane < lengths[32 * v : 32 * (v + 1), :]
        when = [jnp.int32(0)] * 4
        for position in range(4):
            turn = lax.rem(depth_at - order[position, depth_at * 4 + v] + devices, devices)
            when = [jnp.where(turn == i, position, when[i]) for i in range(4)]
        opacity = [slabs[i][v, 3] for i in range(4)]
        weight = [None] * 4
        for i in range(4):
            for j in range(4):
                if i != j:
                    ahead = jnp.where(when[j] < when[i], 1.0, 0.0).astype(F32)
                    clear = 1.0 - ahead * opacity[j]
                    weight[i] = clear if weight[i] is None else weight[i] * clear
        for c in range(4):
            value = sum(weight[i] * (slabs[i][v, c] if c < 3 else opacity[i]) for i in range(4))
            pieces[32 * v : 32 * (v + 1), 128 * c : 128 * (c + 1)] = jnp.where(
                keep, value, 0.0
            ).astype(BF16)
    row_id = lax.broadcasted_iota(jnp.int32, (128, 128), 0) + 1
    pieces[:, 512:640] = row_id.astype(F32).astype(BF16)
    dealt = jnp.dot(select[...], pieces[...], preferred_element_type=F32).astype(BF16)
    half = outgoing.shape[0]
    outgoing[:, 0:512] = dealt[:half, 0:512]
    outgoing[:, 512:1024] = dealt[half:, 0:512]
    outgoing[:, 1024:1088] = dealt[:half, 512:576]
    outgoing[:, 1088:1152] = dealt[half:, 576:640]


def resample(incoming, warp, frame):
    rows = incoming.shape[0]
    ids = incoming[:, 1024:1152].astype(F32)
    lane = lax.broadcasted_iota(jnp.int32, (rows, 128), 1)
    swapped = pltpu.roll(ids, 64, 1)
    line = (lane + 1).astype(F32)
    total = jnp.zeros((128, 512), F32)
    for odd in range(2):
        names = jnp.where((lane < 64) == (odd == 0), ids, swapped)
        place = (names == line).astype(F32).astype(BF16)
        part = incoming[:, 512 * odd : 512 * (odd + 1)]
        total = total + lax.dot_general(place, part, TN, preferred_element_type=F32)
    for v in range(4):
        rows = jnp.concatenate(
            [total[32 * v : 32 * (v + 1), 128 * c : 128 * (c + 1)] for c in range(4)], axis=0
        )
        warped = jnp.zeros((128, 128), F32)
        for _ in range(3):
            part = rows.astype(BF16)
            warped = warped + jnp.dot(part, warp[v], preferred_element_type=F32)
            rows = rows - part.astype(F32)
        for c in range(4):
            frame[pl.ds(128 * v + c, 32, stride=4), :] = warped[32 * c : 32 * (c + 1)]


def body(
    species,
    diffusivity,
    reaction_rate,
    shear_rate,
    colour_weight,
    colour_bias,
    slab_order,
    lengths,
    owners,
    warp_matrix,
):
    depth_at, row_at, col_at = (lax.axis_index(a) for a in ("depth", "row", "col"))
    depth_devices, row_devices, col_devices = (lax.axis_size(a) for a in ("depth", "row", "col"))
    view_count = shear_rate.shape[0] // depth_devices

    place = jnp.stack(
        [
            depth_at,
            row_at,
            col_at,
            jnp.int32(depth_devices - 1),
            jnp.int32(row_devices - 1),
            jnp.int32(col_devices - 1),
        ]
    ).astype(jnp.int32)
    fields = tuple(in_hbm(x) for x in (species, diffusivity, reaction_rate))

    face = jax.ShapeDtypeStruct((4, HALO, 32, 128), BF16)
    low, high = call(
        pack_depth,
        (face, face),
        [HBM_SPEC] * 3,
        [pltpu.VMEM((2, 4, HALO, 32, 128), F32), pltpu.SemaphoreType.DMA((8,))],
    )(*fields)
    before, after = shift_up(high, "depth"), shift_down(low, "depth")
    brick_type = jax.ShapeDtypeStruct((4, PLANES, ROWS, 128), F32)
    brick = call(load_brick, brick_type, [HBM_SPEC] * 3, [pltpu.SemaphoreType.DMA((4,))])(*fields)
    face = jax.ShapeDtypeStruct((HALO, 4 * PLANES, 128), BF16)
    brick, low, high = call(
        pack_rows, (brick_type, face, face), [VMEM_SPEC] * 3, aliases={0: 0}
    )(brick, before, after)
    above, below = turn_by(high, "row", 1), turn_by(low, "row", -1)
    slots = col_devices * view_count * CAPACITY
    lines = view_count * 32
    select, lengths_wide, warp_own = call(
        deal,
        (
            jax.ShapeDtypeStruct((slots, lines), BF16),
            jax.ShapeDtypeStruct((lines, 128), jnp.int32),
            jax.ShapeDtypeStruct((view_count, 128, 128), BF16),
        ),
        [SMEM_SPEC, VMEM_SPEC, VMEM_SPEC, HBM_SPEC],
        [pltpu.SemaphoreType.DMA((1,))],
    )(place, owners.reshape(view_count, 32), lengths.reshape(view_count, 32), in_hbm(warp_matrix))

    brick, select, lengths_wide, warp_own = lax.optimization_barrier(
        (brick, select, lengths_wide, warp_own)
    )
    face = jax.ShapeDtypeStruct((8, 4 * LINES), BF16)
    brick, low, high = call(
        pack_columns, (brick_type, face, face), [SMEM_SPEC] + [VMEM_SPEC] * 3, aliases={1: 0}
    )(place, brick, above, below)
    left = shift_up(high, "col")
    right = shift_down(low, "col")
    wide = pltpu.VMEM((2, PLANES, ROWS, 128), F32)
    shifted_type = jax.ShapeDtypeStruct((SHIFTS,) + species.shape, F32)
    shifted, edges = call(
        advance_own,
        (shifted_type, jax.ShapeDtypeStruct((16, 2 * LINES), F32)),
        [SMEM_SPEC, VMEM_SPEC],
        [wide, wide, pltpu.VMEM((6, PLANES, ROWS, 128), F32)],
        limit=12,
    )(place, brick)
    shifted = call(
        advance_edges,
        shifted_type,
        [SMEM_SPEC] + [VMEM_SPEC] * 6,
        [pltpu.VMEM((n, BLOCKS, 4 * EDGE, 128), F32) for n in (2, 6, 2, 2)],
        aliases={1: 0},
    )(place, shifted, edges, low, high, left, right)

    image = jax.ShapeDtypeStruct((view_count, 4, 32, 128), F32)
    weight, bias = jnp.transpose(colour_weight, (1, 2, 0)), colour_bias.T
    slabs = [None] * 4
    for away in (2, 1, 3, 0):
        if away == SAVER:
            drawn, species_out = call(
                functools.partial(render_and_save, away),
                (image, jax.ShapeDtypeStruct(species.shape, F32)),
                [SMEM_SPEC] * 4 + [VMEM_SPEC],
                [pltpu.SemaphoreType.DMA((1,))],
                out_specs=(VMEM_SPEC, HBM_SPEC),
            )(place, shear_rate, weight, bias, shifted)
        else:
            drawn = call(
                functools.partial(render, away), image, [SMEM_SPEC] * 4 + [VMEM_SPEC]
            )(place, shear_rate, weight, bias, shifted)
        if away:
            drawn = turn_by(drawn, "depth", away)
        slabs[away] = drawn
    outgoing = call(
        composite,
        jax.ShapeDtypeStruct((slots // 2, 1152), BF16),
        [SMEM_SPEC] * 2 + [VMEM_SPEC] * 6,
        [pltpu.VMEM((lines, 640), BF16)],
    )(place, slab_order.T, select, lengths_wide, *slabs)
    incoming = lax.all_to_all(
        outgoing.reshape(col_devices, -1, 1152),
        "col",
        split_axis=0,
        concat_axis=0,
        tiled=True,
    ).reshape(slots // 2, 1152)
    frame = call(resample, jax.ShapeDtypeStruct((4 * lines, 128), F32), [VMEM_SPEC] * 2)(
        incoming, warp_own
    )
    return species_out, frame.reshape(view_count, 32, 4, 128)


def solution(mesh):
    in_specs = (
        P(None, "depth", "row", "col"),
        P("depth", "row", "col"),
        P("depth", "row", "col"),
        P(),
        P(),
        P(),
        P(),
        P("depth", "col", "row"),
        P("depth", "col", "row", None),
        P(),
    )
    out_specs = (P(None, "depth", "row", "col"), P("depth", "row", None, "col"))
    return jax.shard_map(body, mesh=mesh, in_specs=in_specs, out_specs=out_specs, check_vma=False)
```
